32 devices in a mesh: groups: 2 (over y), tm: 4 (over z), chan: 4 (over x, core).
Axes of the slice: x: 2, y: 2, z: 4, core: 2. Of those that a mesh axis runs over, the one named last changes fastest.
Arguments:
- tokens: bfloat16 [1024, 4096], P(('groups', 'tm'), 'chan'), parts along dimension 0, may hold values from -6 to 6
- in_weight: bfloat16 [4096, 8192], P('chan'), may hold values from -0.125 to 0.125
- recur_weight: float32 [2048, 2], P('chan'), may hold values from -0.75 to 0.75
- gate_bias: float32 [2048, 4], P('chan'), may hold values from -2 to 13
- forget_offset: float32 [1024], P(('groups', 'tm')), parts along dimension 0, may hold values from 0 to 14
Outputs:
- hidden_states: float32 [2048, 1024], P('chan', ('groups', 'tm')), parts along dimension 1
The draws below stay inside these ranges and needn't reach their ends.
There are 2 independent parts, one for each index of `groups`. The reference program is written for one: setup_inputs(seed, part) draws one part's arguments, and reference() takes and returns one part's arrays. A program takes and returns all parts, laid end to end along the dimension named above; an argument that names none is the same for every part. Nothing has to cross between parts.
All inputs are finite; a program needn't handle non-finite values.
Results may differ from the reference program's by a relative error of at most 0.0003.
Values may be sent and summed in bfloat16 or wider, within the bound.
No kernel may reach another device: no remote copies, remote signals or barrier semaphores. Data moves between devices by JAX's collectives and lax.ppermute only.
A program may use at most 128 MiB of HBM per device.

```python
import math
import jax
import jax.numpy as jnp
from jax import lax

D = 4096
H = 2048
ITERS = 2
TOKENS = 512


def draw_gate_bias(key, part):
    keys = jax.random.split(jax.random.fold_in(key, 11), 3)
    others = jnp.clip(jax.random.normal(keys[0], (H, 4), jnp.float32) * 0.7, -2.0, 2.0)
    slow_share = 0.5
    slow = jax.random.uniform(keys[1], (H,), jnp.float32) < slow_share
    position = jax.random.uniform(keys[2], (H,), jnp.float32)
    lowest = math.log(30.0)
    middle = math.log(2.0 * TOKENS)
    highest = math.log(32.0 * TOKENS)
    forget = jnp.where(slow, middle + position * (highest - middle), lowest + position * (middle - lowest))
    return others.at[:, 1].set(forget)


def draw_forget_offset(key, part):
    keys = jax.random.split(jax.random.fold_in(key, 23), 2)
    spots = jax.random.randint(keys[0], (6,), 0, TOKENS)
    values = jax.random.uniform(keys[1], (6,), jnp.float32, 10.0, 14.0)
    return jnp.zeros((TOKENS,), jnp.float32).at[spots].set(values)


def strengthened(array, stream_key, source, target, shards_of, factor):
    owner, partner = [(jnp.arange(array.shape[dim]) // (array.shape[dim] // shards_of)).reshape([-1 if axis == dim else 1 for axis in range(array.ndim)]) for dim in (source, target)]
    chosen = jax.random.permutation(stream_key, shards_of)[partner]
    strong = (owner == chosen) | (owner == (partner + shards_of // 2) % shards_of)
    return jnp.where(strong, factor * array, array)


def levels(stream_key, shape, pieces, least, high):
    def one(dim, blocks):
        draws = jax.random.uniform(jax.random.fold_in(jax.random.fold_in(stream_key, 6), dim), (blocks,), jnp.float32, least / len(pieces), high / len(pieces))
        return jnp.repeat(jnp.exp(draws), shape[dim] // blocks).reshape((-1,) + (1,) * (len(shape) - dim - 1))

    level = one(*pieces[0])
    for cut in pieces[1:]:
        level = level * one(*cut)
    return level


def noise(key, shape, deviation, reach, cuts=(), held_as=jnp.bfloat16):
    entries = deviation * jax.random.normal(key, shape, jnp.float32)
    if cuts:
        entries = entries * levels(key, shape, cuts, -0.22, 0.18)
    return jnp.clip(entries, -reach, reach).astype(held_as)


def gaussian_with(stream_key, dims, spread, most, pieces, heavy, held_as=jnp.bfloat16):
    drawn = spread * jax.random.normal(stream_key, dims, jnp.float32)
    if pieces:
        drawn = drawn * levels(stream_key, dims, pieces, -0.22, 0.18)
    return jnp.clip(strengthened(drawn, jax.random.fold_in(stream_key, 3), *heavy), -most, most).astype(held_as)


def setup_inputs(seed: int = 0, part: int = 0) -> dict:
    seeds = jax.random.split(jax.random.key(seed), 6)
    part_keys = jax.random.split(jax.random.fold_in(seeds[5], part), 6)
    tokens = noise(part_keys[0], (TOKENS, D), 1.0, 6.0, ((0, 4), (1, 4)))
    in_weight = gaussian_with(seeds[1], (D, 4 * H), D ** -0.5, 0.125, ((0, 4),), (0, 1, 4, 2.0))
    recur_weight = jnp.clip(jax.random.uniform(seeds[2], (H, 2), jnp.float32, -0.75, 0.75) * levels(seeds[2], (H, 2), ((0, 4),), -0.4, 0.0), -0.75, 0.75)
    gate_bias = draw_gate_bias(jax.random.fold_in(seeds[5], 71), part)
    forget_offset = draw_forget_offset(jax.random.fold_in(jax.random.fold_in(seeds[5], part), 71), part)
    return dict(tokens=tokens, in_weight=in_weight, recur_weight=recur_weight, gate_bias=gate_bias, forget_offset=forget_offset)


def gates(projected, prev_cell, prev_hidden, gate_bias, recur_weight, forget_offset):
    input_gate = jax.nn.sigmoid(projected[:, 0] + gate_bias[:, 0:1])
    forget_gate = jax.nn.sigmoid(projected[:, 1] + gate_bias[:, 1:2] + recur_weight[:, 0:1] * prev_hidden - forget_offset[None, :])
    cand_gate = jnp.tanh(projected[:, 2] + gate_bias[:, 2:3])
    output_gate = jax.nn.sigmoid(projected[:, 3] + gate_bias[:, 3:4] + recur_weight[:, 1:2] * prev_hidden)
    new_cell = forget_gate * prev_cell + input_gate * cand_gate
    squashed = jnp.tanh(new_cell)
    new_hidden = output_gate * squashed
    slope = 1.0 - squashed * squashed
    cell_cell = forget_gate
    cell_hidden = prev_cell * forget_gate * (1.0 - forget_gate) * recur_weight[:, 0:1]
    hidden_cell = output_gate * slope * forget_gate
    hidden_hidden = output_gate * (1.0 - output_gate) * recur_weight[:, 1:2] * squashed + output_gate * slope * cell_hidden
    offset_cell = new_cell - cell_cell * prev_cell - cell_hidden * prev_hidden
    offset_hidden = new_hidden - hidden_cell * prev_cell - hidden_hidden * prev_hidden
    return (cell_cell, cell_hidden, hidden_cell, hidden_hidden, offset_cell, offset_hidden)


def advance(carry, term):
    cell, hidden = carry
    new_cell = term[0] * cell + term[1] * hidden + term[4]
    new_hidden = term[2] * cell + term[3] * hidden + term[5]
    return (new_cell, new_hidden), (new_cell, new_hidden)


def reference(tokens, in_weight, recur_weight, gate_bias, forget_offset):
    projected = jnp.dot(tokens, in_weight, preferred_element_type=jnp.float32)
    projected = projected.reshape(TOKENS, H, 4).transpose(1, 2, 0)
    prev_cell = jnp.zeros((H, TOKENS), jnp.float32)
    prev_hidden = jnp.zeros((H, TOKENS), jnp.float32)
    hiddens = prev_hidden
    for repeat in range(ITERS):
        terms = gates(projected, prev_cell, prev_hidden, gate_bias, recur_weight, forget_offset)
        stacked = jnp.stack(terms).transpose(2, 0, 1)
        start_state = (jnp.zeros((H,), jnp.float32), jnp.zeros((H,), jnp.float32))
        final, (cells, hiddens) = lax.scan(advance, start_state, stacked)
        cells = cells.T
        hiddens = hiddens.T
        prev_cell = jnp.concatenate([jnp.zeros((H, 1), jnp.float32), cells[:, :-1]], axis=1)
        prev_hidden = jnp.concatenate([jnp.zeros((H, 1), jnp.float32), hiddens[:, :-1]], axis=1)
    return hiddens
```

```python
import functools

import jax
import jax.numpy as jnp
from jax import lax
from jax.experimental import pallas as pl
from jax.experimental.pallas import tpu as pltpu
from jax.sharding import PartitionSpec as P

LANES = 128
SUB = 8
GATES = 4
GROUP = LANES * GATES
BINADES = 251.0
LOWEST = 125.0
F32 = jnp.float32
BF16 = jnp.bfloat16


def cost(flops, moved):
    return pl.CostEstimate(flops=int(flops), bytes_accessed=int(moved), transcendentals=0)


def vmem(count):
    return [pl.BlockSpec(memory_space=pltpu.VMEM)] * count


def product_kernel(_, x_ref, give_w_ref, keep_w_ref, give_ref, keep_ref):
    x = x_ref[...]
    give_ref[...] = jnp.dot(x, give_w_ref[...], preferred_element_type=F32)
    keep_ref[...] = jnp.dot(x, keep_w_ref[...], preferred_element_type=F32)


def products(owners, tokens, in_weight, first, width, per_owner, tile):
    steps, depth = tokens.shape
    tiles = width // tile

    def column(which):
        return lambda i, who: (0, who[which] * (per_owner // tile) + first // tile + i)

    out = jax.ShapeDtypeStruct((steps, width), F32)
    return pl.pallas_call(
        product_kernel,
        out_shape=(out, out),
        grid_spec=pltpu.PrefetchScalarGridSpec(
            num_scalar_prefetch=1,
            grid=(tiles,),
            in_specs=[
                pl.BlockSpec((steps, depth), lambda i, who: (0, 0)),
                pl.BlockSpec((depth, tile), column(0)),
                pl.BlockSpec((depth, tile), column(1)),
            ],
            out_specs=[pl.BlockSpec((steps, tile), lambda i, who: (0, i))] * 2,
        ),
        compiler_params=pltpu.CompilerParams(dimension_semantics=("arbitrary",)),
        cost_estimate=cost(4 * steps * depth * width, 4 * depth * width + 8 * steps * width),
        name="products",
    )(owners, tokens, in_weight, in_weight)


def encode_kernel(mine_ref, theirs_ref, out_ref, sum_ref):
    steps, width = mine_ref.shape
    blocks = width // LANES
    top = jnp.zeros((steps, LANES), F32)
    for block in range(blocks):
        cols = pl.ds(block * LANES, LANES)
        both = mine_ref[:, cols] + theirs_ref[:, cols]
        sum_ref[:, cols] = both
        top = jnp.maximum(top, jnp.abs(both))
    top = jnp.max(top, axis=0, keepdims=True)
    top = jnp.maximum(top, 1e-30) * 1.0078125
    scale = top.astype(BF16).astype(F32)
    out_ref[pl.ds(blocks * steps, SUB), :] = jnp.broadcast_to(scale, (SUB, LANES)).astype(BF16)
    inverse = 1.0 / scale
    for block in range(blocks):
        value = sum_ref[:, pl.ds(block * LANES, LANES)]
        level = jnp.sqrt(jnp.abs(value) * inverse) * BINADES - LOWEST
        code = jnp.exp2(level)
        out_ref[pl.ds(block * steps, steps), :] = jnp.where(value < 0.0, -code, code).astype(BF16)


def encoded(mine, theirs):
    steps, width = mine.shape
    rows = steps * (width // LANES) + SUB
    return pl.pallas_call(
        encode_kernel,
        out_shape=jax.ShapeDtypeStruct((rows, LANES), BF16),
        in_specs=vmem(2),
        out_specs=pl.BlockSpec(memory_space=pltpu.VMEM),
        scratch_shapes=[pltpu.VMEM((steps, width), F32)],
        cost_estimate=cost(20 * steps * width, 10 * steps * width),
        name="encode",
    )(mine, theirs)


def decoded(code, scale):
    level = (jnp.log2(jnp.abs(code)) + LOWEST) * (1.0 / BINADES)
    size = level * level * scale
    return jnp.where(code < 0.0, -size, size)


def compose(early, later):
    e1, e2, e3, e4, e5, e6 = early
    l1, l2, l3, l4, l5, l6 = later
    return (
        l1 * e1 + l2 * e3,
        l1 * e2 + l2 * e4,
        l3 * e1 + l4 * e3,
        l3 * e2 + l4 * e4,
        l1 * e5 + l2 * e6 + l5,
        l3 * e5 + l4 * e6 + l6,
    )


def compose_lower(early, later):
    e1, e3, e4, e5, e6 = early
    l1, l3, l4, l5, l6 = later
    return (
        l1 * e1,
        l3 * e1 + l4 * e3,
        l4 * e4,
        l1 * e5 + l5,
        l3 * e5 + l4 * e6 + l6,
    )


def sub_blocks(terms, join, identity):
    row = lax.broadcasted_iota(jnp.int32, (SUB, LANES), 0)
    reach = 1
    while reach < SUB:
        moved = tuple(
            jnp.where(row >= reach, pltpu.roll(term, reach, 0), unit)
            for term, unit in zip(terms, identity)
        )
        terms = join(moved, terms)
        reach *= 2
    before = tuple(
        jnp.where(row >= 1, pltpu.roll(term, 1, 0), unit) for term, unit in zip(terms, identity)
    )
    return before, terms


LOWER_UNIT = (1.0, 0.0, 1.0, 0.0, 0.0)
UNIT = (1.0, 0.0, 0.0, 1.0, 0.0, 0.0)


def sigmoid(x):
    return 1.0 / (1.0 + jnp.exp(-x))


def first_kernel(groups, remotes, earlier, *refs):
    refs = list(refs)
    mine_ref, theirs_ref = refs[:2]
    codes = refs[2 : 2 + remotes]
    bias_ref, weight_ref, offset_ref = refs[2 + remotes : 5 + remotes]
    totals_before = refs[5 + remotes : 5 + remotes + earlier]
    kept_ref, prefix_ref, totals_ref, sum_ref = refs[5 + remotes + earlier :]
    steps = mine_ref.shape[0]
    runs = steps // SUB
    blocks = groups * GATES
    done = 0
    for ref in totals_before:
        totals_ref[pl.ds(done, ref.shape[0]), :] = ref[...]
        done += ref.shape[0]
    scales = [
        ref[pl.ds(blocks * steps, SUB), :][0:1, :].astype(F32) for ref in codes
    ]
    lane = lax.broadcasted_iota(jnp.int32, (SUB, LANES), 1)
    quarter = lane // (LANES // GATES)
    inner = lane % (LANES // GATES)
    picks = [inner * GATES + (quarter - q + GATES) % GATES for q in range(GATES)]
    for group in range(groups):
        for q in range(GATES):
            block = group * GATES + q
            cols = pl.ds(block * LANES, LANES)
            value = mine_ref[:, cols] + theirs_ref[:, cols]
            for ref, scale in zip(codes, scales):
                value = value + decoded(ref[pl.ds(block * steps, steps), :].astype(F32), scale)
            sum_ref[q] = value
        channels = pl.ds(group * LANES, LANES)
        biases = [
            jnp.broadcast_to(bias_ref[k : k + 1, channels], (SUB, LANES)) for k in range(GATES)
        ]
        out_weight = jnp.broadcast_to(weight_ref[1:2, channels], (SUB, LANES))
        run = None
        for i in range(runs):
            loaded = [
                jnp.take_along_axis(sum_ref[q, pl.ds(i, SUB, stride=runs), :], picks[q], axis=1)
                for q in range(GATES)
            ]
            pre = []
            for k in range(GATES):
                part = loaded[(0 - k) % GATES]
                for p in range(1, GATES):
                    part = jnp.where(quarter == p, loaded[(p - k) % GATES], part)
                if k:
                    part = pltpu.roll(part, LANES - k * (LANES // GATES), 1)
                pre.append(part + biases[k])
            pre_forget = pre[1] - offset_ref[pl.ds(i * SUB, SUB), :]
            forget = sigmoid(pre_forget)
            output = sigmoid(pre[3])
            cell = sigmoid(pre[0]) * jnp.tanh(pre[2])
            squashed = jnp.tanh(cell)
            hidden_cell = output * (1.0 - squashed * squashed) * forget
            hidden_hidden = output * (1.0 - output) * out_weight * squashed
            term = (forget, hidden_cell, hidden_hidden, cell, output * squashed)
            run = term if run is None else compose_lower(run, term)
            rows = pl.ds(i * SUB, SUB)
            kept_ref[group, 0, rows, :] = pre_forget
            kept_ref[group, 1, rows, :] = pre[3]
            kept_ref[group, 2, rows, :] = cell
        before, total = sub_blocks(run, compose_lower, LOWER_UNIT)
        for index, term in enumerate(before):
            prefix_ref[group, index] = term
        for index, term in enumerate(total):
            totals_ref[pl.ds(done + group * SUB + index, 1), :] = term[SUB - 1 : SUB, :]
        for index in range(len(total), SUB):
            totals_ref[pl.ds(done + group * SUB + index, 1), :] = jnp.zeros((1, LANES), F32)


def first(mine, theirs, codes, bias, weight, offset, earlier):
    steps, width = mine.shape
    groups = width // GROUP
    rows = sum(e.shape[0] for e in earlier) + groups * SUB
    count = 5 + len(codes) + len(earlier)
    return pl.pallas_call(
        functools.partial(first_kernel, groups, len(codes), len(earlier)),
        out_shape=(
            jax.ShapeDtypeStruct((groups, 3, steps, LANES), F32),
            jax.ShapeDtypeStruct((groups, 5, SUB, LANES), F32),
            jax.ShapeDtypeStruct((rows, LANES), F32),
        ),
        in_specs=vmem(count),
        out_specs=vmem(3),
        scratch_shapes=[pltpu.VMEM((GATES, steps, LANES), F32)],
        cost_estimate=cost(60 * steps * width, 20 * steps * width),
        name="first",
    )(mine, theirs, *codes, bias, weight, offset, *earlier)


def in_turn(me, count, own_xor, received):
    for position in range(count - 1):
        picked = received[0]
        for k in range(2, count):
            picked = jnp.where(position == (me ^ k if own_xor else me - k), received[k - 1], picked)
        yield picked, position < me


def arriving(me_ref, count, own_xor, received, group, lower):
    me = me_ref[0]
    rows = [ref[pl.ds(group * SUB, SUB), :] for ref in received]
    cell = jnp.zeros((1, LANES), F32)
    hidden = jnp.zeros((1, LANES), F32)
    for maps, counts in in_turn(me, count, own_xor, rows):
        if lower:
            a, c, d, u, v = (maps[j : j + 1, :] for j in range(5))
            new_cell = a * cell + u
        else:
            a, b, c, d, u, v = (maps[j : j + 1, :] for j in range(6))
            new_cell = a * cell + b * hidden + u
        new_hidden = c * cell + d * hidden + v
        cell = jnp.where(counts, new_cell, cell)
        hidden = jnp.where(counts, new_hidden, hidden)
    return cell, hidden


def second_kernel(count, own_xor, chunks, me_ref, *refs):
    refs = list(refs)
    received = refs[: count - 1]
    kept = refs[count - 1 : count - 1 + chunks]
    prefixes = refs[count - 1 + chunks : count - 1 + 2 * chunks]
    weight_ref = refs[count - 1 + 2 * chunks]
    hidden_ref, prefix_ref, totals_ref = refs[count + 2 * chunks :]
    group = 0
    for kept_ref, before_ref in zip(kept, prefixes):
        groups, _, steps, _ = kept_ref.shape
        for local in range(groups):
            cell, hidden = arriving(me_ref, count, own_xor, received, group, True)
            a, c, d, u, v = (before_ref[local, j] for j in range(5))
            cell, hidden = a * cell + u, c * cell + d * hidden + v
            channels = pl.ds(group * LANES, LANES)
            forget_weight = jnp.broadcast_to(weight_ref[0:1, channels], (SUB, LANES))
            out_weight = jnp.broadcast_to(weight_ref[1:2, channels], (SUB, LANES))
            run = None
            for i in range(steps // SUB):
                rows = pl.ds(i * SUB, SUB)
                pre_forget = kept_ref[local, 0, rows, :]
                pre_output = kept_ref[local, 1, rows, :]
                fresh = kept_ref[local, 2, rows, :]
                forget = sigmoid(pre_forget + forget_weight * hidden)
                output = sigmoid(pre_output + out_weight * hidden)
                kept_cell = forget * cell
                new_cell = kept_cell + fresh
                squashed = jnp.tanh(new_cell)
                slope = output * (1.0 - squashed * squashed)
                cell_hidden = kept_cell * (1.0 - forget) * forget_weight
                hidden_cell = slope * forget
                hidden_hidden = (
                    output * (1.0 - output) * out_weight * squashed + slope * cell_hidden
                )
                offset_cell = new_cell - kept_cell - cell_hidden * hidden
                offset_hidden = output * squashed - hidden_cell * cell - hidden_hidden * hidden
                term = (
                    forget,
                    cell_hidden,
                    hidden_cell,
                    hidden_hidden,
                    offset_cell,
                    offset_hidden,
                )
                run = term if run is None else compose(run, term)
                hidden_ref[group, 0, rows, :] = run[2]
                hidden_ref[group, 1, rows, :] = run[3]
                hidden_ref[group, 2, rows, :] = run[5]
                forget = sigmoid(pre_forget)
                output = sigmoid(pre_output)
                squashed = jnp.tanh(fresh)
                hidden_cell = output * (1.0 - squashed * squashed) * forget
                hidden_hidden = output * (1.0 - output) * out_weight * squashed
                cell, hidden = (
                    forget * cell + fresh,
                    hidden_cell * cell + hidden_hidden * hidden + output * squashed,
                )
            before, total = sub_blocks(run, compose, UNIT)
            for index, term in enumerate(before):
                prefix_ref[group, index] = term
            for index, term in enumerate(total):
                totals_ref[pl.ds(group * SUB + index, 1), :] = term[SUB - 1 : SUB, :]
            for index in range(len(total), SUB):
                totals_ref[pl.ds(group * SUB + index, 1), :] = jnp.zeros((1, LANES), F32)
            group += 1


def second(me, own_xor, received, kept, prefixes, weight):
    count = len(received) + 1
    steps = kept[0].shape[2]
    groups = sum(k.shape[0] for k in kept)
    return pl.pallas_call(
        functools.partial(second_kernel, count, own_xor, len(kept)),
        out_shape=(
            jax.ShapeDtypeStruct((groups, 3, steps, LANES), F32),
            jax.ShapeDtypeStruct((groups, 6, SUB, LANES), F32),
            jax.ShapeDtypeStruct((groups * SUB, LANES), F32),
        ),
        in_specs=[pl.BlockSpec(memory_space=pltpu.SMEM)] + vmem(count - 1 + 2 * len(kept) + 1),
        out_specs=vmem(3),
        cost_estimate=cost(100 * groups * steps * LANES, 24 * groups * steps * LANES),
        name="second",
    )(me, *received, *kept, *prefixes, weight)


def last_kernel(count, own_xor, me_ref, *refs):
    received = refs[: count - 1]
    hidden_ref, prefix_ref, out_ref, turn_ref = refs[count - 1 :]
    groups, _, steps, _ = hidden_ref.shape
    runs = steps // SUB
    for group in range(groups):
        cell, hidden = arriving(me_ref, count, own_xor, received, group, False)
        a, b, c, d, u, v = (prefix_ref[group, j] for j in range(6))
        cell, hidden = a * cell + b * hidden + u, c * cell + d * hidden + v
        for i in range(runs):
            rows = pl.ds(i * SUB, SUB)
            turn_ref[pl.ds(i, SUB, stride=runs), :] = (
                hidden_ref[group, 0, rows, :] * cell
                + hidden_ref[group, 1, rows, :] * hidden
                + hidden_ref[group, 2, rows, :]
            )
        out_ref[pl.ds(group * LANES, LANES), :] = turn_ref[...].T


def last(me, own_xor, received, hiddens, prefix):
    count = len(received) + 1
    groups, _, steps, _ = hiddens.shape
    return pl.pallas_call(
        functools.partial(last_kernel, count, own_xor),
        out_shape=jax.ShapeDtypeStruct((groups * LANES, steps), F32),
        in_specs=[pl.BlockSpec(memory_space=pltpu.SMEM)] + vmem(count + 1),
        out_specs=pl.BlockSpec(memory_space=pltpu.VMEM),
        scratch_shapes=[pltpu.VMEM((steps, LANES), F32)],
        cost_estimate=cost(10 * groups * steps * LANES, 16 * groups * steps * LANES),
        name="last",
    )(me, *received, hiddens, prefix)


def shards(tokens, in_weight, recur_weight, gate_bias, forget_offset):
    steps = tokens.shape[0]
    channels = recur_weight.shape[0]
    groups = channels // LANES
    per_owner = channels * GATES
    owners = lax.axis_size("chan")
    chips = owners // 2
    blocks = lax.axis_size("tm")
    me = lax.axis_index("chan").astype(jnp.int32)
    chip, core = me // 2, me % 2
    when = lax.axis_index("tm").astype(jnp.int32)[None]
    own_xor = blocks & (blocks - 1) == 0

    bias = gate_bias.T
    weight = recur_weight.T
    offset = jnp.broadcast_to(
        forget_offset.reshape(SUB, steps // SUB).T.reshape(steps, 1), (steps, LANES)
    )

    def to_core(value):
        return lax.ppermute(value, "chan", [(i, i ^ 1) for i in range(owners)])

    def to_chip(value, away):
        pairs = [(i, (i + 2 * away) % owners) for i in range(owners)]
        return lax.ppermute(value, "chan", pairs)

    def to_blocks(value):
        if own_xor:
            return [
                lax.ppermute(value, "tm", [(i, i ^ k) for i in range(blocks)])
                for k in range(1, blocks)
            ]
        return [
            lax.ppermute(value, "tm", [(i, i + k) for i in range(blocks - k)])
            for k in range(1, blocks)
        ]

    chunks = [(g * GROUP, GROUP) for g in range(groups)]
    arrived = [[] for _ in chunks]
    for away in range(1, chips):
        target = (chip + away) % chips
        who = jnp.stack([2 * target + 1 - core, 2 * target + core])
        for slot, (start, width) in enumerate(chunks):
            give, keep = products(who, tokens, in_weight, start, width, per_owner, 256)
            code = encoded(keep, to_core(give))
            arrived[slot].append(to_chip(code, away))
    who = jnp.stack([2 * chip + 1 - core, me])
    kept, prefixes, totals = [], [], None
    for slot, (start, width) in enumerate(chunks):
        give, keep = products(who, tokens, in_weight, start, width, per_owner, 256)
        k, p, totals = first(
            keep,
            to_core(give),
            arrived[slot],
            bias[:, start // GATES : (start + width) // GATES],
            weight[:, start // GATES : (start + width) // GATES],
            offset,
            [] if totals is None else [totals],
        )
        kept.append(k)
        prefixes.append(p)
    hiddens, prefix, totals = second(when, own_xor, to_blocks(totals), kept, prefixes, weight)
    return last(when, own_xor, to_blocks(totals), hiddens, prefix)


def solution(mesh):
    placed = (
        P(("groups", "tm"), "chan"),
        P("chan", None),
        P("chan", None),
        P("chan", None),
        P(("groups", "tm")),
    )
    return jax.shard_map(
        shards, mesh=mesh, in_specs=placed, out_specs=P("chan", ("groups", "tm")), check_vma=False
    )
```

```python
import functools

import jax
import jax.numpy as jnp
from jax import lax
from jax.experimental import pallas as pl
from jax.experimental.pallas import tpu as pltpu
from jax.sharding import PartitionSpec as P

LANES = 128
SUB = 8
GATES = 4
GROUP = LANES * GATES
BINADES = 251.0
LOWEST = 125.0
F32 = jnp.float32
BF16 = jnp.bfloat16


def cost(flops, moved):
    return pl.CostEstimate(flops=int(flops), bytes_accessed=int(moved), transcendentals=0)


def vmem(count):
    return [pl.BlockSpec(memory_space=pltpu.VMEM)] * count


def anywhere(count):
    return [pl.BlockSpec(memory_space=pl.ANY)] * count


def on_chip(value):
    return pltpu.with_memory_space_constraint(value, pltpu.VMEM)


PARAMS = pltpu.CompilerParams(vmem_limit_bytes=16 << 20)


def product_kernel(chips, away, first, width, per_owner, tile, tokens_ref, weight_ref, *refs):
    give_ref, keep_ref, x_ref, w_ref, sems = refs[-5:]
    me = lax.axis_index("chan")
    chip, core = me // 2, me % 2
    target = lax.rem(chip + away, chips)
    tiles = width // tile
    tokens_copy = pltpu.make_async_copy(tokens_ref, x_ref, sems.at[2 * tiles])
    tokens_copy.start()
    copies = []
    for which, owner in enumerate((2 * target + 1 - core, 2 * target + core)):
        for i in range(tiles):
            slot = which * tiles + i
            column = pl.multiple_of(owner * per_owner + first + i * tile, tile)
            copies.append(
                pltpu.make_async_copy(
                    weight_ref.at[:, pl.ds(column, tile)], w_ref.at[slot], sems.at[slot]
                )
            )
            copies[-1].start()
    tokens_copy.wait()
    for slot, copy in enumerate(copies):
        out_ref = give_ref if slot < tiles else keep_ref
        copy.wait()
        out_ref[:, pl.ds(slot % tiles * tile, tile)] = jnp.dot(
            x_ref[...], w_ref[slot], preferred_element_type=F32
        )


def products(tokens, in_weight, chips, away, first, width, per_owner, after):
    steps, depth = tokens.shape
    tile = 2 * LANES
    slots = 2 * width // tile
    out = pltpu.VMEM((steps, width), F32)
    return pl.pallas_call(
        functools.partial(product_kernel, chips, away, first, width, per_owner, tile),
        out_shape=(out, out),
        in_specs=anywhere(2 + len(after)),
        out_specs=vmem(2),
        scratch_shapes=[
            pltpu.VMEM((steps, depth), BF16),
            pltpu.VMEM((slots, depth, tile), BF16),
            pltpu.SemaphoreType.DMA((slots + 1,)),
        ],
        compiler_params=PARAMS,
        cost_estimate=cost(4 * steps * depth * width, 4 * depth * width + 8 * steps * width),
        name="products",
    )(tokens, in_weight, *after)


def encode_kernel(mine_ref, theirs_ref, out_ref, sum_ref):
    steps, width = mine_ref.shape
    blocks = width // LANES
    top = jnp.zeros((steps, LANES), F32)
    for block in range(blocks):
        cols = pl.ds(block * LANES, LANES)
        both = mine_ref[:, cols] + theirs_ref[:, cols]
        sum_ref[:, cols] = both
        top = jnp.maximum(top, jnp.abs(both))
    top = jnp.max(top, axis=0, keepdims=True)
    top = jnp.maximum(top, 1e-30) * 1.0078125
    scale = top.astype(BF16).astype(F32)
    out_ref[pl.ds(blocks * steps, SUB), :] = jnp.broadcast_to(scale, (SUB, LANES)).astype(BF16)
    inverse = 1.0 / scale
    for block in range(blocks):
        value = sum_ref[:, pl.ds(block * LANES, LANES)]
        level = jnp.sqrt(jnp.abs(value) * inverse) * BINADES - LOWEST
        code = jnp.exp2(level)
        out_ref[pl.ds(block * steps, steps), :] = jnp.where(value < 0.0, -code, code).astype(BF16)


def encoded(mine, theirs):
    steps, width = mine.shape
    rows = steps * (width // LANES) + SUB
    return pl.pallas_call(
        encode_kernel,
        out_shape=pltpu.VMEM((rows, LANES), BF16),
        in_specs=vmem(2),
        out_specs=pl.BlockSpec(memory_space=pltpu.VMEM),
        scratch_shapes=[pltpu.VMEM((steps, width), F32)],
        compiler_params=PARAMS,
        cost_estimate=cost(20 * steps * width, 10 * steps * width),
        name="encode",
    )(mine, theirs)


def decoded(code, scale):
    level = (jnp.log2(jnp.abs(code)) + LOWEST) * (1.0 / BINADES)
    size = level * level * scale
    return jnp.where(code < 0.0, -size, size)


def compose(early, later):
    e1, e2, e3, e4, e5, e6 = early
    l1, l2, l3, l4, l5, l6 = later
    return (
        l1 * e1 + l2 * e3,
        l1 * e2 + l2 * e4,
        l3 * e1 + l4 * e3,
        l3 * e2 + l4 * e4,
        l1 * e5 + l2 * e6 + l5,
        l3 * e5 + l4 * e6 + l6,
    )


def compose_lower(early, later):
    e1, e3, e4, e5, e6 = early
    l1, l3, l4, l5, l6 = later
    return (
        l1 * e1,
        l3 * e1 + l4 * e3,
        l4 * e4,
        l1 * e5 + l5,
        l3 * e5 + l4 * e6 + l6,
    )


def sub_blocks(terms, join, identity):
    row = lax.broadcasted_iota(jnp.int32, (SUB, LANES), 0)
    reach = 1
    while reach < SUB:
        moved = tuple(
            jnp.where(row >= reach, pltpu.roll(term, reach, 0), unit)
            for term, unit in zip(terms, identity)
        )
        terms = join(moved, terms)
        reach *= 2
    before = tuple(
        jnp.where(row >= 1, pltpu.roll(term, 1, 0), unit) for term, unit in zip(terms, identity)
    )
    return before, terms


LOWER_UNIT = (1.0, 0.0, 1.0, 0.0, 0.0)
UNIT = (1.0, 0.0, 0.0, 1.0, 0.0, 0.0)


def sigmoid(x):
    return 1.0 / (1.0 + jnp.exp(-x))


def first_kernel(start, groups, remotes, earlier, *refs):
    refs = list(refs)
    mine_ref, theirs_ref = refs[:2]
    codes = refs[2 : 2 + remotes]
    bias_ref, weight_ref, offset_ref = refs[2 + remotes : 5 + remotes]
    totals_before = refs[5 + remotes : 5 + remotes + earlier]
    kept_ref, prefix_ref, totals_ref, sum_ref, late_ref = refs[5 + remotes + earlier :]
    steps = mine_ref.shape[0]
    runs = steps // SUB
    blocks = groups * GATES
    done = 0
    for ref in totals_before:
        totals_ref[pl.ds(done, ref.shape[0]), :] = ref[...]
        done += ref.shape[0]
    scales = [
        ref[pl.ds(blocks * steps, SUB), :][0:1, :].astype(F32) for ref in codes
    ]
    late_ref[...] = jnp.broadcast_to(offset_ref[...], (LANES, steps)).T
    lane = lax.broadcasted_iota(jnp.int32, (SUB, LANES), 1)
    quarter = lane // (LANES // GATES)
    inner = lane % (LANES // GATES)
    picks = [inner * GATES + (quarter - q + GATES) % GATES for q in range(GATES)]
    for group in range(groups):
        for q in range(GATES):
            block = group * GATES + q
            cols = pl.ds(start * GROUP + block * LANES, LANES)
            value = mine_ref[:, cols] + theirs_ref[:, cols]
            for ref, scale in zip(codes, scales):
                value = value + decoded(ref[pl.ds(block * steps, steps), :].astype(F32), scale)
            sum_ref[q] = value
        channels = pl.ds((start + group) * LANES, LANES)
        biases = [
            jnp.broadcast_to(bias_ref[k : k + 1, channels], (SUB, LANES)) for k in range(GATES)
        ]
        out_weight = jnp.broadcast_to(weight_ref[1:2, channels], (SUB, LANES))
        run = None
        for i in range(runs):
            loaded = [
                jnp.take_along_axis(sum_ref[q, pl.ds(i, SUB, stride=runs), :], picks[q], axis=1)
                for q in range(GATES)
            ]
            pre = []
            for k in range(GATES):
                part = loaded[(0 - k) % GATES]
                for p in range(1, GATES):
                    part = jnp.where(quarter == p, loaded[(p - k) % GATES], part)
                if k:
                    part = pltpu.roll(part, LANES - k * (LANES // GATES), 1)
                pre.append(part + biases[k])
            pre_forget = pre[1] - late_ref[pl.ds(i, SUB, stride=runs), :]
            forget = sigmoid(pre_forget)
            output = sigmoid(pre[3])
            cell = sigmoid(pre[0]) * jnp.tanh(pre[2])
            squashed = jnp.tanh(cell)
            hidden_cell = output * (1.0 - squashed * squashed) * forget
            hidden_hidden = output * (1.0 - output) * out_weight * squashed
            term = (forget, hidden_cell, hidden_hidden, cell, output * squashed)
            run = term if run is None else compose_lower(run, term)
            rows = pl.ds(i * SUB, SUB)
            kept_ref[group, 0, rows, :] = pre_forget
            kept_ref[group, 1, rows, :] = pre[3]
            kept_ref[group, 2, rows, :] = cell
        before, total = sub_blocks(run, compose_lower, LOWER_UNIT)
        for index, term in enumerate(before):
            prefix_ref[group, index] = term
        for index, term in enumerate(total):
            totals_ref[pl.ds(done + group * SUB + index, 1), :] = term[SUB - 1 : SUB, :]
        for index in range(len(total), SUB):
            totals_ref[pl.ds(done + group * SUB + index, 1), :] = jnp.zeros((1, LANES), F32)


def first(start, groups, mine, theirs, codes, bias, weight, offset, earlier):
    steps = mine.shape[0]
    rows = sum(e.shape[0] for e in earlier) + groups * SUB
    count = 5 + len(codes) + len(earlier)
    return pl.pallas_call(
        functools.partial(first_kernel, start, groups, len(codes), len(earlier)),
        out_shape=(
            pltpu.VMEM((groups, 3, steps, LANES), F32),
            pltpu.VMEM((groups, 5, SUB, LANES), F32),
            pltpu.VMEM((rows, LANES), F32),
        ),
        in_specs=vmem(count),
        out_specs=vmem(3),
        scratch_shapes=[
            pltpu.VMEM((GATES, steps, LANES), F32),
            pltpu.VMEM((steps, LANES), F32),
        ],
        compiler_params=PARAMS,
        cost_estimate=cost(60 * steps * groups * GROUP, 20 * steps * groups * GROUP),
        name="first",
    )(mine, theirs, *codes, bias, weight, offset, *earlier)


def in_turn(me, count, own_xor, received):
    for position in range(count - 1):
        picked = received[0]
        for k in range(2, count):
            picked = jnp.where(position == (me ^ k if own_xor else me - k), received[k - 1], picked)
        yield picked, position < me


def arriving(count, own_xor, received, group, lower):
    me = lax.axis_index("tm")
    rows = [ref[pl.ds(group * SUB, SUB), :] for ref in received]
    cell = jnp.zeros((1, LANES), F32)
    hidden = jnp.zeros((1, LANES), F32)
    for maps, counts in in_turn(me, count, own_xor, rows):
        if lower:
            a, c, d, u, v = (maps[j : j + 1, :] for j in range(5))
            new_cell = a * cell + u
        else:
            a, b, c, d, u, v = (maps[j : j + 1, :] for j in range(6))
            new_cell = a * cell + b * hidden + u
        new_hidden = c * cell + d * hidden + v
        cell = jnp.where(counts, new_cell, cell)
        hidden = jnp.where(counts, new_hidden, hidden)
    return cell, hidden


def second_kernel(count, own_xor, chunks, *refs):
    refs = list(refs)
    received = refs[: count - 1]
    kept = refs[count - 1 : count - 1 + chunks]
    prefixes = refs[count - 1 + chunks : count - 1 + 2 * chunks]
    weight_ref = refs[count - 1 + 2 * chunks]
    hidden_ref, prefix_ref, totals_ref = refs[count + 2 * chunks :]
    group = 0
    for kept_ref, before_ref in zip(kept, prefixes):
        groups, _, steps, _ = kept_ref.shape
        for local in range(groups):
            cell, hidden = arriving(count, own_xor, received, group, True)
            a, c, d, u, v = (before_ref[local, j] for j in range(5))
            cell, hidden = a * cell + u, c * cell + d * hidden + v
            channels = pl.ds(group * LANES, LANES)
            forget_weight = jnp.broadcast_to(weight_ref[0:1, channels], (SUB, LANES))
            out_weight = jnp.broadcast_to(weight_ref[1:2, channels], (SUB, LANES))
            run = None
            for i in range(steps // SUB):
                rows = pl.ds(i * SUB, SUB)
                pre_forget = kept_ref[local, 0, rows, :]
                pre_output = kept_ref[local, 1, rows, :]
                fresh = kept_ref[local, 2, rows, :]
                forget = sigmoid(pre_forget + forget_weight * hidden)
                output = sigmoid(pre_output + out_weight * hidden)
                kept_cell = forget * cell
                new_cell = kept_cell + fresh
                squashed = jnp.tanh(new_cell)
                slope = output * (1.0 - squashed * squashed)
                cell_hidden = kept_cell * (1.0 - forget) * forget_weight
                hidden_cell = slope * forget
                hidden_hidden = (
                    output * (1.0 - output) * out_weight * squashed + slope * cell_hidden
                )
                offset_cell = new_cell - kept_cell - cell_hidden * hidden
                offset_hidden = output * squashed - hidden_cell * cell - hidden_hidden * hidden
                term = (
                    forget,
                    cell_hidden,
                    hidden_cell,
                    hidden_hidden,
                    offset_cell,
                    offset_hidden,
                )
                run = term if run is None else compose(run, term)
                hidden_ref[group, 0, rows, :] = run[2]
                hidden_ref[group, 1, rows, :] = run[3]
                hidden_ref[group, 2, rows, :] = run[5]
                forget = sigmoid(pre_forget)
                output = sigmoid(pre_output)
                squashed = jnp.tanh(fresh)
                hidden_cell = output * (1.0 - squashed * squashed) * forget
                hidden_hidden = output * (1.0 - output) * out_weight * squashed
                cell, hidden = (
                    forget * cell + fresh,
                    hidden_cell * cell + hidden_hidden * hidden + output * squashed,
                )
            before, total = sub_blocks(run, compose, UNIT)
            for index, term in enumerate(before):
                prefix_ref[group, index] = term
            for index, term in enumerate(total):
                totals_ref[pl.ds(group * SUB + index, 1), :] = term[SUB - 1 : SUB, :]
            for index in range(len(total), SUB):
                totals_ref[pl.ds(group * SUB + index, 1), :] = jnp.zeros((1, LANES), F32)
            group += 1


def second(own_xor, received, kept, prefixes, weight):
    count = len(received) + 1
    steps = kept[0].shape[2]
    groups = sum(k.shape[0] for k in kept)
    return pl.pallas_call(
        functools.partial(second_kernel, count, own_xor, len(kept)),
        out_shape=(
            pltpu.VMEM((groups, 3, steps, LANES), F32),
            pltpu.VMEM((groups, 6, SUB, LANES), F32),
            pltpu.VMEM((groups * SUB, LANES), F32),
        ),
        in_specs=vmem(count - 1 + 2 * len(kept) + 1),
        out_specs=vmem(3),
        compiler_params=PARAMS,
        cost_estimate=cost(100 * groups * steps * LANES, 24 * groups * steps * LANES),
        name="second",
    )(*received, *kept, *prefixes, weight)


def last_kernel(count, own_xor, *refs):
    received = refs[: count - 1]
    hidden_ref, prefix_ref, out_ref, turn_ref = refs[count - 1 :]
    groups, _, steps, _ = hidden_ref.shape
    runs = steps // SUB
    for group in range(groups):
        cell, hidden = arriving(count, own_xor, received, group, False)
        a, b, c, d, u, v = (prefix_ref[group, j] for j in range(6))
        cell, hidden = a * cell + b * hidden + u, c * cell + d * hidden + v
        for i in range(runs):
            rows = pl.ds(i * SUB, SUB)
            turn_ref[pl.ds(i, SUB, stride=runs), :] = (
                hidden_ref[group, 0, rows, :] * cell
                + hidden_ref[group, 1, rows, :] * hidden
                + hidden_ref[group, 2, rows, :]
            )
        out_ref[pl.ds(group * LANES, LANES), :] = turn_ref[...].T


def last(own_xor, received, hiddens, prefix):
    count = len(received) + 1
    groups, _, steps, _ = hiddens.shape
    return pl.pallas_call(
        functools.partial(last_kernel, count, own_xor),
        out_shape=jax.ShapeDtypeStruct((groups * LANES, steps), F32),
        in_specs=vmem(count + 1),
        compiler_params=PARAMS,
        out_specs=pl.BlockSpec(memory_space=pltpu.VMEM),
        scratch_shapes=[pltpu.VMEM((steps, LANES), F32)],
        cost_estimate=cost(10 * groups * steps * LANES, 16 * groups * steps * LANES),
        name="last",
    )(*received, hiddens, prefix)


def shards(tokens, in_weight, recur_weight, gate_bias, forget_offset):
    steps = tokens.shape[0]
    channels = recur_weight.shape[0]
    groups = channels // LANES
    per_owner = channels * GATES
    owners = lax.axis_size("chan")
    chips = owners // 2
    blocks = lax.axis_size("tm")
    own_xor = blocks & (blocks - 1) == 0

    bias = on_chip(gate_bias.T)
    weight = on_chip(recur_weight.T)
    offset = on_chip(forget_offset.reshape(1, steps))

    def to_core(value):
        return on_chip(lax.ppermute(value, "chan", [(i, i ^ 1) for i in range(owners)]))

    def to_chip(value, away):
        pairs = [(i, (i + 2 * away) % owners) for i in range(owners)]
        return on_chip(lax.ppermute(value, "chan", pairs))

    def to_blocks(value):
        if own_xor:
            return [
                on_chip(lax.ppermute(value, "tm", [(i, i ^ k) for i in range(blocks)]))
                for k in range(1, blocks)
            ]
        return [
            on_chip(lax.ppermute(value, "tm", [(i, i + k) for i in range(blocks - k)]))
            for k in range(1, blocks)
        ]

    arrived = [[] for _ in range(groups)]
    codes = []
    for away in range(1, chips):
        for group in range(groups):
            give, keep = products(
                tokens, in_weight, chips, away, group * GROUP, GROUP, per_owner, codes[-2:-1]
            )
            codes.append(encoded(keep, to_core(give)))
            arrived[group].append(to_chip(codes[-1], away))
    give, keep = products(tokens, in_weight, chips, 0, 0, per_owner, per_owner, codes[-1:])
    given = to_core(give)
    kept, prefixes, totals = [], [], []
    for group in range(groups):
        k, p, total = first(group, 1, keep, given, arrived[group], bias, weight, offset, totals)
        totals = [total]
        kept.append(k)
        prefixes.append(p)
    hiddens, prefix, total = second(own_xor, to_blocks(totals[0]), kept, prefixes, weight)
    return last(own_xor, to_blocks(total), hiddens, prefix)


def solution(mesh):
    placed = (
        P(("groups", "tm"), "chan"),
        P("chan", None),
        P("chan", None),
        P("chan", None),
        P(("groups", "tm")),
    )
    return jax.shard_map(
        shards, mesh=mesh, in_specs=placed, out_specs=P("chan", ("groups", "tm")), check_vma=False
    )
```

```python
import functools

import jax
import jax.numpy as jnp
from jax import lax
from jax.experimental import pallas as pl
from jax.experimental.pallas import tpu as pltpu
from jax.sharding import PartitionSpec as P


LANES = 128
SUB = 8
GATES = 4
GROUP = LANES * GATES
BINADES = 251.0
LOWEST = 125.0
F32 = jnp.float32
BF16 = jnp.bfloat16


def cost(flops, moved):
    return pl.CostEstimate(flops=int(flops), bytes_accessed=int(moved), transcendentals=0)


def vmem(count):
    return [pl.BlockSpec(memory_space=pltpu.VMEM)] * count


def in_hbm(count):
    return [pl.BlockSpec(memory_space=pltpu.HBM)] * count


def off_chip(value):
    return pltpu.with_memory_space_constraint(value, pltpu.HBM)


def on_chip(value):
    return pltpu.with_memory_space_constraint(value, pltpu.VMEM)


PARAMS = pltpu.CompilerParams(vmem_limit_bytes=16 << 20)


def product_kernel(chips, away, first, width, per_owner, tile, tokens_ref, weight_ref, *refs):
    give_ref, keep_ref, x_ref, w_ref, sems = refs[-5:]
    me = lax.axis_index("chan")
    chip, core = me // 2, me % 2
    target = lax.rem(chip + away, chips)
    tiles = width // tile
    tokens_copy = pltpu.make_async_copy(tokens_ref, x_ref, sems.at[2 * tiles])
    tokens_copy.start()
    copies = []
    for which, owner in enumerate((2 * target + 1 - core, 2 * target + core)):
        for i in range(tiles):
            slot = which * tiles + i
            column = pl.multiple_of(owner * per_owner + first + i * tile, tile)
            copies.append(
                pltpu.make_async_copy(
                    weight_ref.at[:, pl.ds(column, tile)], w_ref.at[slot], sems.at[slot]
                )
            )
            copies[-1].start()
    tokens_copy.wait()
    for slot, copy in enumerate(copies):
        out_ref = give_ref if slot < tiles else keep_ref
        copy.wait()
        out_ref[:, pl.ds(slot % tiles * tile, tile)] = jnp.dot(
            x_ref[...], w_ref[slot], preferred_element_type=F32
        )


def products(tokens, in_weight, chips, away, first, width, per_owner, after):
    steps, depth = tokens.shape
    tile = 2 * LANES
    slots = 2 * width // tile
    out = pltpu.VMEM((steps, width), F32)
    return pl.pallas_call(
        functools.partial(product_kernel, chips, away, first, width, per_owner, tile),
        out_shape=(out, out),
        in_specs=in_hbm(2) + vmem(len(after)),
        out_specs=vmem(2),
        scratch_shapes=[
            pltpu.VMEM((steps, depth), BF16),
            pltpu.VMEM((slots, depth, tile), BF16),
            pltpu.SemaphoreType.DMA((slots + 1,)),
        ],
        compiler_params=PARAMS,
        cost_estimate=cost(4 * steps * depth * width, 4 * depth * width + 8 * steps * width),
        name="products",
    )(tokens, in_weight, *after)


def encode_kernel(mine_ref, theirs_ref, out_ref, sum_ref):
    steps, width = mine_ref.shape
    blocks = width // LANES
    top = jnp.zeros((steps, LANES), F32)
    for block in range(blocks):
        cols = pl.ds(block * LANES, LANES)
        both = mine_ref[:, cols] + theirs_ref[:, cols]
        sum_ref[:, cols] = both
        top = jnp.maximum(top, jnp.abs(both))
    top = jnp.max(top, axis=0, keepdims=True)
    top = jnp.maximum(top, 1e-30) * 1.0078125
    scale = top.astype(BF16).astype(F32)
    out_ref[pl.ds(blocks * steps, SUB), :] = jnp.broadcast_to(scale, (SUB, LANES)).astype(BF16)
    inverse = 1.0 / scale
    for block in range(blocks):
        value = sum_ref[:, pl.ds(block * LANES, LANES)]
        level = jnp.sqrt(jnp.abs(value) * inverse) * BINADES - LOWEST
        code = jnp.exp2(level)
        out_ref[pl.ds(block * steps, steps), :] = jnp.where(value < 0.0, -code, code).astype(BF16)


def encoded(mine, theirs):
    steps, width = mine.shape
    rows = steps * (width // LANES) + SUB
    return pl.pallas_call(
        encode_kernel,
        out_shape=pltpu.VMEM((rows, LANES), BF16),
        in_specs=vmem(2),
        out_specs=pl.BlockSpec(memory_space=pltpu.VMEM),
        scratch_shapes=[pltpu.VMEM((steps, width), F32)],
        compiler_params=PARAMS,
        cost_estimate=cost(20 * steps * width, 10 * steps * width),
        name="encode",
    )(mine, theirs)


def decoded(code, scale):
    level = (jnp.log2(jnp.abs(code)) + LOWEST) * (1.0 / BINADES)
    size = level * level * scale
    return jnp.where(code < 0.0, -size, size)


def compose(early, later):
    e1, e2, e3, e4, e5, e6 = early
    l1, l2, l3, l4, l5, l6 = later
    return (
        l1 * e1 + l2 * e3,
        l1 * e2 + l2 * e4,
        l3 * e1 + l4 * e3,
        l3 * e2 + l4 * e4,
        l1 * e5 + l2 * e6 + l5,
        l3 * e5 + l4 * e6 + l6,
    )


def compose_lower(early, later):
    e1, e3, e4, e5, e6 = early
    l1, l3, l4, l5, l6 = later
    return (
        l1 * e1,
        l3 * e1 + l4 * e3,
        l4 * e4,
        l1 * e5 + l5,
        l3 * e5 + l4 * e6 + l6,
    )


def sub_blocks(terms, join, identity):
    row = lax.broadcasted_iota(jnp.int32, (SUB, LANES), 0)
    reach = 1
    while reach < SUB:
        moved = tuple(
            jnp.where(row >= reach, pltpu.roll(term, reach, 0), unit)
            for term, unit in zip(terms, identity)
        )
        terms = join(moved, terms)
        reach *= 2
    before = tuple(
        jnp.where(row >= 1, pltpu.roll(term, 1, 0), unit) for term, unit in zip(terms, identity)
    )
    return before, terms


LOWER_UNIT = (1.0, 0.0, 1.0, 0.0, 0.0)
UNIT = (1.0, 0.0, 0.0, 1.0, 0.0, 0.0)


def sigmoid(x):
    return 1.0 / (1.0 + jnp.exp(-x))


def first_kernel(start, groups, remotes, earlier, *refs):
    refs = list(refs)
    mine_ref, theirs_ref = refs[:2]
    codes = refs[2 : 2 + remotes]
    bias_ref, weight_ref, offset_ref = refs[2 + remotes : 5 + remotes]
    totals_before = refs[5 + remotes : 5 + remotes + earlier]
    kept_ref, prefix_ref, totals_ref, sum_ref, late_ref = refs[5 + remotes + earlier :]
    steps = mine_ref.shape[0]
    runs = steps // SUB
    blocks = groups * GATES
    done = 0
    for ref in totals_before:
        totals_ref[pl.ds(done, ref.shape[0]), :] = ref[...]
        done += ref.shape[0]
    scales = [
        ref[pl.ds(blocks * steps, SUB), :][0:1, :].astype(F32) for ref in codes
    ]
    late_ref[...] = jnp.broadcast_to(offset_ref[...], (LANES, steps)).T
    lane = lax.broadcasted_iota(jnp.int32, (SUB, LANES), 1)
    quarter = lane // (LANES // GATES)
    inner = lane % (LANES // GATES)
    picks = [inner * GATES + (quarter - q + GATES) % GATES for q in range(GATES)]
    for group in range(groups):
        for q in range(GATES):
            block = group * GATES + q
            cols = pl.ds(start * GROUP + block * LANES, LANES)
            value = mine_ref[:, cols] + theirs_ref[:, cols]
            for ref, scale in zip(codes, scales):
                value = value + decoded(ref[pl.ds(block * steps, steps), :].astype(F32), scale)
            sum_ref[q] = value
        channels = pl.ds((start + group) * LANES, LANES)
        biases = [
            jnp.broadcast_to(bias_ref[k : k + 1, channels], (SUB, LANES)) for k in range(GATES)
        ]
        out_weight = jnp.broadcast_to(weight_ref[1:2, channels], (SUB, LANES))
        run = None
        for i in range(runs):
            loaded = [
                jnp.take_along_axis(sum_ref[q, pl.ds(i, SUB, stride=runs), :], picks[q], axis=1)
                for q in range(GATES)
            ]
            pre = []
            for k in range(GATES):
                part = loaded[(0 - k) % GATES]
                for p in range(1, GATES):
                    part = jnp.where(quarter == p, loaded[(p - k) % GATES], part)
                if k:
                    part = pltpu.roll(part, LANES - k * (LANES // GATES), 1)
                pre.append(part + biases[k])
            pre_forget = pre[1] - late_ref[pl.ds(i, SUB, stride=runs), :]
            forget = sigmoid(pre_forget)
            output = sigmoid(pre[3])
            cell = sigmoid(pre[0]) * jnp.tanh(pre[2])
            squashed = jnp.tanh(cell)
            hidden_cell = output * (1.0 - squashed * squashed) * forget
            hidden_hidden = output * (1.0 - output) * out_weight * squashed
            term = (forget, hidden_cell, hidden_hidden, cell, output * squashed)
            run = term if run is None else compose_lower(run, term)
            rows = pl.ds(i * SUB, SUB)
            kept_ref[group, 0, rows, :] = pre_forget
            kept_ref[group, 1, rows, :] = pre[3]
            kept_ref[group, 2, rows, :] = cell
        before, total = sub_blocks(run, compose_lower, LOWER_UNIT)
        for index, term in enumerate(before):
            prefix_ref[group, index] = term
        for index, term in enumerate(total):
            totals_ref[pl.ds(done + group * SUB + index, 1), :] = term[SUB - 1 : SUB, :]
        for index in range(len(total), SUB):
            totals_ref[pl.ds(done + group * SUB + index, 1), :] = jnp.zeros((1, LANES), F32)


def first(start, groups, mine, theirs, codes, bias, weight, offset, earlier):
    steps = mine.shape[0]
    rows = sum(e.shape[0] for e in earlier) + groups * SUB
    count = 5 + len(codes) + len(earlier)
    return pl.pallas_call(
        functools.partial(first_kernel, start, groups, len(codes), len(earlier)),
        out_shape=(
            pltpu.VMEM((groups, 3, steps, LANES), F32),
            pltpu.VMEM((groups, 5, SUB, LANES), F32),
            pltpu.VMEM((rows, LANES), F32),
        ),
        in_specs=vmem(count),
        out_specs=vmem(3),
        scratch_shapes=[
            pltpu.VMEM((GATES, steps, LANES), F32),
            pltpu.VMEM((steps, LANES), F32),
        ],
        compiler_params=PARAMS,
        cost_estimate=cost(60 * steps * groups * GROUP, 20 * steps * groups * GROUP),
        name="first",
    )(mine, theirs, *codes, bias, weight, offset, *earlier)


def in_turn(me, count, own_xor, received):
    for position in range(count - 1):
        picked = received[0]
        for k in range(2, count):
            picked = jnp.where(position == (me ^ k if own_xor else me - k), received[k - 1], picked)
        yield picked, position < me


def arriving(count, own_xor, received, group, lower):
    me = lax.axis_index("tm")
    rows = [ref[pl.ds(group * SUB, SUB), :] for ref in received]
    cell = jnp.zeros((1, LANES), F32)
    hidden = jnp.zeros((1, LANES), F32)
    for maps, counts in in_turn(me, count, own_xor, rows):
        if lower:
            a, c, d, u, v = (maps[j : j + 1, :] for j in range(5))
            new_cell = a * cell + u
        else:
            a, b, c, d, u, v = (maps[j : j + 1, :] for j in range(6))
            new_cell = a * cell + b * hidden + u
        new_hidden = c * cell + d * hidden + v
        cell = jnp.where(counts, new_cell, cell)
        hidden = jnp.where(counts, new_hidden, hidden)
    return cell, hidden


def second_kernel(count, own_xor, chunks, *refs):
    refs = list(refs)
    received = refs[: count - 1]
    kept = refs[count - 1 : count - 1 + chunks]
    prefixes = refs[count - 1 + chunks : count - 1 + 2 * chunks]
    weight_ref = refs[count - 1 + 2 * chunks]
    hidden_ref, prefix_ref, totals_ref = refs[count + 2 * chunks :]
    group = 0
    for kept_ref, before_ref in zip(kept, prefixes):
        groups, _, steps, _ = kept_ref.shape
        for local in range(groups):
            cell, hidden = arriving(count, own_xor, received, group, True)
            a, c, d, u, v = (before_ref[local, j] for j in range(5))
            cell, hidden = a * cell + u, c * cell + d * hidden + v
            channels = pl.ds(group * LANES, LANES)
            forget_weight = jnp.broadcast_to(weight_ref[0:1, channels], (SUB, LANES))
            out_weight = jnp.broadcast_to(weight_ref[1:2, channels], (SUB, LANES))
            run = None
            for i in range(steps // SUB):
                rows = pl.ds(i * SUB, SUB)
                pre_forget = kept_ref[local, 0, rows, :]
                pre_output = kept_ref[local, 1, rows, :]
                fresh = kept_ref[local, 2, rows, :]
                forget = sigmoid(pre_forget + forget_weight * hidden)
                output = sigmoid(pre_output + out_weight * hidden)
                kept_cell = forget * cell
                new_cell = kept_cell + fresh
                squashed = jnp.tanh(new_cell)
                slope = output * (1.0 - squashed * squashed)
                cell_hidden = kept_cell * (1.0 - forget) * forget_weight
                hidden_cell = slope * forget
                hidden_hidden = (
                    output * (1.0 - output) * out_weight * squashed + slope * cell_hidden
                )
                offset_cell = new_cell - kept_cell - cell_hidden * hidden
                offset_hidden = output * squashed - hidden_cell * cell - hidden_hidden * hidden
                term = (
                    forget,
                    cell_hidden,
                    hidden_cell,
                    hidden_hidden,
                    offset_cell,
                    offset_hidden,
                )
                run = term if run is None else compose(run, term)
                hidden_ref[group, 0, rows, :] = run[2]
                hidden_ref[group, 1, rows, :] = run[3]
                hidden_ref[group, 2, rows, :] = run[5]
                forget = sigmoid(pre_forget)
                output = sigmoid(pre_output)
                squashed = jnp.tanh(fresh)
                hidden_cell = output * (1.0 - squashed * squashed) * forget
                hidden_hidden = output * (1.0 - output) * out_weight * squashed
                cell, hidden = (
                    forget * cell + fresh,
                    hidden_cell * cell + hidden_hidden * hidden + output * squashed,
                )
            before, total = sub_blocks(run, compose, UNIT)
            for index, term in enumerate(before):
                prefix_ref[group, index] = term
            for index, term in enumerate(total):
                totals_ref[pl.ds(group * SUB + index, 1), :] = term[SUB - 1 : SUB, :]
            for index in range(len(total), SUB):
                totals_ref[pl.ds(group * SUB + index, 1), :] = jnp.zeros((1, LANES), F32)
            group += 1


def second(own_xor, received, kept, prefixes, weight):
    count = len(received) + 1
    steps = kept[0].shape[2]
    groups = sum(k.shape[0] for k in kept)
    return pl.pallas_call(
        functools.partial(second_kernel, count, own_xor, len(kept)),
        out_shape=(
            pltpu.VMEM((groups, 3, steps, LANES), F32),
            pltpu.VMEM((groups, 6, SUB, LANES), F32),
            pltpu.VMEM((groups * SUB, LANES), F32),
        ),
        in_specs=vmem(count - 1 + 2 * len(kept) + 1),
        out_specs=vmem(3),
        compiler_params=PARAMS,
        cost_estimate=cost(100 * groups * steps * LANES, 24 * groups * steps * LANES),
        name="second",
    )(*received, *kept, *prefixes, weight)


def last_kernel(count, own_xor, *refs):
    received = refs[: count - 1]
    hidden_ref, prefix_ref, out_ref, turn_ref = refs[count - 1 :]
    groups, _, steps, _ = hidden_ref.shape
    runs = steps // SUB
    for group in range(groups):
        cell, hidden = arriving(count, own_xor, received, group, False)
        a, b, c, d, u, v = (prefix_ref[group, j] for j in range(6))
        cell, hidden = a * cell + b * hidden + u, c * cell + d * hidden + v
        for i in range(runs):
            rows = pl.ds(i * SUB, SUB)
            turn_ref[pl.ds(i, SUB, stride=runs), :] = (
                hidden_ref[group, 0, rows, :] * cell
                + hidden_ref[group, 1, rows, :] * hidden
                + hidden_ref[group, 2, rows, :]
            )
        out_ref[pl.ds(group * LANES, LANES), :] = turn_ref[...].T


def last(own_xor, received, hiddens, prefix):
    count = len(received) + 1
    groups, _, steps, _ = hiddens.shape
    return pl.pallas_call(
        functools.partial(last_kernel, count, own_xor),
        out_shape=jax.ShapeDtypeStruct((groups * LANES, steps), F32),
        in_specs=vmem(count + 1),
        compiler_params=PARAMS,
        out_specs=pl.BlockSpec(memory_space=pltpu.VMEM),
        scratch_shapes=[pltpu.VMEM((steps, LANES), F32)],
        cost_estimate=cost(10 * groups * steps * LANES, 16 * groups * steps * LANES),
        name="last",
    )(*received, hiddens, prefix)


def shards(tokens, in_weight, recur_weight, gate_bias, forget_offset):
    steps = tokens.shape[0]
    channels = recur_weight.shape[0]
    groups = channels // LANES
    per_owner = channels * GATES
    owners = lax.axis_size("chan")
    chips = owners // 2
    blocks = lax.axis_size("tm")
    own_xor = blocks & (blocks - 1) == 0

    bias = on_chip(gate_bias.T)
    weight = on_chip(recur_weight.T)
    offset = on_chip(forget_offset.reshape(1, steps))

    def to_core(value):
        return on_chip(lax.ppermute(value, "chan", [(i, i ^ 1) for i in range(owners)]))

    def to_chip(value, away):
        pairs = [(i, (i + 2 * away) % owners) for i in range(owners)]
        return on_chip(lax.ppermute(value, "chan", pairs))

    def to_blocks(value):
        if own_xor:
            return [
                on_chip(lax.ppermute(value, "tm", [(i, i ^ k) for i in range(blocks)]))
                for k in range(1, blocks)
            ]
        return [
            on_chip(lax.ppermute(value, "tm", [(i, i + k) for i in range(blocks - k)]))
            for k in range(1, blocks)
        ]

    tokens, in_weight = off_chip(tokens), off_chip(in_weight)
    arrived = [[] for _ in range(groups)]
    codes = []
    for away in range(1, chips):
        for group in range(groups):
            give, keep = products(
                tokens, in_weight, chips, away, group * GROUP, GROUP, per_owner, codes[-2:-1]
            )
            given = to_core(give)
            codes.append(encoded(keep, given))
            arrived[group].append(to_chip(codes[-1], away))
    give, keep = products(tokens, in_weight, chips, 0, 0, per_owner, per_owner, codes[-1:])
    given = to_core(give)
    kept, prefixes, totals = [], [], []
    for group in range(groups):
        k, p, total = first(group, 1, keep, given, arrived[group], bias, weight, offset, totals)
        totals = [total]
        kept.append(k)
        prefixes.append(p)
    hiddens, prefix, total = second(own_xor, to_blocks(totals[0]), kept, prefixes, weight)
    return last(own_xor, to_blocks(total), hiddens, prefix)


def solution(mesh):
    placed = (
        P(("groups", "tm"), "chan"),
        P("chan", None),
        P("chan", None),
        P("chan", None),
        P(("groups", "tm")),
    )

    return jax.shard_map(
        shards, mesh=mesh, in_specs=placed, out_specs=P("chan", ("groups", "tm")), check_vma=False
    )
```

```python
import functools

import jax
import jax.numpy as jnp
from jax import lax
from jax.experimental import pallas as pl
from jax.experimental.pallas import tpu as pltpu
from jax.sharding import PartitionSpec as P


LANES = 128
SUB = 8
GATES = 4
GROUP = LANES * GATES
BINADES = 251.0
LOWEST = 125.0
F32 = jnp.float32
BF16 = jnp.bfloat16


def cost(flops, moved):
    return pl.CostEstimate(flops=int(flops), bytes_accessed=int(moved), transcendentals=0)


def vmem(count):
    return [pl.BlockSpec(memory_space=pltpu.VMEM)] * count


def in_hbm(count):
    return [pl.BlockSpec(memory_space=pltpu.HBM)] * count


def off_chip(value):
    return pltpu.with_memory_space_constraint(value, pltpu.HBM)


def on_chip(value):
    return pltpu.with_memory_space_constraint(value, pltpu.VMEM)


PARAMS = pltpu.CompilerParams(vmem_limit_bytes=16 << 20)


def product_kernel(chips, away, first, width, per_owner, tile, tokens_ref, weight_ref, *refs):
    give_ref, keep_ref, x_ref, w_ref, sems = refs[-5:]
    me = lax.axis_index("chan")
    chip, core = me // 2, me % 2
    target = lax.rem(chip + away, chips)
    tiles = width // tile
    tokens_copy = pltpu.make_async_copy(tokens_ref, x_ref, sems.at[2 * tiles])
    tokens_copy.start()
    copies = []
    for which, owner in enumerate((2 * target + 1 - core, 2 * target + core)):
        for i in range(tiles):
            slot = which * tiles + i
            column = pl.multiple_of(owner * per_owner + first + i * tile, tile)
            copies.append(
                pltpu.make_async_copy(
                    weight_ref.at[:, pl.ds(column, tile)], w_ref.at[slot], sems.at[slot]
                )
            )
            copies[-1].start()
    tokens_copy.wait()
    for slot, copy in enumerate(copies):
        out_ref = give_ref if slot < tiles else keep_ref
        copy.wait()
        out_ref[:, pl.ds(slot % tiles * tile, tile)] = jnp.dot(
            x_ref[...], w_ref[slot], preferred_element_type=F32
        )


def products(tokens, in_weight, chips, away, first, width, per_owner, after):
    steps, depth = tokens.shape
    tile = GROUP
    slots = 2 * width // tile
    out = pltpu.VMEM((steps, width), F32)
    return pl.pallas_call(
        functools.partial(product_kernel, chips, away, first, width, per_owner, tile),
        out_shape=(out, out),
        in_specs=in_hbm(2) + vmem(len(after)),
        out_specs=vmem(2),
        scratch_shapes=[
            pltpu.VMEM((steps, depth), BF16),
            pltpu.VMEM((slots, depth, tile), BF16),
            pltpu.SemaphoreType.DMA((slots + 1,)),
        ],
        compiler_params=PARAMS,
        cost_estimate=cost(4 * steps * depth * width, 4 * depth * width + 8 * steps * width),
        name="products",
    )(tokens, in_weight, *after)


def encode_kernel(mine_ref, theirs_ref, out_ref, sum_ref):
    steps, width = mine_ref.shape
    blocks = width // LANES
    top = jnp.zeros((steps, LANES), F32)
    for block in range(blocks):
        cols = pl.ds(block * LANES, LANES)
        both = mine_ref[:, cols] + theirs_ref[:, cols]
        sum_ref[:, cols] = both
        top = jnp.maximum(top, jnp.abs(both))
    top = jnp.max(top, axis=0, keepdims=True)
    top = jnp.maximum(top, 1e-30) * 1.0078125
    scale = top.astype(BF16).astype(F32)
    out_ref[pl.ds(blocks * steps, SUB), :] = jnp.broadcast_to(scale, (SUB, LANES)).astype(BF16)
    inverse = 1.0 / scale
    for block in range(blocks):
        value = sum_ref[:, pl.ds(block * LANES, LANES)]
        level = jnp.sqrt(jnp.abs(value) * inverse) * BINADES - LOWEST
        code = jnp.exp2(level)
        out_ref[pl.ds(block * steps, steps), :] = jnp.where(value < 0.0, -code, code).astype(BF16)


def encoded(mine, theirs):
    steps, width = mine.shape
    rows = steps * (width // LANES) + SUB
    return pl.pallas_call(
        encode_kernel,
        out_shape=pltpu.VMEM((rows, LANES), BF16),
        in_specs=vmem(2),
        out_specs=pl.BlockSpec(memory_space=pltpu.VMEM),
        scratch_shapes=[pltpu.VMEM((steps, width), F32)],
        compiler_params=PARAMS,
        cost_estimate=cost(20 * steps * width, 10 * steps * width),
        name="encode",
    )(mine, theirs)


def decoded(code, scale):
    level = (jnp.log2(jnp.abs(code)) + LOWEST) * (1.0 / BINADES)
    size = level * level * scale
    return jnp.where(code < 0.0, -size, size)


def compose(early, later):
    e1, e2, e3, e4, e5, e6 = early
    l1, l2, l3, l4, l5, l6 = later
    return (
        l1 * e1 + l2 * e3,
        l1 * e2 + l2 * e4,
        l3 * e1 + l4 * e3,
        l3 * e2 + l4 * e4,
        l1 * e5 + l2 * e6 + l5,
        l3 * e5 + l4 * e6 + l6,
    )


def compose_lower(early, later):
    e1, e3, e4, e5, e6 = early
    l1, l3, l4, l5, l6 = later
    return (
        l1 * e1,
        l3 * e1 + l4 * e3,
        l4 * e4,
        l1 * e5 + l5,
        l3 * e5 + l4 * e6 + l6,
    )


def sub_blocks(terms, join, identity):
    row = lax.broadcasted_iota(jnp.int32, (SUB, LANES), 0)
    reach = 1
    while reach < SUB:
        moved = tuple(
            jnp.where(row >= reach, pltpu.roll(term, reach, 0), unit)
            for term, unit in zip(terms, identity)
        )
        terms = join(moved, terms)
        reach *= 2
    before = tuple(
        jnp.where(row >= 1, pltpu.roll(term, 1, 0), unit) for term, unit in zip(terms, identity)
    )
    return before, terms


LOWER_UNIT = (1.0, 0.0, 1.0, 0.0, 0.0)
UNIT = (1.0, 0.0, 0.0, 1.0, 0.0, 0.0)


def sigmoid(x):
    return 1.0 / (1.0 + jnp.exp(-x))


def first_kernel(start, groups, remotes, earlier, *refs):
    refs = list(refs)
    mine_ref, theirs_ref = refs[:2]
    codes = refs[2 : 2 + remotes]
    bias_ref, weight_ref, offset_ref = refs[2 + remotes : 5 + remotes]
    totals_before = refs[5 + remotes : 5 + remotes + earlier]
    kept_ref, prefix_ref, totals_ref, sum_ref, late_ref = refs[5 + remotes + earlier :]
    steps = mine_ref.shape[0]
    runs = steps // SUB
    blocks = groups * GATES
    done = 0
    for ref in totals_before:
        totals_ref[pl.ds(done, ref.shape[0]), :] = ref[...]
        done += ref.shape[0]
    scales = [
        ref[pl.ds(blocks * steps, SUB), :][0:1, :].astype(F32) for ref in codes
    ]
    late_ref[...] = jnp.broadcast_to(offset_ref[...], (LANES, steps)).T
    lane = lax.broadcasted_iota(jnp.int32, (SUB, LANES), 1)
    quarter = lane // (LANES // GATES)
    inner = lane % (LANES // GATES)
    picks = [inner * GATES + (quarter - q + GATES) % GATES for q in range(GATES)]
    for group in range(groups):
        for q in range(GATES):
            block = group * GATES + q
            cols = pl.ds(start * GROUP + block * LANES, LANES)
            value = mine_ref[:, cols] + theirs_ref[:, cols]
            for ref, scale in zip(codes, scales):
                value = value + decoded(ref[pl.ds(block * steps, steps), :].astype(F32), scale)
            sum_ref[q] = value
        channels = pl.ds((start + group) * LANES, LANES)
        biases = [
            jnp.broadcast_to(bias_ref[k : k + 1, channels], (SUB, LANES)) for k in range(GATES)
        ]
        out_weight = jnp.broadcast_to(weight_ref[1:2, channels], (SUB, LANES))
        run = None
        for i in range(runs):
            loaded = [
                jnp.take_along_axis(sum_ref[q, pl.ds(i, SUB, stride=runs), :], picks[q], axis=1)
                for q in range(GATES)
            ]
            pre = []
            for k in range(GATES):
                part = loaded[(0 - k) % GATES]
                for p in range(1, GATES):
                    part = jnp.where(quarter == p, loaded[(p - k) % GATES], part)
                if k:
                    part = pltpu.roll(part, LANES - k * (LANES // GATES), 1)
                pre.append(part + biases[k])
            pre_forget = pre[1] - late_ref[pl.ds(i, SUB, stride=runs), :]
            forget = sigmoid(pre_forget)
            output = sigmoid(pre[3])
            cell = sigmoid(pre[0]) * jnp.tanh(pre[2])
            squashed = jnp.tanh(cell)
            hidden_cell = output * (1.0 - squashed * squashed) * forget
            hidden_hidden = output * (1.0 - output) * out_weight * squashed
            term = (forget, hidden_cell, hidden_hidden, cell, output * squashed)
            run = term if run is None else compose_lower(run, term)
            rows = pl.ds(i * SUB, SUB)
            kept_ref[group, 0, rows, :] = pre_forget
            kept_ref[group, 1, rows, :] = pre[3]
            kept_ref[group, 2, rows, :] = cell
        before, total = sub_blocks(run, compose_lower, LOWER_UNIT)
        for index, term in enumerate(before):
            prefix_ref[group, index] = term
        for index, term in enumerate(total):
            totals_ref[pl.ds(done + group * SUB + index, 1), :] = term[SUB - 1 : SUB, :]
        for index in range(len(total), SUB):
            totals_ref[pl.ds(done + group * SUB + index, 1), :] = jnp.zeros((1, LANES), F32)


def first(start, groups, mine, theirs, codes, bias, weight, offset, earlier):
    steps = mine.shape[0]
    rows = sum(e.shape[0] for e in earlier) + groups * SUB
    count = 5 + len(codes) + len(earlier)
    return pl.pallas_call(
        functools.partial(first_kernel, start, groups, len(codes), len(earlier)),
        out_shape=(
            pltpu.VMEM((groups, 3, steps, LANES), F32),
            pltpu.VMEM((groups, 5, SUB, LANES), F32),
            pltpu.VMEM((rows, LANES), F32),
        ),
        in_specs=vmem(count),
        out_specs=vmem(3),
        scratch_shapes=[
            pltpu.VMEM((GATES, steps, LANES), F32),
            pltpu.VMEM((steps, LANES), F32),
        ],
        compiler_params=PARAMS,
        cost_estimate=cost(60 * steps * groups * GROUP, 20 * steps * groups * GROUP),
        name="first",
    )(mine, theirs, *codes, bias, weight, offset, *earlier)


def in_turn(me, count, own_xor, received):
    for position in range(count - 1):
        picked = received[0]
        for k in range(2, count):
            picked = jnp.where(position == (me ^ k if own_xor else me - k), received[k - 1], picked)
        yield picked, position < me


def arriving(count, own_xor, received, group, lower):
    me = lax.axis_index("tm")
    rows = [ref[pl.ds(group * SUB, SUB), :] for ref in received]
    cell = jnp.zeros((1, LANES), F32)
    hidden = jnp.zeros((1, LANES), F32)
    for maps, counts in in_turn(me, count, own_xor, rows):
        if lower:
            a, c, d, u, v = (maps[j : j + 1, :] for j in range(5))
            new_cell = a * cell + u
        else:
            a, b, c, d, u, v = (maps[j : j + 1, :] for j in range(6))
            new_cell = a * cell + b * hidden + u
        new_hidden = c * cell + d * hidden + v
        cell = jnp.where(counts, new_cell, cell)
        hidden = jnp.where(counts, new_hidden, hidden)
    return cell, hidden


def second_kernel(count, own_xor, chunks, *refs):
    refs = list(refs)
    received = refs[: count - 1]
    kept = refs[count - 1 : count - 1 + chunks]
    prefixes = refs[count - 1 + chunks : count - 1 + 2 * chunks]
    weight_ref = refs[count - 1 + 2 * chunks]
    hidden_ref, prefix_ref, totals_ref = refs[count + 2 * chunks :]
    group = 0
    for kept_ref, before_ref in zip(kept, prefixes):
        groups, _, steps, _ = kept_ref.shape
        for local in range(groups):
            cell, hidden = arriving(count, own_xor, received, group, True)
            a, c, d, u, v = (before_ref[local, j] for j in range(5))
            cell, hidden = a * cell + u, c * cell + d * hidden + v
            channels = pl.ds(group * LANES, LANES)
            forget_weight = jnp.broadcast_to(weight_ref[0:1, channels], (SUB, LANES))
            out_weight = jnp.broadcast_to(weight_ref[1:2, channels], (SUB, LANES))
            run = None
            for i in range(steps // SUB):
                rows = pl.ds(i * SUB, SUB)
                pre_forget = kept_ref[local, 0, rows, :]
                pre_output = kept_ref[local, 1, rows, :]
                fresh = kept_ref[local, 2, rows, :]
                forget = sigmoid(pre_forget + forget_weight * hidden)
                output = sigmoid(pre_output + out_weight * hidden)
                kept_cell = forget * cell
                new_cell = kept_cell + fresh
                squashed = jnp.tanh(new_cell)
                slope = output * (1.0 - squashed * squashed)
                cell_hidden = kept_cell * (1.0 - forget) * forget_weight
                hidden_cell = slope * forget
                hidden_hidden = (
                    output * (1.0 - output) * out_weight * squashed + slope * cell_hidden
                )
                offset_cell = new_cell - kept_cell - cell_hidden * hidden
                offset_hidden = output * squashed - hidden_cell * cell - hidden_hidden * hidden
                term = (
                    forget,
                    cell_hidden,
                    hidden_cell,
                    hidden_hidden,
                    offset_cell,
                    offset_hidden,
                )
                run = term if run is None else compose(run, term)
                hidden_ref[group, 0, rows, :] = run[2]
                hidden_ref[group, 1, rows, :] = run[3]
                hidden_ref[group, 2, rows, :] = run[5]
                forget = sigmoid(pre_forget)
                output = sigmoid(pre_output)
                squashed = jnp.tanh(fresh)
                hidden_cell = output * (1.0 - squashed * squashed) * forget
                hidden_hidden = output * (1.0 - output) * out_weight * squashed
                cell, hidden = (
                    forget * cell + fresh,
                    hidden_cell * cell + hidden_hidden * hidden + output * squashed,
                )
            before, total = sub_blocks(run, compose, UNIT)
            for index, term in enumerate(before):
                prefix_ref[group, index] = term
            for index, term in enumerate(total):
                totals_ref[pl.ds(group * SUB + index, 1), :] = term[SUB - 1 : SUB, :]
            for index in range(len(total), SUB):
                totals_ref[pl.ds(group * SUB + index, 1), :] = jnp.zeros((1, LANES), F32)
            group += 1


def second(own_xor, received, kept, prefixes, weight):
    count = len(received) + 1
    steps = kept[0].shape[2]
    groups = sum(k.shape[0] for k in kept)
    return pl.pallas_call(
        functools.partial(second_kernel, count, own_xor, len(kept)),
        out_shape=(
            pltpu.VMEM((groups, 3, steps, LANES), F32),
            pltpu.VMEM((groups, 6, SUB, LANES), F32),
            pltpu.VMEM((groups * SUB, LANES), F32),
        ),
        in_specs=vmem(count - 1 + 2 * len(kept) + 1),
        out_specs=vmem(3),
        compiler_params=PARAMS,
        cost_estimate=cost(100 * groups * steps * LANES, 24 * groups * steps * LANES),
        name="second",
    )(*received, *kept, *prefixes, weight)


def last_kernel(count, own_xor, *refs):
    received = refs[: count - 1]
    hidden_ref, prefix_ref, out_ref, turn_ref = refs[count - 1 :]
    groups, _, steps, _ = hidden_ref.shape
    runs = steps // SUB
    for group in range(groups):
        cell, hidden = arriving(count, own_xor, received, group, False)
        a, b, c, d, u, v = (prefix_ref[group, j] for j in range(6))
        cell, hidden = a * cell + b * hidden + u, c * cell + d * hidden + v
        for i in range(runs):
            rows = pl.ds(i * SUB, SUB)
            turn_ref[pl.ds(i, SUB, stride=runs), :] = (
                hidden_ref[group, 0, rows, :] * cell
                + hidden_ref[group, 1, rows, :] * hidden
                + hidden_ref[group, 2, rows, :]
            )
        out_ref[pl.ds(group * LANES, LANES), :] = turn_ref[...].T


def last(own_xor, received, hiddens, prefix):
    count = len(received) + 1
    groups, _, steps, _ = hiddens.shape
    return pl.pallas_call(
        functools.partial(last_kernel, count, own_xor),
        out_shape=jax.ShapeDtypeStruct((groups * LANES, steps), F32),
        in_specs=vmem(count + 1),
        compiler_params=PARAMS,
        out_specs=pl.BlockSpec(memory_space=pltpu.VMEM),
        scratch_shapes=[pltpu.VMEM((steps, LANES), F32)],
        cost_estimate=cost(10 * groups * steps * LANES, 16 * groups * steps * LANES),
        name="last",
    )(*received, hiddens, prefix)


def shards(tokens, in_weight, recur_weight, gate_bias, forget_offset):
    steps = tokens.shape[0]
    channels = recur_weight.shape[0]
    groups = channels // LANES
    per_owner = channels * GATES
    owners = lax.axis_size("chan")
    chips = owners // 2
    blocks = lax.axis_size("tm")
    own_xor = blocks & (blocks - 1) == 0

    bias = on_chip(gate_bias.T)
    weight = on_chip(recur_weight.T)
    offset = on_chip(forget_offset.reshape(1, steps))

    def to_core(value):
        return on_chip(lax.ppermute(value, "chan", [(i, i ^ 1) for i in range(owners)]))

    def to_chip(value, away):
        pairs = [(i, (i + 2 * away) % owners) for i in range(owners)]
        return on_chip(lax.ppermute(value, "chan", pairs))

    def to_blocks(value):
        arriving = []
        for k in range(1, blocks):
            pairs = [(i, i ^ k if own_xor else i + k) for i in range(blocks)]
            sent = lax.ppermute(value, "tm", [pair for pair in pairs if pair[1] < blocks])
            arriving.append(on_chip(sent))
        return arriving

    tokens, in_weight = off_chip(tokens), off_chip(in_weight)
    arrived = [[] for _ in range(groups)]
    codes = []
    for away in range(1, chips):
        for group in range(groups):
            give, keep = products(
                tokens, in_weight, chips, away, group * GROUP, GROUP, per_owner, codes[-2:-1]
            )
            given = to_core(give)
            codes.append(encoded(keep, given))
            arrived[group].append(to_chip(codes[-1], away))
    give, keep = products(tokens, in_weight, chips, 0, 0, per_owner, per_owner, codes[-1:])
    given = to_core(give)
    kept, prefixes, totals = [], [], []
    for group in range(groups):
        k, p, total = first(group, 1, keep, given, arrived[group], bias, weight, offset, totals)
        totals = [total]
        kept.append(k)
        prefixes.append(p)
    hiddens, prefix, total = second(own_xor, to_blocks(totals[0]), kept, prefixes, weight)
    return last(own_xor, to_blocks(total), hiddens, prefix)


def solution(mesh):
    placed = (
        P(("groups", "tm"), "chan"),
        P("chan", None),
        P("chan", None),
        P("chan", None),
        P(("groups", "tm")),
    )

    return jax.shard_map(
        shards, mesh=mesh, in_specs=placed, out_specs=P("chan", ("groups", "tm")), check_vma=False
    )
```

```python
import functools

import jax
import jax.numpy as jnp
from jax import lax
from jax.experimental import pallas as pl
from jax.experimental.pallas import tpu as pltpu
from jax.sharding import PartitionSpec as P


LANES = 128
SUB = 8
GATES = 4
GROUP = LANES * GATES
BINADES = 251.0
LOWEST = 125.0
GIVE, KEEP = 0, 1
F32 = jnp.float32
BF16 = jnp.bfloat16


def cost(flops, moved):
    return pl.CostEstimate(flops=int(flops), bytes_accessed=int(moved), transcendentals=0)


def vmem(count):
    return [pl.BlockSpec(memory_space=pltpu.VMEM)] * count


def in_hbm(count):
    return [pl.BlockSpec(memory_space=pltpu.HBM)] * count


def off_chip(value):
    return pltpu.with_memory_space_constraint(value, pltpu.HBM)


def on_chip(value):
    return pltpu.with_memory_space_constraint(value, pltpu.VMEM)


PARAMS = pltpu.CompilerParams(vmem_limit_bytes=16 << 20)


def product_kernel(chips, away, parts, first, per_owner, tile, tokens_ref, weight_ref, *refs):
    outs, (x_ref, w_ref, sems) = refs[-3 - len(parts) : -3], refs[-3:]
    me = lax.axis_index("chan")
    chip, core = me // 2, me % 2
    target = lax.rem(chip + away, chips)
    tiles = outs[0].shape[1] // tile
    slots = len(parts) * tiles
    tokens_copy = pltpu.make_async_copy(tokens_ref, x_ref, sems.at[slots])
    tokens_copy.start()
    copies = []
    for slot in range(slots):
        owner = 2 * target + (core if parts[slot // tiles] == KEEP else 1 - core)
        column = pl.multiple_of(owner * per_owner + first + slot % tiles * tile, tile)
        copies.append(
            pltpu.make_async_copy(
                weight_ref.at[:, pl.ds(column, tile)], w_ref.at[slot], sems.at[slot]
            )
        )
        copies[-1].start()
    tokens_copy.wait()
    for slot, copy in enumerate(copies):
        copy.wait()
        outs[slot // tiles][:, pl.ds(slot % tiles * tile, tile)] = jnp.dot(
            x_ref[...], w_ref[slot], preferred_element_type=F32
        )


def products(tokens, in_weight, chips, away, parts, first, width, per_owner, after):
    steps, depth = tokens.shape
    tile = GROUP
    slots = len(parts) * width // tile
    return pl.pallas_call(
        functools.partial(product_kernel, chips, away, parts, first, per_owner, tile),
        out_shape=[pltpu.VMEM((steps, width), F32)] * len(parts),
        in_specs=in_hbm(2) + vmem(len(after)),
        out_specs=vmem(len(parts)),
        scratch_shapes=[
            pltpu.VMEM((steps, depth), BF16),
            pltpu.VMEM((slots, depth, tile), BF16),
            pltpu.SemaphoreType.DMA((slots + 1,)),
        ],
        compiler_params=PARAMS,
        cost_estimate=cost(2 * slots * steps * depth * tile, 2 * slots * depth * tile),
        name="products",
    )(tokens, in_weight, *after)


def encode_kernel(mine_ref, theirs_ref, out_ref, sum_ref):
    steps, width = mine_ref.shape
    blocks = width // LANES
    top = jnp.zeros((steps, LANES), F32)
    for block in range(blocks):
        cols = pl.ds(block * LANES, LANES)
        both = mine_ref[:, cols] + theirs_ref[:, cols]
        sum_ref[:, cols] = both
        top = jnp.maximum(top, jnp.abs(both))
    top = jnp.max(top, axis=0, keepdims=True)
    top = jnp.maximum(top, 1e-30) * 1.0078125
    scale = top.astype(BF16).astype(F32)
    out_ref[pl.ds(blocks * steps, SUB), :] = jnp.broadcast_to(scale, (SUB, LANES)).astype(BF16)
    inverse = 1.0 / scale
    for block in range(blocks):
        value = sum_ref[:, pl.ds(block * LANES, LANES)]
        level = jnp.sqrt(jnp.abs(value) * inverse) * BINADES - LOWEST
        code = jnp.exp2(level)
        out_ref[pl.ds(block * steps, steps), :] = jnp.where(value < 0.0, -code, code).astype(BF16)


def encoded(mine, theirs):
    steps, width = mine.shape
    rows = steps * (width // LANES) + SUB
    return pl.pallas_call(
        encode_kernel,
        out_shape=pltpu.VMEM((rows, LANES), BF16),
        in_specs=vmem(2),
        out_specs=pl.BlockSpec(memory_space=pltpu.VMEM),
        scratch_shapes=[pltpu.VMEM((steps, width), F32)],
        compiler_params=PARAMS,
        cost_estimate=cost(20 * steps * width, 10 * steps * width),
        name="encode",
    )(mine, theirs)


def decoded(code, scale):
    level = (jnp.log2(jnp.abs(code)) + LOWEST) * (1.0 / BINADES)
    size = level * level * scale
    return jnp.where(code < 0.0, -size, size)


def compose(early, later):
    e1, e2, e3, e4, e5, e6 = early
    l1, l2, l3, l4, l5, l6 = later
    return (
        l1 * e1 + l2 * e3,
        l1 * e2 + l2 * e4,
        l3 * e1 + l4 * e3,
        l3 * e2 + l4 * e4,
        l1 * e5 + l2 * e6 + l5,
        l3 * e5 + l4 * e6 + l6,
    )


def compose_lower(early, later):
    e1, e3, e4, e5, e6 = early
    l1, l3, l4, l5, l6 = later
    return (
        l1 * e1,
        l3 * e1 + l4 * e3,
        l4 * e4,
        l1 * e5 + l5,
        l3 * e5 + l4 * e6 + l6,
    )


def sub_blocks(terms, join, identity):
    row = lax.broadcasted_iota(jnp.int32, (SUB, LANES), 0)
    reach = 1
    while reach < SUB:
        moved = tuple(
            jnp.where(row >= reach, pltpu.roll(term, reach, 0), unit)
            for term, unit in zip(terms, identity)
        )
        terms = join(moved, terms)
        reach *= 2
    before = tuple(
        jnp.where(row >= 1, pltpu.roll(term, 1, 0), unit) for term, unit in zip(terms, identity)
    )
    return before, terms


LOWER_UNIT = (1.0, 0.0, 1.0, 0.0, 0.0)
UNIT = (1.0, 0.0, 0.0, 1.0, 0.0, 0.0)


def sigmoid(x):
    return 1.0 / (1.0 + jnp.exp(-x))


def first_kernel(start, groups, remotes, earlier, *refs):
    refs = list(refs)
    mine_ref, theirs_ref = refs[:2]
    codes = refs[2 : 2 + remotes]
    bias_ref, weight_ref, offset_ref = refs[2 + remotes : 5 + remotes]
    totals_before = refs[5 + remotes : 5 + remotes + earlier]
    kept_ref, prefix_ref, totals_ref, sum_ref, late_ref = refs[5 + remotes + earlier :]
    steps = mine_ref.shape[0]
    runs = steps // SUB
    blocks = groups * GATES
    done = 0
    for ref in totals_before:
        totals_ref[pl.ds(done, ref.shape[0]), :] = ref[...]
        done += ref.shape[0]
    scales = [
        ref[pl.ds(blocks * steps, SUB), :][0:1, :].astype(F32) for ref in codes
    ]
    late_ref[...] = jnp.broadcast_to(offset_ref[...], (LANES, steps)).T
    lane = lax.broadcasted_iota(jnp.int32, (SUB, LANES), 1)
    quarter = lane // (LANES // GATES)
    inner = lane % (LANES // GATES)
    picks = [inner * GATES + (quarter - q + GATES) % GATES for q in range(GATES)]
    for group in range(groups):
        for q in range(GATES):
            block = group * GATES + q
            cols = pl.ds(start * GROUP + block * LANES, LANES)
            value = mine_ref[:, cols] + theirs_ref[:, cols]
            for ref, scale in zip(codes, scales):
                value = value + decoded(ref[pl.ds(block * steps, steps), :].astype(F32), scale)
            sum_ref[q] = value
        channels = pl.ds((start + group) * LANES, LANES)
        biases = [
            jnp.broadcast_to(bias_ref[k : k + 1, channels], (SUB, LANES)) for k in range(GATES)
        ]
        out_weight = jnp.broadcast_to(weight_ref[1:2, channels], (SUB, LANES))
        run = None
        for i in range(runs):
            loaded = [
                jnp.take_along_axis(sum_ref[q, pl.ds(i, SUB, stride=runs), :], picks[q], axis=1)
                for q in range(GATES)
            ]
            pre = []
            for k in range(GATES):
                part = loaded[(0 - k) % GATES]
                for p in range(1, GATES):
                    part = jnp.where(quarter == p, loaded[(p - k) % GATES], part)
                if k:
                    part = pltpu.roll(part, LANES - k * (LANES // GATES), 1)
                pre.append(part + biases[k])
            pre_forget = pre[1] - late_ref[pl.ds(i, SUB, stride=runs), :]
            forget = sigmoid(pre_forget)
            output = sigmoid(pre[3])
            cell = sigmoid(pre[0]) * jnp.tanh(pre[2])
            squashed = jnp.tanh(cell)
            hidden_cell = output * (1.0 - squashed * squashed) * forget
            hidden_hidden = output * (1.0 - output) * out_weight * squashed
            term = (forget, hidden_cell, hidden_hidden, cell, output * squashed)
            run = term if run is None else compose_lower(run, term)
            rows = pl.ds(i * SUB, SUB)
            kept_ref[group, 0, rows, :] = pre_forget
            kept_ref[group, 1, rows, :] = pre[3]
            kept_ref[group, 2, rows, :] = cell
        before, total = sub_blocks(run, compose_lower, LOWER_UNIT)
        for index, term in enumerate(before):
            prefix_ref[group, index] = term
        for index, term in enumerate(total):
            totals_ref[pl.ds(done + group * SUB + index, 1), :] = term[SUB - 1 : SUB, :]
        for index in range(len(total), SUB):
            totals_ref[pl.ds(done + group * SUB + index, 1), :] = jnp.zeros((1, LANES), F32)


def first(start, groups, mine, theirs, codes, bias, weight, offset, earlier):
    steps = mine.shape[0]
    rows = sum(e.shape[0] for e in earlier) + groups * SUB
    count = 5 + len(codes) + len(earlier)
    return pl.pallas_call(
        functools.partial(first_kernel, start, groups, len(codes), len(earlier)),
        out_shape=(
            pltpu.VMEM((groups, 3, steps, LANES), F32),
            pltpu.VMEM((groups, 5, SUB, LANES), F32),
            pltpu.VMEM((rows, LANES), F32),
        ),
        in_specs=vmem(count),
        out_specs=vmem(3),
        scratch_shapes=[
            pltpu.VMEM((GATES, steps, LANES), F32),
            pltpu.VMEM((steps, LANES), F32),
        ],
        compiler_params=PARAMS,
        cost_estimate=cost(60 * steps * groups * GROUP, 20 * steps * groups * GROUP),
        name="first",
    )(mine, theirs, *codes, bias, weight, offset, *earlier)


def in_turn(me, count, own_xor, received):
    for position in range(count - 1):
        picked = received[0]
        for k in range(2, count):
            picked = jnp.where(position == (me ^ k if own_xor else me - k), received[k - 1], picked)
        yield picked, position < me


def arriving(count, own_xor, received, group, lower):
    me = lax.axis_index("tm")
    rows = [ref[pl.ds(group * SUB, SUB), :] for ref in received]
    cell = jnp.zeros((1, LANES), F32)
    hidden = jnp.zeros((1, LANES), F32)
    for maps, counts in in_turn(me, count, own_xor, rows):
        if lower:
            a, c, d, u, v = (maps[j : j + 1, :] for j in range(5))
            new_cell = a * cell + u
        else:
            a, b, c, d, u, v = (maps[j : j + 1, :] for j in range(6))
            new_cell = a * cell + b * hidden + u
        new_hidden = c * cell + d * hidden + v
        cell = jnp.where(counts, new_cell, cell)
        hidden = jnp.where(counts, new_hidden, hidden)
    return cell, hidden


def second_kernel(count, own_xor, chunks, *refs):
    refs = list(refs)
    received = refs[: count - 1]
    kept = refs[count - 1 : count - 1 + chunks]
    prefixes = refs[count - 1 + chunks : count - 1 + 2 * chunks]
    weight_ref = refs[count - 1 + 2 * chunks]
    hidden_ref, prefix_ref, totals_ref = refs[count + 2 * chunks :]
    group = 0
    for kept_ref, before_ref in zip(kept, prefixes):
        groups, _, steps, _ = kept_ref.shape
        for local in range(groups):
            cell, hidden = arriving(count, own_xor, received, group, True)
            a, c, d, u, v = (before_ref[local, j] for j in range(5))
            cell, hidden = a * cell + u, c * cell + d * hidden + v
            channels = pl.ds(group * LANES, LANES)
            forget_weight = jnp.broadcast_to(weight_ref[0:1, channels], (SUB, LANES))
            out_weight = jnp.broadcast_to(weight_ref[1:2, channels], (SUB, LANES))
            run = None
            for i in range(steps // SUB):
                rows = pl.ds(i * SUB, SUB)
                pre_forget = kept_ref[local, 0, rows, :]
                pre_output = kept_ref[local, 1, rows, :]
                fresh = kept_ref[local, 2, rows, :]
                forget = sigmoid(pre_forget + forget_weight * hidden)
                output = sigmoid(pre_output + out_weight * hidden)
                kept_cell = forget * cell
                new_cell = kept_cell + fresh
                squashed = jnp.tanh(new_cell)
                slope = output * (1.0 - squashed * squashed)
                cell_hidden = kept_cell * (1.0 - forget) * forget_weight
                hidden_cell = slope * forget
                hidden_hidden = (
                    output * (1.0 - output) * out_weight * squashed + slope * cell_hidden
                )
                offset_cell = new_cell - kept_cell - cell_hidden * hidden
                offset_hidden = output * squashed - hidden_cell * cell - hidden_hidden * hidden
                term = (
                    forget,
                    cell_hidden,
                    hidden_cell,
                    hidden_hidden,
                    offset_cell,
                    offset_hidden,
                )
                run = term if run is None else compose(run, term)
                hidden_ref[group, 0, rows, :] = run[2]
                hidden_ref[group, 1, rows, :] = run[3]
                hidden_ref[group, 2, rows, :] = run[5]
                forget = sigmoid(pre_forget)
                output = sigmoid(pre_output)
                squashed = jnp.tanh(fresh)
                hidden_cell = output * (1.0 - squashed * squashed) * forget
                hidden_hidden = output * (1.0 - output) * out_weight * squashed
                cell, hidden = (
                    forget * cell + fresh,
                    hidden_cell * cell + hidden_hidden * hidden + output * squashed,
                )
            before, total = sub_blocks(run, compose, UNIT)
            for index, term in enumerate(before):
                prefix_ref[group, index] = term
            for index, term in enumerate(total):
                totals_ref[pl.ds(group * SUB + index, 1), :] = term[SUB - 1 : SUB, :]
            for index in range(len(total), SUB):
                totals_ref[pl.ds(group * SUB + index, 1), :] = jnp.zeros((1, LANES), F32)
            group += 1


def second(own_xor, received, kept, prefixes, weight):
    count = len(received) + 1
    steps = kept[0].shape[2]
    groups = sum(k.shape[0] for k in kept)
    return pl.pallas_call(
        functools.partial(second_kernel, count, own_xor, len(kept)),
        out_shape=(
            pltpu.VMEM((groups, 3, steps, LANES), F32),
            pltpu.VMEM((groups, 6, SUB, LANES), F32),
            pltpu.VMEM((groups * SUB, LANES), F32),
        ),
        in_specs=vmem(count - 1 + 2 * len(kept) + 1),
        out_specs=vmem(3),
        compiler_params=PARAMS,
        cost_estimate=cost(100 * groups * steps * LANES, 24 * groups * steps * LANES),
        name="second",
    )(*received, *kept, *prefixes, weight)


def last_kernel(count, own_xor, *refs):
    received = refs[: count - 1]
    hidden_ref, prefix_ref, out_ref, turn_ref, made_ref, sems = refs[count - 1 :]
    groups, _, steps, _ = hidden_ref.shape
    runs = steps // SUB
    copies = []
    for group in range(groups):
        cell, hidden = arriving(count, own_xor, received, group, False)
        a, b, c, d, u, v = (prefix_ref[group, j] for j in range(6))
        cell, hidden = a * cell + b * hidden + u, c * cell + d * hidden + v
        for i in range(runs):
            rows = pl.ds(i * SUB, SUB)
            turn_ref[pl.ds(i, SUB, stride=runs), :] = (
                hidden_ref[group, 0, rows, :] * cell
                + hidden_ref[group, 1, rows, :] * hidden
                + hidden_ref[group, 2, rows, :]
            )
        rows = pl.ds(group * LANES, LANES)
        made_ref[rows, :] = turn_ref[...].T
        copies.append(pltpu.make_async_copy(made_ref.at[rows], out_ref.at[rows], sems.at[group]))
        copies[-1].start()
    for copy in copies:
        copy.wait()


def last(own_xor, received, hiddens, prefix):
    count = len(received) + 1
    groups, _, steps, _ = hiddens.shape
    return pl.pallas_call(
        functools.partial(last_kernel, count, own_xor),
        out_shape=jax.ShapeDtypeStruct((groups * LANES, steps), F32),
        in_specs=vmem(count + 1),
        compiler_params=PARAMS,
        out_specs=pl.BlockSpec(memory_space=pltpu.HBM),
        scratch_shapes=[
            pltpu.VMEM((steps, LANES), F32),
            pltpu.VMEM((groups * LANES, steps), F32),
            pltpu.SemaphoreType.DMA((groups,)),
        ],
        cost_estimate=cost(10 * groups * steps * LANES, 16 * groups * steps * LANES),
        name="last",
    )(*received, hiddens, prefix)


def shards(tokens, in_weight, recur_weight, gate_bias, forget_offset):
    steps = tokens.shape[0]
    channels = recur_weight.shape[0]
    groups = channels // LANES
    per_owner = channels * GATES
    owners = lax.axis_size("chan")
    chips = owners // 2
    blocks = lax.axis_size("tm")
    own_xor = blocks & (blocks - 1) == 0

    bias = on_chip(gate_bias.T)
    weight = on_chip(recur_weight.T)
    offset = on_chip(forget_offset.reshape(1, steps))

    def to_core(value):
        return on_chip(lax.ppermute(value, "chan", [(i, i ^ 1) for i in range(owners)]))

    def to_chip(value, away):
        pairs = [(i, (i + 2 * away) % owners) for i in range(owners)]
        return on_chip(lax.ppermute(value, "chan", pairs))

    def to_blocks(value):
        arriving = []
        for k in range(1, blocks):
            pairs = [(i, i ^ k if own_xor else i + k) for i in range(blocks)]
            sent = lax.ppermute(value, "tm", [pair for pair in pairs if pair[1] < blocks])
            arriving.append(on_chip(sent))
        return arriving

    tokens, in_weight = off_chip(tokens), off_chip(in_weight)
    arrived = [[] for _ in range(groups)]
    codes = []
    for away in range(1, chips):
        for group in range(groups):
            give, keep = products(
                tokens,
                in_weight,
                chips,
                away,
                (GIVE, KEEP),
                group * GROUP,
                GROUP,
                per_owner,
                codes[-2:-1],
            )
            given = to_core(give)
            codes.append(encoded(keep, given))
            arrived[group].append(to_chip(codes[-1], away))
    local = (per_owner, per_owner, codes[-1:])
    (give,) = products(tokens, in_weight, chips, 0, (GIVE,), 0, *local)
    given = to_core(give)
    (keep,) = products(tokens, in_weight, chips, 0, (KEEP,), 0, *local)
    kept, prefixes, totals = [], [], []
    for group in range(groups):
        k, p, total = first(group, 1, keep, given, arrived[group], bias, weight, offset, totals)
        totals = [total]
        kept.append(k)
        prefixes.append(p)
    hiddens, prefix, total = second(own_xor, to_blocks(totals[0]), kept, prefixes, weight)
    return last(own_xor, to_blocks(total), hiddens, prefix)


def solution(mesh):
    placed = (
        P(("groups", "tm"), "chan"),
        P("chan", None),
        P("chan", None),
        P("chan", None),
        P(("groups", "tm")),
    )

    return jax.shard_map(
        shards, mesh=mesh, in_specs=placed, out_specs=P("chan", ("groups", "tm")), check_vma=False
    )
```

```python
import functools

import jax
import jax.numpy as jnp
from jax import lax
from jax.experimental import pallas as pl
from jax.experimental.pallas import tpu as pltpu
from jax.sharding import PartitionSpec as P


LANES = 128
SUB = 8
GATES = 4
GROUP = LANES * GATES
BINADES = 251.0
LOWEST = 125.0
GIVE, KEEP = 0, 1
F32 = jnp.float32
BF16 = jnp.bfloat16


def cost(flops, moved):
    return pl.CostEstimate(flops=int(flops), bytes_accessed=int(moved), transcendentals=0)


def vmem(count):
    return [pl.BlockSpec(memory_space=pltpu.VMEM)] * count


def in_hbm(count):
    return [pl.BlockSpec(memory_space=pltpu.HBM)] * count


def off_chip(value):
    return pltpu.with_memory_space_constraint(value, pltpu.HBM)


def on_chip(value):
    return pltpu.with_memory_space_constraint(value, pltpu.VMEM)


PARAMS = pltpu.CompilerParams(vmem_limit_bytes=16 << 20)


def product_kernel(chips, away, parts, first, per_owner, tile, tokens_ref, weight_ref, *refs):
    outs, (x_ref, w_ref, sems) = refs[-3 - len(parts) : -3], refs[-3:]
    me = lax.axis_index("chan")
    chip, core = me // 2, me % 2
    target = lax.rem(chip + away, chips)
    tiles = outs[0].shape[1] // tile
    slots = len(parts) * tiles
    tokens_copy = pltpu.make_async_copy(tokens_ref, x_ref, sems.at[slots])
    tokens_copy.start()
    copies = []
    for slot in range(slots):
        owner = 2 * target + (core if parts[slot // tiles] == KEEP else 1 - core)
        column = pl.multiple_of(owner * per_owner + first + slot % tiles * tile, tile)
        copies.append(
            pltpu.make_async_copy(
                weight_ref.at[:, pl.ds(column, tile)], w_ref.at[slot], sems.at[slot]
            )
        )
        copies[-1].start()
    tokens_copy.wait()
    for slot, copy in enumerate(copies):
        copy.wait()
        outs[slot // tiles][:, pl.ds(slot % tiles * tile, tile)] = jnp.dot(
            x_ref[...], w_ref[slot], preferred_element_type=F32
        )


def products(tokens, in_weight, chips, away, parts, first, width, per_owner, after):
    steps, depth = tokens.shape
    tile = GROUP
    slots = len(parts) * width // tile
    return pl.pallas_call(
        functools.partial(product_kernel, chips, away, parts, first, per_owner, tile),
        out_shape=[pltpu.VMEM((steps, width), F32)] * len(parts),
        in_specs=in_hbm(2) + vmem(len(after)),
        out_specs=vmem(len(parts)),
        scratch_shapes=[
            pltpu.VMEM((steps, depth), BF16),
            pltpu.VMEM((slots, depth, tile), BF16),
            pltpu.SemaphoreType.DMA((slots + 1,)),
        ],
        compiler_params=PARAMS,
        cost_estimate=cost(2 * slots * steps * depth * tile, 2 * slots * depth * tile),
        name="products",
    )(tokens, in_weight, *after)


def encode_kernel(mine_ref, theirs_ref, out_ref, sum_ref):
    steps, width = mine_ref.shape
    blocks = width // LANES
    top = jnp.zeros((steps, LANES), F32)
    for block in range(blocks):
        cols = pl.ds(block * LANES, LANES)
        both = mine_ref[:, cols] + theirs_ref[:, cols]
        sum_ref[:, cols] = both
        top = jnp.maximum(top, jnp.abs(both))
    top = jnp.max(top, axis=0, keepdims=True)
    top = jnp.maximum(top, 1e-30) * 1.0078125
    scale = top.astype(BF16).astype(F32)
    out_ref[pl.ds(blocks * steps, SUB), :] = jnp.broadcast_to(scale, (SUB, LANES)).astype(BF16)
    inverse = 1.0 / scale
    for block in range(blocks):
        value = sum_ref[:, pl.ds(block * LANES, LANES)]
        level = jnp.sqrt(jnp.abs(value) * inverse) * BINADES - LOWEST
        code = jnp.exp2(level)
        out_ref[pl.ds(block * steps, steps), :] = jnp.where(value < 0.0, -code, code).astype(BF16)


def encoded(mine, theirs):
    steps, width = mine.shape
    rows = steps * (width // LANES) + SUB
    return pl.pallas_call(
        encode_kernel,
        out_shape=pltpu.VMEM((rows, LANES), BF16),
        in_specs=vmem(2),
        out_specs=pl.BlockSpec(memory_space=pltpu.VMEM),
        scratch_shapes=[pltpu.VMEM((steps, width), F32)],
        compiler_params=PARAMS,
        cost_estimate=cost(20 * steps * width, 10 * steps * width),
        name="encode",
    )(mine, theirs)


def decoded(code, scale):
    level = (jnp.log2(jnp.abs(code)) + LOWEST) * (1.0 / BINADES)
    size = level * level * scale
    return jnp.where(code < 0.0, -size, size)


def compose(early, later):
    e1, e2, e3, e4, e5, e6 = early
    l1, l2, l3, l4, l5, l6 = later
    return (
        l1 * e1 + l2 * e3,
        l1 * e2 + l2 * e4,
        l3 * e1 + l4 * e3,
        l3 * e2 + l4 * e4,
        l1 * e5 + l2 * e6 + l5,
        l3 * e5 + l4 * e6 + l6,
    )


def compose_lower(early, later):
    e1, e3, e4, e5, e6 = early
    l1, l3, l4, l5, l6 = later
    return (
        l1 * e1,
        l3 * e1 + l4 * e3,
        l4 * e4,
        l1 * e5 + l5,
        l3 * e5 + l4 * e6 + l6,
    )


def sub_blocks(terms, join, identity):
    row = lax.broadcasted_iota(jnp.int32, (SUB, LANES), 0)
    reach = 1
    while reach < SUB:
        moved = tuple(
            jnp.where(row >= reach, pltpu.roll(term, reach, 0), unit)
            for term, unit in zip(terms, identity)
        )
        terms = join(moved, terms)
        reach *= 2
    before = tuple(
        jnp.where(row >= 1, pltpu.roll(term, 1, 0), unit) for term, unit in zip(terms, identity)
    )
    return before, terms


LOWER_UNIT = (1.0, 0.0, 1.0, 0.0, 0.0)
UNIT = (1.0, 0.0, 0.0, 1.0, 0.0, 0.0)


def sigmoid(x):
    return 1.0 / (1.0 + jnp.exp(-x))


def first_kernel(start, groups, remotes, earlier, *refs):
    refs = list(refs)
    mine_ref, theirs_ref = refs[:2]
    codes = refs[2 : 2 + remotes]
    bias_ref, weight_ref, offset_ref = refs[2 + remotes : 5 + remotes]
    totals_before = refs[5 + remotes : 5 + remotes + earlier]
    kept_ref, prefix_ref, totals_ref, sum_ref, late_ref = refs[5 + remotes + earlier :]
    steps = mine_ref.shape[0]
    runs = steps // SUB
    blocks = groups * GATES
    done = 0
    for ref in totals_before:
        totals_ref[pl.ds(done, ref.shape[0]), :] = ref[...]
        done += ref.shape[0]
    scales = [
        ref[pl.ds(blocks * steps, SUB), :][0:1, :].astype(F32) for ref in codes
    ]
    late_ref[...] = jnp.broadcast_to(offset_ref[...], (LANES, steps)).T
    lane = lax.broadcasted_iota(jnp.int32, (SUB, LANES), 1)
    quarter = lane // (LANES // GATES)
    inner = lane % (LANES // GATES)
    picks = [inner * GATES + (quarter - q + GATES) % GATES for q in range(GATES)]
    for group in range(groups):
        for q in range(GATES):
            block = group * GATES + q
            cols = pl.ds(start * GROUP + block * LANES, LANES)
            value = mine_ref[:, cols] + theirs_ref[:, cols]
            for ref, scale in zip(codes, scales):
                value = value + decoded(ref[pl.ds(block * steps, steps), :].astype(F32), scale)
            sum_ref[q] = value
        channels = pl.ds((start + group) * LANES, LANES)
        biases = [
            jnp.broadcast_to(bias_ref[k : k + 1, channels], (SUB, LANES)) for k in range(GATES)
        ]
        out_weight = jnp.broadcast_to(weight_ref[1:2, channels], (SUB, LANES))
        run = None
        for i in range(runs):
            loaded = [
                jnp.take_along_axis(sum_ref[q, pl.ds(i, SUB, stride=runs), :], picks[q], axis=1)
                for q in range(GATES)
            ]
            pre = []
            for k in range(GATES):
                part = loaded[(0 - k) % GATES]
                for p in range(1, GATES):
                    part = jnp.where(quarter == p, loaded[(p - k) % GATES], part)
                if k:
                    part = pltpu.roll(part, LANES - k * (LANES // GATES), 1)
                pre.append(part + biases[k])
            pre_forget = pre[1] - late_ref[pl.ds(i, SUB, stride=runs), :]
            forget = sigmoid(pre_forget)
            output = sigmoid(pre[3])
            cell = sigmoid(pre[0]) * jnp.tanh(pre[2])
            squashed = jnp.tanh(cell)
            hidden_cell = output * (1.0 - squashed * squashed) * forget
            hidden_hidden = output * (1.0 - output) * out_weight * squashed
            term = (forget, hidden_cell, hidden_hidden, cell, output * squashed)
            run = term if run is None else compose_lower(run, term)
            rows = pl.ds(i * SUB, SUB)
            kept_ref[group, 0, rows, :] = pre_forget
            kept_ref[group, 1, rows, :] = pre[3]
            kept_ref[group, 2, rows, :] = cell
        before, total = sub_blocks(run, compose_lower, LOWER_UNIT)
        for index, term in enumerate(before):
            prefix_ref[group, index] = term
        for index, term in enumerate(total):
            totals_ref[pl.ds(done + group * SUB + index, 1), :] = term[SUB - 1 : SUB, :]
        for index in range(len(total), SUB):
            totals_ref[pl.ds(done + group * SUB + index, 1), :] = jnp.zeros((1, LANES), F32)


def first(start, groups, mine, theirs, codes, bias, weight, offset, earlier):
    steps = mine.shape[0]
    rows = sum(e.shape[0] for e in earlier) + groups * SUB
    count = 5 + len(codes) + len(earlier)
    return pl.pallas_call(
        functools.partial(first_kernel, start, groups, len(codes), len(earlier)),
        out_shape=(
            pltpu.VMEM((groups, 3, steps, LANES), F32),
            pltpu.VMEM((groups, 5, SUB, LANES), F32),
            pltpu.VMEM((rows, LANES), F32),
        ),
        in_specs=vmem(count),
        out_specs=vmem(3),
        scratch_shapes=[
            pltpu.VMEM((GATES, steps, LANES), F32),
            pltpu.VMEM((steps, LANES), F32),
        ],
        compiler_params=PARAMS,
        cost_estimate=cost(60 * steps * groups * GROUP, 20 * steps * groups * GROUP),
        name="first",
    )(mine, theirs, *codes, bias, weight, offset, *earlier)


def in_turn(me, count, own_xor, received):
    for position in range(count - 1):
        picked = received[0]
        for k in range(2, count):
            picked = jnp.where(position == (me ^ k if own_xor else me - k), received[k - 1], picked)
        yield picked, position < me


def arriving(count, own_xor, received, group, lower):
    me = lax.axis_index("tm")
    rows = [ref[pl.ds(group * SUB, SUB), :] for ref in received]
    cell = jnp.zeros((1, LANES), F32)
    hidden = jnp.zeros((1, LANES), F32)
    for maps, counts in in_turn(me, count, own_xor, rows):
        if lower:
            a, c, d, u, v = (maps[j : j + 1, :] for j in range(5))
            new_cell = a * cell + u
        else:
            a, b, c, d, u, v = (maps[j : j + 1, :] for j in range(6))
            new_cell = a * cell + b * hidden + u
        new_hidden = c * cell + d * hidden + v
        cell = jnp.where(counts, new_cell, cell)
        hidden = jnp.where(counts, new_hidden, hidden)
    return cell, hidden


def second_kernel(count, own_xor, chunks, *refs):
    refs = list(refs)
    received = refs[: count - 1]
    kept = refs[count - 1 : count - 1 + chunks]
    prefixes = refs[count - 1 + chunks : count - 1 + 2 * chunks]
    weight_ref = refs[count - 1 + 2 * chunks]
    hidden_ref, prefix_ref, totals_ref = refs[count + 2 * chunks :]
    group = 0
    for kept_ref, before_ref in zip(kept, prefixes):
        groups, _, steps, _ = kept_ref.shape
        for local in range(groups):
            cell, hidden = arriving(count, own_xor, received, group, True)
            a, c, d, u, v = (before_ref[local, j] for j in range(5))
            cell, hidden = a * cell + u, c * cell + d * hidden + v
            channels = pl.ds(group * LANES, LANES)
            forget_weight = jnp.broadcast_to(weight_ref[0:1, channels], (SUB, LANES))
            out_weight = jnp.broadcast_to(weight_ref[1:2, channels], (SUB, LANES))
            run = None
            for i in range(steps // SUB):
                rows = pl.ds(i * SUB, SUB)
                pre_forget = kept_ref[local, 0, rows, :]
                pre_output = kept_ref[local, 1, rows, :]
                fresh = kept_ref[local, 2, rows, :]
                forget = sigmoid(pre_forget + forget_weight * hidden)
                output = sigmoid(pre_output + out_weight * hidden)
                kept_cell = forget * cell
                new_cell = kept_cell + fresh
                squashed = jnp.tanh(new_cell)
                slope = output * (1.0 - squashed * squashed)
                cell_hidden = kept_cell * (1.0 - forget) * forget_weight
                hidden_cell = slope * forget
                hidden_hidden = (
                    output * (1.0 - output) * out_weight * squashed + slope * cell_hidden
                )
                offset_cell = new_cell - kept_cell - cell_hidden * hidden
                offset_hidden = output * squashed - hidden_cell * cell - hidden_hidden * hidden
                term = (
                    forget,
                    cell_hidden,
                    hidden_cell,
                    hidden_hidden,
                    offset_cell,
                    offset_hidden,
                )
                run = term if run is None else compose(run, term)
                hidden_ref[group, 0, rows, :] = run[2]
                hidden_ref[group, 1, rows, :] = run[3]
                hidden_ref[group, 2, rows, :] = run[5]
                forget = sigmoid(pre_forget)
                output = sigmoid(pre_output)
                squashed = jnp.tanh(fresh)
                hidden_cell = output * (1.0 - squashed * squashed) * forget
                hidden_hidden = output * (1.0 - output) * out_weight * squashed
                cell, hidden = (
                    forget * cell + fresh,
                    hidden_cell * cell + hidden_hidden * hidden + output * squashed,
                )
            before, total = sub_blocks(run, compose, UNIT)
            for index, term in enumerate(before):
                prefix_ref[group, index] = term
            for index, term in enumerate(total):
                totals_ref[pl.ds(group * SUB + index, 1), :] = term[SUB - 1 : SUB, :]
            for index in range(len(total), SUB):
                totals_ref[pl.ds(group * SUB + index, 1), :] = jnp.zeros((1, LANES), F32)
            group += 1


def second(own_xor, received, kept, prefixes, weight):
    count = len(received) + 1
    steps = kept[0].shape[2]
    groups = sum(k.shape[0] for k in kept)
    return pl.pallas_call(
        functools.partial(second_kernel, count, own_xor, len(kept)),
        out_shape=(
            pltpu.VMEM((groups, 3, steps, LANES), F32),
            pltpu.VMEM((groups, 6, SUB, LANES), F32),
            pltpu.VMEM((groups * SUB, LANES), F32),
        ),
        in_specs=vmem(count - 1 + 2 * len(kept) + 1),
        out_specs=vmem(3),
        compiler_params=PARAMS,
        cost_estimate=cost(100 * groups * steps * LANES, 24 * groups * steps * LANES),
        name="second",
    )(*received, *kept, *prefixes, weight)


def last_kernel(count, own_xor, *refs):
    received = refs[: count - 1]
    hidden_ref, prefix_ref, out_ref, turn_ref, made_ref, sems = refs[count - 1 :]
    groups, _, steps, _ = hidden_ref.shape
    runs = steps // SUB
    copies = []
    for group in range(groups):
        cell, hidden = arriving(count, own_xor, received, group, False)
        a, b, c, d, u, v = (prefix_ref[group, j] for j in range(6))
        cell, hidden = a * cell + b * hidden + u, c * cell + d * hidden + v
        for i in range(runs):
            rows = pl.ds(i * SUB, SUB)
            turn_ref[pl.ds(i, SUB, stride=runs), :] = (
                hidden_ref[group, 0, rows, :] * cell
                + hidden_ref[group, 1, rows, :] * hidden
                + hidden_ref[group, 2, rows, :]
            )
        rows = pl.ds(group * LANES, LANES)
        made_ref[rows, :] = turn_ref[...].T
        copies.append(pltpu.make_async_copy(made_ref.at[rows], out_ref.at[rows], sems.at[group]))
        copies[-1].start()
    for copy in copies:
        copy.wait()


def last(own_xor, received, hiddens, prefix):
    count = len(received) + 1
    groups, _, steps, _ = hiddens.shape
    return pl.pallas_call(
        functools.partial(last_kernel, count, own_xor),
        out_shape=jax.ShapeDtypeStruct((groups * LANES, steps), F32),
        in_specs=vmem(count + 1),
        compiler_params=PARAMS,
        out_specs=pl.BlockSpec(memory_space=pltpu.HBM),
        scratch_shapes=[
            pltpu.VMEM((steps, LANES), F32),
            pltpu.VMEM((groups * LANES, steps), F32),
            pltpu.SemaphoreType.DMA((groups,)),
        ],
        cost_estimate=cost(10 * groups * steps * LANES, 16 * groups * steps * LANES),
        name="last",
    )(*received, hiddens, prefix)


def chunks_of(groups):
    half = max(1, groups // 2)
    return [(0, half)] + [(group, 1) for group in range(half, groups)]


def shards(tokens, in_weight, recur_weight, gate_bias, forget_offset):
    steps = tokens.shape[0]
    channels = recur_weight.shape[0]
    groups = channels // LANES
    per_owner = channels * GATES
    owners = lax.axis_size("chan")
    chips = owners // 2
    blocks = lax.axis_size("tm")
    own_xor = blocks & (blocks - 1) == 0

    bias = on_chip(gate_bias.T)
    weight = on_chip(recur_weight.T)
    offset = on_chip(forget_offset.reshape(1, steps))

    def to_core(value):
        return on_chip(lax.ppermute(value, "chan", [(i, i ^ 1) for i in range(owners)]))

    def to_chip(value, away):
        pairs = [(i, (i + 2 * away) % owners) for i in range(owners)]
        return on_chip(lax.ppermute(value, "chan", pairs))

    def to_blocks(value):
        arriving = []
        for k in range(1, blocks):
            pairs = [(i, i ^ k if own_xor else i + k) for i in range(blocks)]
            sent = lax.ppermute(value, "tm", [pair for pair in pairs if pair[1] < blocks])
            arriving.append(on_chip(sent))
        return arriving

    tokens, in_weight = off_chip(tokens), off_chip(in_weight)
    chunks = chunks_of(groups)
    arrived = [[] for _ in chunks]
    codes = []
    for away in range(1, chips):
        for slot, (start, count) in enumerate(chunks):
            give, keep = products(
                tokens,
                in_weight,
                chips,
                away,
                (GIVE, KEEP),
                start * GROUP,
                count * GROUP,
                per_owner,
                codes[-2:-1],
            )
            given = to_core(give)
            codes.append(encoded(keep, given))
            arrived[slot].append(to_chip(codes[-1], away))
    local = (per_owner, per_owner, codes[-1:])
    (give,) = products(tokens, in_weight, chips, 0, (GIVE,), 0, *local)
    given = to_core(give)
    (keep,) = products(tokens, in_weight, chips, 0, (KEEP,), 0, *local)
    kept, prefixes, totals = [], [], []
    for (start, count), codes in zip(chunks, arrived):
        k, p, total = first(start, count, keep, given, codes, bias, weight, offset, totals)
        totals = [total]
        kept.append(k)
        prefixes.append(p)
    hiddens, prefix, total = second(own_xor, to_blocks(totals[0]), kept, prefixes, weight)
    return last(own_xor, to_blocks(total), hiddens, prefix)


def solution(mesh):
    placed = (
        P(("groups", "tm"), "chan"),
        P("chan", None),
        P("chan", None),
        P("chan", None),
        P(("groups", "tm")),
    )

    return jax.shard_map(
        shards, mesh=mesh, in_specs=placed, out_specs=P("chan", ("groups", "tm")), check_vma=False
    )
```

```python
import functools

import jax
import jax.numpy as jnp
from jax import lax
from jax.experimental import pallas as pl
from jax.experimental.pallas import tpu as pltpu
from jax.sharding import PartitionSpec as P


LANES = 128
SUB = 8
GATES = 4
GROUP = LANES * GATES
BINADES = 251.0
LOWEST = 125.0
GIVE, KEEP = 0, 1
HALVES = 2
F32 = jnp.float32
BF16 = jnp.bfloat16


def cost(flops, moved):
    return pl.CostEstimate(flops=int(flops), bytes_accessed=int(moved), transcendentals=0)


def vmem(count):
    return [pl.BlockSpec(memory_space=pltpu.VMEM)] * count


def in_hbm(count):
    return [pl.BlockSpec(memory_space=pltpu.HBM)] * count


def off_chip(value):
    return pltpu.with_memory_space_constraint(value, pltpu.HBM)


def on_chip(value):
    return pltpu.with_memory_space_constraint(value, pltpu.VMEM)


PARAMS = pltpu.CompilerParams(vmem_limit_bytes=16 << 20)


def product_kernel(chips, away, parts, first, per_owner, tile, tokens_ref, weight_ref, *refs):
    outs, (x_ref, w_ref, sems) = refs[-3 - len(parts) : -3], refs[-3:]
    me = lax.axis_index("chan")
    chip, core = me // 2, me % 2
    target = lax.rem(chip + away, chips)
    tiles = outs[0].shape[1] // tile
    slots = len(parts) * tiles
    depth = x_ref.shape[1] // HALVES
    tokens_copy = pltpu.make_async_copy(tokens_ref, x_ref, sems.at[slots * HALVES])
    tokens_copy.start()
    copies = []
    for slot in range(slots):
        owner = 2 * target + (core if parts[slot // tiles] == KEEP else 1 - core)
        column = pl.multiple_of(owner * per_owner + first + slot % tiles * tile, tile)
        for half in range(HALVES):
            rows = pl.ds(half * depth, depth)
            copies.append(
                pltpu.make_async_copy(
                    weight_ref.at[rows, pl.ds(column, tile)],
                    w_ref.at[slot, rows],
                    sems.at[slot * HALVES + half],
                )
            )
            copies[-1].start()
    tokens_copy.wait()
    for index, copy in enumerate(copies):
        slot, half = index // HALVES, index % HALVES
        rows = pl.ds(half * depth, depth)
        out_ref, cols = outs[slot // tiles], pl.ds(slot % tiles * tile, tile)
        copy.wait()
        part = jnp.dot(x_ref[:, rows], w_ref[slot, rows, :], preferred_element_type=F32)
        out_ref[:, cols] = part if half == 0 else out_ref[:, cols] + part


def products(tokens, in_weight, chips, away, parts, first, width, per_owner, after):
    steps, depth = tokens.shape
    tile = GROUP
    slots = len(parts) * width // tile
    return pl.pallas_call(
        functools.partial(product_kernel, chips, away, parts, first, per_owner, tile),
        out_shape=[pltpu.VMEM((steps, width), F32)] * len(parts),
        in_specs=in_hbm(2) + vmem(len(after)),
        out_specs=vmem(len(parts)),
        scratch_shapes=[
            pltpu.VMEM((steps, depth), BF16),
            pltpu.VMEM((slots, depth, tile), BF16),
            pltpu.SemaphoreType.DMA((slots * HALVES + 1,)),
        ],
        compiler_params=PARAMS,
        cost_estimate=cost(2 * slots * steps * depth * tile, 2 * slots * depth * tile),
        name="products",
    )(tokens, in_weight, *after)


def encode_kernel(mine_ref, theirs_ref, out_ref, sum_ref):
    steps, width = mine_ref.shape
    blocks = width // LANES
    top = jnp.zeros((steps, LANES), F32)
    for block in range(blocks):
        cols = pl.ds(block * LANES, LANES)
        both = mine_ref[:, cols] + theirs_ref[:, cols]
        sum_ref[:, cols] = both
        top = jnp.maximum(top, jnp.abs(both))
    top = jnp.max(top, axis=0, keepdims=True)
    top = jnp.maximum(top, 1e-30) * 1.0078125
    scale = top.astype(BF16).astype(F32)
    out_ref[pl.ds(blocks * steps, SUB), :] = jnp.broadcast_to(scale, (SUB, LANES)).astype(BF16)
    inverse = 1.0 / scale
    for block in range(blocks):
        value = sum_ref[:, pl.ds(block * LANES, LANES)]
        level = jnp.sqrt(jnp.abs(value) * inverse) * BINADES - LOWEST
        code = jnp.exp2(level)
        out_ref[pl.ds(block * steps, steps), :] = jnp.where(value < 0.0, -code, code).astype(BF16)


def encoded(mine, theirs):
    steps, width = mine.shape
    rows = steps * (width // LANES) + SUB
    return pl.pallas_call(
        encode_kernel,
        out_shape=pltpu.VMEM((rows, LANES), BF16),
        in_specs=vmem(2),
        out_specs=pl.BlockSpec(memory_space=pltpu.VMEM),
        scratch_shapes=[pltpu.VMEM((steps, width), F32)],
        compiler_params=PARAMS,
        cost_estimate=cost(20 * steps * width, 10 * steps * width),
        name="encode",
    )(mine, theirs)


def decoded(code, scale):
    level = (jnp.log2(jnp.abs(code)) + LOWEST) * (1.0 / BINADES)
    size = level * level * scale
    return jnp.where(code < 0.0, -size, size)


def compose(early, later):
    e1, e2, e3, e4, e5, e6 = early
    l1, l2, l3, l4, l5, l6 = later
    return (
        l1 * e1 + l2 * e3,
        l1 * e2 + l2 * e4,
        l3 * e1 + l4 * e3,
        l3 * e2 + l4 * e4,
        l1 * e5 + l2 * e6 + l5,
        l3 * e5 + l4 * e6 + l6,
    )


def compose_lower(early, later):
    e1, e3, e4, e5, e6 = early
    l1, l3, l4, l5, l6 = later
    return (
        l1 * e1,
        l3 * e1 + l4 * e3,
        l4 * e4,
        l1 * e5 + l5,
        l3 * e5 + l4 * e6 + l6,
    )


def sub_blocks(terms, join, identity):
    row = lax.broadcasted_iota(jnp.int32, (SUB, LANES), 0)
    reach = 1
    while reach < SUB:
        moved = tuple(
            jnp.where(row >= reach, pltpu.roll(term, reach, 0), unit)
            for term, unit in zip(terms, identity)
        )
        terms = join(moved, terms)
        reach *= 2
    before = tuple(
        jnp.where(row >= 1, pltpu.roll(term, 1, 0), unit) for term, unit in zip(terms, identity)
    )
    return before, terms


LOWER_UNIT = (1.0, 0.0, 1.0, 0.0, 0.0)
UNIT = (1.0, 0.0, 0.0, 1.0, 0.0, 0.0)


def sigmoid(x):
    return 1.0 / (1.0 + jnp.exp(-x))


def first_kernel(start, place, remotes, earlier, *refs):
    groups = 1
    refs = list(refs)
    mine_ref, theirs_ref = refs[:2]
    codes = refs[2 : 2 + remotes]
    bias_ref, weight_ref, offset_ref = refs[2 + remotes : 5 + remotes]
    totals_before = refs[5 + remotes : 5 + remotes + earlier]
    kept_ref, prefix_ref, totals_ref, sum_ref, late_ref = refs[5 + remotes + earlier :]
    steps = mine_ref.shape[0]
    runs = steps // SUB
    done = 0
    for ref in totals_before:
        totals_ref[pl.ds(done, ref.shape[0]), :] = ref[...]
        done += ref.shape[0]
    scales = [
        ref[pl.ds(ref.shape[0] - SUB, SUB), :][0:1, :].astype(F32) for ref in codes
    ]
    late_ref[...] = jnp.broadcast_to(offset_ref[...], (LANES, steps)).T
    lane = lax.broadcasted_iota(jnp.int32, (SUB, LANES), 1)
    quarter = lane // (LANES // GATES)
    inner = lane % (LANES // GATES)
    picks = [inner * GATES + (quarter - q + GATES) % GATES for q in range(GATES)]
    for group in range(groups):
        for q in range(GATES):
            block = group * GATES + q
            cols = pl.ds(start * GROUP + block * LANES, LANES)
            value = mine_ref[:, cols] + theirs_ref[:, cols]
            for ref, scale in zip(codes, scales):
                rows = pl.ds((place * GATES + block) * steps, steps)
                value = value + decoded(ref[rows, :].astype(F32), scale)
            sum_ref[q] = value
        channels = pl.ds((start + group) * LANES, LANES)
        biases = [
            jnp.broadcast_to(bias_ref[k : k + 1, channels], (SUB, LANES)) for k in range(GATES)
        ]
        out_weight = jnp.broadcast_to(weight_ref[1:2, channels], (SUB, LANES))
        run = None
        for i in range(runs):
            loaded = [
                jnp.take_along_axis(sum_ref[q, pl.ds(i, SUB, stride=runs), :], picks[q], axis=1)
                for q in range(GATES)
            ]
            pre = []
            for k in range(GATES):
                part = loaded[(0 - k) % GATES]
                for p in range(1, GATES):
                    part = jnp.where(quarter == p, loaded[(p - k) % GATES], part)
                if k:
                    part = pltpu.roll(part, LANES - k * (LANES // GATES), 1)
                pre.append(part + biases[k])
            pre_forget = pre[1] - late_ref[pl.ds(i, SUB, stride=runs), :]
            forget = sigmoid(pre_forget)
            output = sigmoid(pre[3])
            cell = sigmoid(pre[0]) * jnp.tanh(pre[2])
            squashed = jnp.tanh(cell)
            hidden_cell = output * (1.0 - squashed * squashed) * forget
            hidden_hidden = output * (1.0 - output) * out_weight * squashed
            term = (forget, hidden_cell, hidden_hidden, cell, output * squashed)
            run = term if run is None else compose_lower(run, term)
            rows = pl.ds(i * SUB, SUB)
            kept_ref[group, 0, rows, :] = pre_forget
            kept_ref[group, 1, rows, :] = pre[3]
            kept_ref[group, 2, rows, :] = cell
        before, total = sub_blocks(run, compose_lower, LOWER_UNIT)
        for index, term in enumerate(before):
            prefix_ref[group, index] = term
        for index, term in enumerate(total):
            totals_ref[pl.ds(done + group * SUB + index, 1), :] = term[SUB - 1 : SUB, :]
        for index in range(len(total), SUB):
            totals_ref[pl.ds(done + group * SUB + index, 1), :] = jnp.zeros((1, LANES), F32)


def first(start, place, mine, theirs, codes, bias, weight, offset, earlier):
    steps = mine.shape[0]
    groups = 1
    rows = sum(e.shape[0] for e in earlier) + groups * SUB
    count = 5 + len(codes) + len(earlier)
    return pl.pallas_call(
        functools.partial(first_kernel, start, place, len(codes), len(earlier)),
        out_shape=(
            pltpu.VMEM((groups, 3, steps, LANES), F32),
            pltpu.VMEM((groups, 5, SUB, LANES), F32),
            pltpu.VMEM((rows, LANES), F32),
        ),
        in_specs=vmem(count),
        out_specs=vmem(3),
        scratch_shapes=[
            pltpu.VMEM((GATES, steps, LANES), F32),
            pltpu.VMEM((steps, LANES), F32),
        ],
        compiler_params=PARAMS,
        cost_estimate=cost(60 * steps * groups * GROUP, 20 * steps * groups * GROUP),
        name="first",
    )(mine, theirs, *codes, bias, weight, offset, *earlier)


def in_turn(me, count, own_xor, received):
    for position in range(count - 1):
        picked = received[0]
        for k in range(2, count):
            picked = jnp.where(position == (me ^ k if own_xor else me - k), received[k - 1], picked)
        yield picked, position < me


def arriving(count, own_xor, received, group, lower):
    me = lax.axis_index("tm")
    rows = [ref[pl.ds(group * SUB, SUB), :] for ref in received]
    cell = jnp.zeros((1, LANES), F32)
    hidden = jnp.zeros((1, LANES), F32)
    for maps, counts in in_turn(me, count, own_xor, rows):
        if lower:
            a, c, d, u, v = (maps[j : j + 1, :] for j in range(5))
            new_cell = a * cell + u
        else:
            a, b, c, d, u, v = (maps[j : j + 1, :] for j in range(6))
            new_cell = a * cell + b * hidden + u
        new_hidden = c * cell + d * hidden + v
        cell = jnp.where(counts, new_cell, cell)
        hidden = jnp.where(counts, new_hidden, hidden)
    return cell, hidden


def second_kernel(count, own_xor, chunks, *refs):
    refs = list(refs)
    received = refs[: count - 1]
    kept = refs[count - 1 : count - 1 + chunks]
    prefixes = refs[count - 1 + chunks : count - 1 + 2 * chunks]
    weight_ref = refs[count - 1 + 2 * chunks]
    hidden_ref, prefix_ref, totals_ref = refs[count + 2 * chunks :]
    group = 0
    for kept_ref, before_ref in zip(kept, prefixes):
        groups, _, steps, _ = kept_ref.shape
        for local in range(groups):
            cell, hidden = arriving(count, own_xor, received, group, True)
            a, c, d, u, v = (before_ref[local, j] for j in range(5))
            cell, hidden = a * cell + u, c * cell + d * hidden + v
            channels = pl.ds(group * LANES, LANES)
            forget_weight = jnp.broadcast_to(weight_ref[0:1, channels], (SUB, LANES))
            out_weight = jnp.broadcast_to(weight_ref[1:2, channels], (SUB, LANES))
            run = None
            for i in range(steps // SUB):
                rows = pl.ds(i * SUB, SUB)
                pre_forget = kept_ref[local, 0, rows, :]
                pre_output = kept_ref[local, 1, rows, :]
                fresh = kept_ref[local, 2, rows, :]
                forget = sigmoid(pre_forget + forget_weight * hidden)
                output = sigmoid(pre_output + out_weight * hidden)
                kept_cell = forget * cell
                new_cell = kept_cell + fresh
                squashed = jnp.tanh(new_cell)
                slope = output * (1.0 - squashed * squashed)
                cell_hidden = kept_cell * (1.0 - forget) * forget_weight
                hidden_cell = slope * forget
                hidden_hidden = (
                    output * (1.0 - output) * out_weight * squashed + slope * cell_hidden
                )
                offset_cell = new_cell - kept_cell - cell_hidden * hidden
                offset_hidden = output * squashed - hidden_cell * cell - hidden_hidden * hidden
                term = (
                    forget,
                    cell_hidden,
                    hidden_cell,
                    hidden_hidden,
                    offset_cell,
                    offset_hidden,
                )
                run = term if run is None else compose(run, term)
                hidden_ref[group, 0, rows, :] = run[2]
                hidden_ref[group, 1, rows, :] = run[3]
                hidden_ref[group, 2, rows, :] = run[5]
                forget = sigmoid(pre_forget)
                output = sigmoid(pre_output)
                squashed = jnp.tanh(fresh)
                hidden_cell = output * (1.0 - squashed * squashed) * forget
                hidden_hidden = output * (1.0 - output) * out_weight * squashed
                cell, hidden = (
                    forget * cell + fresh,
                    hidden_cell * cell + hidden_hidden * hidden + output * squashed,
                )
            before, total = sub_blocks(run, compose, UNIT)
            for index, term in enumerate(before):
                prefix_ref[group, index] = term
            for index, term in enumerate(total):
                totals_ref[pl.ds(group * SUB + index, 1), :] = term[SUB - 1 : SUB, :]
            for index in range(len(total), SUB):
                totals_ref[pl.ds(group * SUB + index, 1), :] = jnp.zeros((1, LANES), F32)
            group += 1


def second(own_xor, received, kept, prefixes, weight):
    count = len(received) + 1
    steps = kept[0].shape[2]
    groups = sum(k.shape[0] for k in kept)
    return pl.pallas_call(
        functools.partial(second_kernel, count, own_xor, len(kept)),
        out_shape=(
            pltpu.VMEM((groups, 3, steps, LANES), F32),
            pltpu.VMEM((groups, 6, SUB, LANES), F32),
            pltpu.VMEM((groups * SUB, LANES), F32),
        ),
        in_specs=vmem(count - 1 + 2 * len(kept) + 1),
        out_specs=vmem(3),
        compiler_params=PARAMS,
        cost_estimate=cost(100 * groups * steps * LANES, 24 * groups * steps * LANES),
        name="second",
    )(*received, *kept, *prefixes, weight)


def last_kernel(count, own_xor, *refs):
    received = refs[: count - 1]
    hidden_ref, prefix_ref, out_ref, turn_ref, made_ref, sems = refs[count - 1 :]
    groups, _, steps, _ = hidden_ref.shape
    runs = steps // SUB
    copies = []
    for group in range(groups):
        cell, hidden = arriving(count, own_xor, received, group, False)
        a, b, c, d, u, v = (prefix_ref[group, j] for j in range(6))
        cell, hidden = a * cell + b * hidden + u, c * cell + d * hidden + v
        for i in range(runs):
            rows = pl.ds(i * SUB, SUB)
            turn_ref[pl.ds(i, SUB, stride=runs), :] = (
                hidden_ref[group, 0, rows, :] * cell
                + hidden_ref[group, 1, rows, :] * hidden
                + hidden_ref[group, 2, rows, :]
            )
        rows = pl.ds(group * LANES, LANES)
        made_ref[rows, :] = turn_ref[...].T
        copies.append(pltpu.make_async_copy(made_ref.at[rows], out_ref.at[rows], sems.at[group]))
        copies[-1].start()
    for copy in copies:
        copy.wait()


def last(own_xor, received, hiddens, prefix):
    count = len(received) + 1
    groups, _, steps, _ = hiddens.shape
    return pl.pallas_call(
        functools.partial(last_kernel, count, own_xor),
        out_shape=jax.ShapeDtypeStruct((groups * LANES, steps), F32),
        in_specs=vmem(count + 1),
        compiler_params=PARAMS,
        out_specs=pl.BlockSpec(memory_space=pltpu.HBM),
        scratch_shapes=[
            pltpu.VMEM((steps, LANES), F32),
            pltpu.VMEM((groups * LANES, steps), F32),
            pltpu.SemaphoreType.DMA((groups,)),
        ],
        cost_estimate=cost(10 * groups * steps * LANES, 16 * groups * steps * LANES),
        name="last",
    )(*received, hiddens, prefix)


def chunks_of(groups):
    middle = [(1, groups - 2)] if groups > 2 else []
    return [(0, 1)] + middle + [(groups - 1, 1)] * (groups > 1)


def shards(tokens, in_weight, recur_weight, gate_bias, forget_offset):
    steps = tokens.shape[0]
    channels = recur_weight.shape[0]
    groups = channels // LANES
    per_owner = channels * GATES
    owners = lax.axis_size("chan")
    chips = owners // 2
    blocks = lax.axis_size("tm")
    own_xor = blocks & (blocks - 1) == 0

    bias = on_chip(gate_bias.T)
    weight = on_chip(recur_weight.T)
    offset = on_chip(forget_offset.reshape(1, steps))

    def to_core(value):
        return on_chip(lax.ppermute(value, "chan", [(i, i ^ 1) for i in range(owners)]))

    def to_chip(value, away):
        pairs = [(i, (i + 2 * away) % owners) for i in range(owners)]
        return on_chip(lax.ppermute(value, "chan", pairs))

    def to_blocks(value):
        arriving = []
        for k in range(1, blocks):
            pairs = [(i, i ^ k if own_xor else i + k) for i in range(blocks)]
            sent = lax.ppermute(value, "tm", [pair for pair in pairs if pair[1] < blocks])
            arriving.append(on_chip(sent))
        return arriving

    tokens, in_weight = off_chip(tokens), off_chip(in_weight)
    chunks = chunks_of(groups)
    arrived = [[] for _ in chunks]
    codes = []
    for away in range(1, chips):
        for slot, (start, count) in enumerate(chunks):
            give, keep = products(
                tokens,
                in_weight,
                chips,
                away,
                (GIVE, KEEP),
                start * GROUP,
                count * GROUP,
                per_owner,
                codes[-2:-1],
            )
            given = to_core(give)
            codes.append(encoded(keep, given))
            arrived[slot].append(to_chip(codes[-1], away))
    local = (per_owner, per_owner, codes[-1:])
    (give,) = products(tokens, in_weight, chips, 0, (GIVE,), 0, *local)
    given = to_core(give)
    (keep,) = products(tokens, in_weight, chips, 0, (KEEP,), 0, *local)
    kept, prefixes, totals = [], [], []
    for (start, count), codes in zip(chunks, arrived):
        for place in range(count):
            k, p, total = first(
                start + place, place, keep, given, codes, bias, weight, offset, totals
            )
            totals = [total]
            kept.append(k)
            prefixes.append(p)
    hiddens, prefix, total = second(own_xor, to_blocks(totals[0]), kept, prefixes, weight)
    return last(own_xor, to_blocks(total), hiddens, prefix)


def solution(mesh):
    placed = (
        P(("groups", "tm"), "chan"),
        P("chan", None),
        P("chan", None),
        P("chan", None),
        P(("groups", "tm")),
    )

    return jax.shard_map(
        shards, mesh=mesh, in_specs=placed, out_specs=P("chan", ("groups", "tm")), check_vma=False
    )
```

```python
import functools

import jax
import jax.numpy as jnp
from jax import lax
from jax.experimental import pallas as pl
from jax.experimental.pallas import tpu as pltpu
from jax.sharding import PartitionSpec as P


LANES = 128
SUB = 8
GATES = 4
GROUP = LANES * GATES
BINADES = 251.0
LOWEST = 125.0
GIVE, KEEP = 0, 1
HALVES = 1
F32 = jnp.float32
BF16 = jnp.bfloat16


def cost(flops, moved):
    return pl.CostEstimate(flops=int(flops), bytes_accessed=int(moved), transcendentals=0)


def vmem(count):
    return [pl.BlockSpec(memory_space=pltpu.VMEM)] * count


def in_hbm(count):
    return [pl.BlockSpec(memory_space=pltpu.HBM)] * count


def off_chip(value):
    return pltpu.with_memory_space_constraint(value, pltpu.HBM)


def on_chip(value):
    return pltpu.with_memory_space_constraint(value, pltpu.VMEM)


PARAMS = pltpu.CompilerParams(vmem_limit_bytes=16 << 20)


def product_kernel(chips, away, parts, first, per_owner, tile, tokens_ref, weight_ref, *refs):
    outs, (x_ref, w_ref, sems) = refs[-3 - len(parts) : -3], refs[-3:]
    me = lax.axis_index("chan")
    chip, core = me // 2, me % 2
    target = lax.rem(chip + away, chips)
    tiles = outs[0].shape[1] // tile
    slots = len(parts) * tiles
    depth = x_ref.shape[1] // HALVES
    tokens_copy = pltpu.make_async_copy(tokens_ref, x_ref, sems.at[slots * HALVES])
    tokens_copy.start()
    copies = []
    for slot in range(slots):
        owner = 2 * target + (core if parts[slot // tiles] == KEEP else 1 - core)
        column = pl.multiple_of(owner * per_owner + first + slot % tiles * tile, tile)
        for half in range(HALVES):
            rows = pl.ds(half * depth, depth)
            copies.append(
                pltpu.make_async_copy(
                    weight_ref.at[rows, pl.ds(column, tile)],
                    w_ref.at[slot, rows],
                    sems.at[slot * HALVES + half],
                )
            )
            copies[-1].start()
    tokens_copy.wait()
    for index, copy in enumerate(copies):
        slot, half = index // HALVES, index % HALVES
        rows = pl.ds(half * depth, depth)
        out_ref, cols = outs[slot // tiles], pl.ds(slot % tiles * tile, tile)
        copy.wait()
        part = jnp.dot(x_ref[:, rows], w_ref[slot, rows, :], preferred_element_type=F32)
        out_ref[:, cols] = part if half == 0 else out_ref[:, cols] + part


def products(tokens, in_weight, chips, away, parts, first, width, per_owner, after):
    steps, depth = tokens.shape
    tile = GROUP
    slots = len(parts) * width // tile
    return pl.pallas_call(
        functools.partial(product_kernel, chips, away, parts, first, per_owner, tile),
        out_shape=[pltpu.VMEM((steps, width), F32)] * len(parts),
        in_specs=in_hbm(2) + vmem(len(after)),
        out_specs=vmem(len(parts)),
        scratch_shapes=[
            pltpu.VMEM((steps, depth), BF16),
            pltpu.VMEM((slots, depth, tile), BF16),
            pltpu.SemaphoreType.DMA((slots * HALVES + 1,)),
        ],
        compiler_params=PARAMS,
        cost_estimate=cost(2 * slots * steps * depth * tile, 2 * slots * depth * tile),
        name="products",
    )(tokens, in_weight, *after)


def encode_kernel(mine_ref, theirs_ref, out_ref, sum_ref):
    steps, width = mine_ref.shape
    blocks = width // LANES
    top = jnp.zeros((steps, LANES), F32)
    for block in range(blocks):
        cols = pl.ds(block * LANES, LANES)
        both = mine_ref[:, cols] + theirs_ref[:, cols]
        sum_ref[:, cols] = both
        top = jnp.maximum(top, jnp.abs(both))
    top = jnp.max(top, axis=0, keepdims=True)
    top = jnp.maximum(top, 1e-30) * 1.0078125
    scale = top.astype(BF16).astype(F32)
    out_ref[pl.ds(blocks * steps, SUB), :] = jnp.broadcast_to(scale, (SUB, LANES)).astype(BF16)
    inverse = 1.0 / scale
    for block in range(blocks):
        value = sum_ref[:, pl.ds(block * LANES, LANES)]
        level = jnp.sqrt(jnp.abs(value) * inverse) * BINADES - LOWEST
        code = jnp.exp2(level)
        out_ref[pl.ds(block * steps, steps), :] = jnp.where(value < 0.0, -code, code).astype(BF16)


def encoded(mine, theirs):
    steps, width = mine.shape
    rows = steps * (width // LANES) + SUB
    return pl.pallas_call(
        encode_kernel,
        out_shape=pltpu.VMEM((rows, LANES), BF16),
        in_specs=vmem(2),
        out_specs=pl.BlockSpec(memory_space=pltpu.VMEM),
        scratch_shapes=[pltpu.VMEM((steps, width), F32)],
        compiler_params=PARAMS,
        cost_estimate=cost(20 * steps * width, 10 * steps * width),
        name="encode",
    )(mine, theirs)


def decoded(code, scale):
    level = (jnp.log2(jnp.abs(code)) + LOWEST) * (1.0 / BINADES)
    size = level * level * scale
    return jnp.where(code < 0.0, -size, size)


def compose(early, later):
    e1, e2, e3, e4, e5, e6 = early
    l1, l2, l3, l4, l5, l6 = later
    return (
        l1 * e1 + l2 * e3,
        l1 * e2 + l2 * e4,
        l3 * e1 + l4 * e3,
        l3 * e2 + l4 * e4,
        l1 * e5 + l2 * e6 + l5,
        l3 * e5 + l4 * e6 + l6,
    )


def compose_lower(early, later):
    e1, e3, e4, e5, e6 = early
    l1, l3, l4, l5, l6 = later
    return (
        l1 * e1,
        l3 * e1 + l4 * e3,
        l4 * e4,
        l1 * e5 + l5,
        l3 * e5 + l4 * e6 + l6,
    )


def sub_blocks(terms, join, identity):
    row = lax.broadcasted_iota(jnp.int32, (SUB, LANES), 0)
    reach = 1
    while reach < SUB:
        moved = tuple(
            jnp.where(row >= reach, pltpu.roll(term, reach, 0), unit)
            for term, unit in zip(terms, identity)
        )
        terms = join(moved, terms)
        reach *= 2
    before = tuple(
        jnp.where(row >= 1, pltpu.roll(term, 1, 0), unit) for term, unit in zip(terms, identity)
    )
    return before, terms


LOWER_UNIT = (1.0, 0.0, 1.0, 0.0, 0.0)
UNIT = (1.0, 0.0, 0.0, 1.0, 0.0, 0.0)


def sigmoid(x):
    return 1.0 / (1.0 + jnp.exp(-x))


def first_kernel(start, place, remotes, earlier, *refs):
    groups = 1
    refs = list(refs)
    mine_ref, theirs_ref = refs[:2]
    codes = refs[2 : 2 + remotes]
    bias_ref, weight_ref, offset_ref = refs[2 + remotes : 5 + remotes]
    totals_before = refs[5 + remotes : 5 + remotes + earlier]
    kept_ref, prefix_ref, totals_ref, sum_ref, late_ref = refs[5 + remotes + earlier :]
    steps = mine_ref.shape[0]
    runs = steps // SUB
    done = 0
    for ref in totals_before:
        totals_ref[pl.ds(done, ref.shape[0]), :] = ref[...]
        done += ref.shape[0]
    scales = [
        ref[pl.ds(ref.shape[0] - SUB, SUB), :][0:1, :].astype(F32) for ref in codes
    ]
    late_ref[...] = jnp.broadcast_to(offset_ref[...], (LANES, steps)).T
    lane = lax.broadcasted_iota(jnp.int32, (SUB, LANES), 1)
    quarter = lane // (LANES // GATES)
    inner = lane % (LANES // GATES)
    picks = [inner * GATES + (quarter - q + GATES) % GATES for q in range(GATES)]
    for group in range(groups):
        for q in range(GATES):
            block = group * GATES + q
            cols = pl.ds(start * GROUP + block * LANES, LANES)
            value = mine_ref[:, cols] + theirs_ref[:, cols]
            for ref, scale in zip(codes, scales):
                rows = pl.ds((place * GATES + block) * steps, steps)
                value = value + decoded(ref[rows, :].astype(F32), scale)
            sum_ref[q] = value
        channels = pl.ds((start + group) * LANES, LANES)
        biases = [
            jnp.broadcast_to(bias_ref[k : k + 1, channels], (SUB, LANES)) for k in range(GATES)
        ]
        out_weight = jnp.broadcast_to(weight_ref[1:2, channels], (SUB, LANES))
        run = None
        for i in range(runs):
            loaded = [
                jnp.take_along_axis(sum_ref[q, pl.ds(i, SUB, stride=runs), :], picks[q], axis=1)
                for q in range(GATES)
            ]
            pre = []
            for k in range(GATES):
                part = loaded[(0 - k) % GATES]
                for p in range(1, GATES):
                    part = jnp.where(quarter == p, loaded[(p - k) % GATES], part)
                if k:
                    part = pltpu.roll(part, LANES - k * (LANES // GATES), 1)
                pre.append(part + biases[k])
            pre_forget = pre[1] - late_ref[pl.ds(i, SUB, stride=runs), :]
            forget = sigmoid(pre_forget)
            output = sigmoid(pre[3])
            cell = sigmoid(pre[0]) * jnp.tanh(pre[2])
            squashed = jnp.tanh(cell)
            hidden_cell = output * (1.0 - squashed * squashed) * forget
            hidden_hidden = output * (1.0 - output) * out_weight * squashed
            term = (forget, hidden_cell, hidden_hidden, cell, output * squashed)
            run = term if run is None else compose_lower(run, term)
            rows = pl.ds(i * SUB, SUB)
            kept_ref[group, 0, rows, :] = pre_forget
            kept_ref[group, 1, rows, :] = pre[3]
            kept_ref[group, 2, rows, :] = cell
        before, total = sub_blocks(run, compose_lower, LOWER_UNIT)
        for index, term in enumerate(before):
            prefix_ref[group, index] = term
        for index, term in enumerate(total):
            totals_ref[pl.ds(done + group * SUB + index, 1), :] = term[SUB - 1 : SUB, :]
        for index in range(len(total), SUB):
            totals_ref[pl.ds(done + group * SUB + index, 1), :] = jnp.zeros((1, LANES), F32)


def first(start, place, mine, theirs, codes, bias, weight, offset, earlier):
    steps = mine.shape[0]
    groups = 1
    rows = sum(e.shape[0] for e in earlier) + groups * SUB
    count = 5 + len(codes) + len(earlier)
    return pl.pallas_call(
        functools.partial(first_kernel, start, place, len(codes), len(earlier)),
        out_shape=(
            pltpu.VMEM((groups, 3, steps, LANES), F32),
            pltpu.VMEM((groups, 5, SUB, LANES), F32),
            pltpu.VMEM((rows, LANES), F32),
        ),
        in_specs=vmem(count),
        out_specs=vmem(3),
        scratch_shapes=[
            pltpu.VMEM((GATES, steps, LANES), F32),
            pltpu.VMEM((steps, LANES), F32),
        ],
        compiler_params=PARAMS,
        cost_estimate=cost(60 * steps * groups * GROUP, 20 * steps * groups * GROUP),
        name="first",
    )(mine, theirs, *codes, bias, weight, offset, *earlier)


def in_turn(me, count, own_xor, received):
    for position in range(count - 1):
        picked = received[0]
        for k in range(2, count):
            picked = jnp.where(position == (me ^ k if own_xor else me - k), received[k - 1], picked)
        yield picked, position < me


def arriving(count, own_xor, received, group, lower):
    me = lax.axis_index("tm")
    rows = [ref[pl.ds(group * SUB, SUB), :] for ref in received]
    cell = jnp.zeros((1, LANES), F32)
    hidden = jnp.zeros((1, LANES), F32)
    for maps, counts in in_turn(me, count, own_xor, rows):
        if lower:
            a, c, d, u, v = (maps[j : j + 1, :] for j in range(5))
            new_cell = a * cell + u
        else:
            a, b, c, d, u, v = (maps[j : j + 1, :] for j in range(6))
            new_cell = a * cell + b * hidden + u
        new_hidden = c * cell + d * hidden + v
        cell = jnp.where(counts, new_cell, cell)
        hidden = jnp.where(counts, new_hidden, hidden)
    return cell, hidden


def second_kernel(count, own_xor, chunks, *refs):
    refs = list(refs)
    received = refs[: count - 1]
    kept = refs[count - 1 : count - 1 + chunks]
    prefixes = refs[count - 1 + chunks : count - 1 + 2 * chunks]
    weight_ref = refs[count - 1 + 2 * chunks]
    hidden_ref, prefix_ref, totals_ref = refs[count + 2 * chunks :]
    group = 0
    for kept_ref, before_ref in zip(kept, prefixes):
        groups, _, steps, _ = kept_ref.shape
        for local in range(groups):
            cell, hidden = arriving(count, own_xor, received, group, True)
            a, c, d, u, v = (before_ref[local, j] for j in range(5))
            cell, hidden = a * cell + u, c * cell + d * hidden + v
            channels = pl.ds(group * LANES, LANES)
            forget_weight = jnp.broadcast_to(weight_ref[0:1, channels], (SUB, LANES))
            out_weight = jnp.broadcast_to(weight_ref[1:2, channels], (SUB, LANES))
            run = None
            for i in range(steps // SUB):
                rows = pl.ds(i * SUB, SUB)
                pre_forget = kept_ref[local, 0, rows, :]
                pre_output = kept_ref[local, 1, rows, :]
                fresh = kept_ref[local, 2, rows, :]
                forget = sigmoid(pre_forget + forget_weight * hidden)
                output = sigmoid(pre_output + out_weight * hidden)
                kept_cell = forget * cell
                new_cell = kept_cell + fresh
                squashed = jnp.tanh(new_cell)
                slope = output * (1.0 - squashed * squashed)
                cell_hidden = kept_cell * (1.0 - forget) * forget_weight
                hidden_cell = slope * forget
                hidden_hidden = (
                    output * (1.0 - output) * out_weight * squashed + slope * cell_hidden
                )
                offset_cell = new_cell - kept_cell - cell_hidden * hidden
                offset_hidden = output * squashed - hidden_cell * cell - hidden_hidden * hidden
                term = (
                    forget,
                    cell_hidden,
                    hidden_cell,
                    hidden_hidden,
                    offset_cell,
                    offset_hidden,
                )
                run = term if run is None else compose(run, term)
                hidden_ref[group, 0, rows, :] = run[2]
                hidden_ref[group, 1, rows, :] = run[3]
                hidden_ref[group, 2, rows, :] = run[5]
                forget = sigmoid(pre_forget)
                output = sigmoid(pre_output)
                squashed = jnp.tanh(fresh)
                hidden_cell = output * (1.0 - squashed * squashed) * forget
                hidden_hidden = output * (1.0 - output) * out_weight * squashed
                cell, hidden = (
                    forget * cell + fresh,
                    hidden_cell * cell + hidden_hidden * hidden + output * squashed,
                )
            before, total = sub_blocks(run, compose, UNIT)
            for index, term in enumerate(before):
                prefix_ref[group, index] = term
            for index, term in enumerate(total):
                totals_ref[pl.ds(group * SUB + index, 1), :] = term[SUB - 1 : SUB, :]
            for index in range(len(total), SUB):
                totals_ref[pl.ds(group * SUB + index, 1), :] = jnp.zeros((1, LANES), F32)
            group += 1


def second(own_xor, received, kept, prefixes, weight):
    count = len(received) + 1
    steps = kept[0].shape[2]
    groups = sum(k.shape[0] for k in kept)
    return pl.pallas_call(
        functools.partial(second_kernel, count, own_xor, len(kept)),
        out_shape=(
            pltpu.VMEM((groups, 3, steps, LANES), F32),
            pltpu.VMEM((groups, 6, SUB, LANES), F32),
            pltpu.VMEM((groups * SUB, LANES), F32),
        ),
        in_specs=vmem(count - 1 + 2 * len(kept) + 1),
        out_specs=vmem(3),
        compiler_params=PARAMS,
        cost_estimate=cost(100 * groups * steps * LANES, 24 * groups * steps * LANES),
        name="second",
    )(*received, *kept, *prefixes, weight)


def last_kernel(count, own_xor, *refs):
    received = refs[: count - 1]
    hidden_ref, prefix_ref, out_ref, turn_ref, made_ref, sems = refs[count - 1 :]
    groups, _, steps, _ = hidden_ref.shape
    runs = steps // SUB
    copies = []
    for group in range(groups):
        cell, hidden = arriving(count, own_xor, received, group, False)
        a, b, c, d, u, v = (prefix_ref[group, j] for j in range(6))
        cell, hidden = a * cell + b * hidden + u, c * cell + d * hidden + v
        for i in range(runs):
            rows = pl.ds(i * SUB, SUB)
            turn_ref[pl.ds(i, SUB, stride=runs), :] = (
                hidden_ref[group, 0, rows, :] * cell
                + hidden_ref[group, 1, rows, :] * hidden
                + hidden_ref[group, 2, rows, :]
            )
        rows = pl.ds(group * LANES, LANES)
        made_ref[rows, :] = turn_ref[...].T
        copies.append(pltpu.make_async_copy(made_ref.at[rows], out_ref.at[rows], sems.at[group]))
        copies[-1].start()
    for copy in copies:
        copy.wait()


def last(own_xor, received, hiddens, prefix):
    count = len(received) + 1
    groups, _, steps, _ = hiddens.shape
    return pl.pallas_call(
        functools.partial(last_kernel, count, own_xor),
        out_shape=jax.ShapeDtypeStruct((groups * LANES, steps), F32),
        in_specs=vmem(count + 1),
        compiler_params=PARAMS,
        out_specs=pl.BlockSpec(memory_space=pltpu.HBM),
        scratch_shapes=[
            pltpu.VMEM((steps, LANES), F32),
            pltpu.VMEM((groups * LANES, steps), F32),
            pltpu.SemaphoreType.DMA((groups,)),
        ],
        cost_estimate=cost(10 * groups * steps * LANES, 16 * groups * steps * LANES),
        name="last",
    )(*received, hiddens, prefix)


def chunks_of(groups):
    half = max(1, groups // 2)
    return [(0, half)] + [(group, 1) for group in range(half, groups)]


def shards(tokens, in_weight, recur_weight, gate_bias, forget_offset):
    steps = tokens.shape[0]
    channels = recur_weight.shape[0]
    groups = channels // LANES
    per_owner = channels * GATES
    owners = lax.axis_size("chan")
    chips = owners // 2
    blocks = lax.axis_size("tm")
    own_xor = blocks & (blocks - 1) == 0

    bias = on_chip(gate_bias.T)
    weight = on_chip(recur_weight.T)
    offset = on_chip(forget_offset.reshape(1, steps))

    def to_core(value):
        return on_chip(lax.ppermute(value, "chan", [(i, i ^ 1) for i in range(owners)]))

    def to_chip(value, away):
        pairs = [(i, (i + 2 * away) % owners) for i in range(owners)]
        return on_chip(lax.ppermute(value, "chan", pairs))

    def to_blocks(value):
        arriving = []
        for k in range(1, blocks):
            pairs = [(i, i ^ k if own_xor else i + k) for i in range(blocks)]
            sent = lax.ppermute(value, "tm", [pair for pair in pairs if pair[1] < blocks])
            arriving.append(on_chip(sent))
        return arriving

    tokens, in_weight = off_chip(tokens), off_chip(in_weight)
    chunks = chunks_of(groups)
    arrived = [[] for _ in chunks]
    codes = []
    for away in range(1, chips):
        for slot, (start, count) in enumerate(chunks):
            after = codes[-2:][:1]

            def partial(parts):
                return products(
                    tokens,
                    in_weight,
                    chips,
                    away,
                    parts,
                    start * GROUP,
                    count * GROUP,
                    per_owner,
                    after,
                )

            if codes:
                give, keep = partial((GIVE, KEEP))
            else:
                (give,) = partial((GIVE,))
                (keep,) = partial((KEEP,))
            given = to_core(give)
            codes.append(encoded(keep, given))
            arrived[slot].append(to_chip(codes[-1], away))
    local = (per_owner, per_owner, codes[-1:])
    (give,) = products(tokens, in_weight, chips, 0, (GIVE,), 0, *local)
    given = to_core(give)
    (keep,) = products(tokens, in_weight, chips, 0, (KEEP,), 0, *local)
    kept, prefixes, totals = [], [], []
    for (start, count), codes in zip(chunks, arrived):
        for place in range(count):
            k, p, total = first(
                start + place, place, keep, given, codes, bias, weight, offset, totals
            )
            totals = [total]
            kept.append(k)
            prefixes.append(p)
    hiddens, prefix, total = second(own_xor, to_blocks(totals[0]), kept, prefixes, weight)
    return last(own_xor, to_blocks(total), hiddens, prefix)


def solution(mesh):
    placed = (
        P(("groups", "tm"), "chan"),
        P("chan", None),
        P("chan", None),
        P("chan", None),
        P(("groups", "tm")),
    )

    return jax.shard_map(
        shards, mesh=mesh, in_specs=placed, out_specs=P("chan", ("groups", "tm")), check_vma=False
    )
```

```python
import functools

import jax
import jax.numpy as jnp
from jax import lax
from jax.experimental import pallas as pl
from jax.experimental.pallas import tpu as pltpu
from jax.sharding import PartitionSpec as P


LANES = 128
SUB = 8
GATES = 4
GROUP = LANES * GATES
BINADES = 251.0
LOWEST = 125.0
GIVE, KEEP = 0, 1
F32 = jnp.float32
BF16 = jnp.bfloat16


def cost(flops, moved):
    return pl.CostEstimate(flops=int(flops), bytes_accessed=int(moved), transcendentals=0)


def vmem(count):
    return [pl.BlockSpec(memory_space=pltpu.VMEM)] * count


def in_hbm(count):
    return [pl.BlockSpec(memory_space=pltpu.HBM)] * count


def off_chip(value):
    return pltpu.with_memory_space_constraint(value, pltpu.HBM)


def on_chip(value):
    return pltpu.with_memory_space_constraint(value, pltpu.VMEM)


PARAMS = pltpu.CompilerParams(vmem_limit_bytes=16 << 20)


def product_kernel(chips, parts, per_owner, tokens_ref, weight_ref, *refs):
    outs, (x_ref, w_ref, sems) = refs[-3 - len(parts) : -3], refs[-3:]
    me = lax.axis_index("chan")
    chip, core = me // 2, me % 2
    tokens_copy = pltpu.make_async_copy(tokens_ref, x_ref, sems.at[w_ref.shape[0]])
    tokens_copy.start()
    copies = []
    for (away, which, first, width), out_ref in zip(parts, outs):
        owner = 2 * lax.rem(chip + away, chips) + (core if which == KEEP else 1 - core)
        for start in range(0, width, GROUP):
            slot = len(copies)
            column = pl.multiple_of(owner * per_owner + first + start, GROUP)
            copy = pltpu.make_async_copy(
                weight_ref.at[:, pl.ds(column, GROUP)], w_ref.at[slot], sems.at[slot]
            )
            copy.start()
            copies.append((copy, out_ref, start))
    tokens_copy.wait()
    for slot, (copy, out_ref, start) in enumerate(copies):
        copy.wait()
        out_ref[:, pl.ds(start, GROUP)] = jnp.dot(
            x_ref[...], w_ref[slot], preferred_element_type=F32
        )


def products(tokens, in_weight, chips, per_owner, parts, after):
    steps, depth = tokens.shape
    slots = sum(width for _, _, _, width in parts) // GROUP
    return pl.pallas_call(
        functools.partial(product_kernel, chips, parts, per_owner),
        out_shape=[pltpu.VMEM((steps, width), F32) for _, _, _, width in parts],
        in_specs=in_hbm(2) + vmem(len(after)),
        out_specs=vmem(len(parts)),
        scratch_shapes=[
            pltpu.VMEM((steps, depth), BF16),
            pltpu.VMEM((slots, depth, GROUP), BF16),
            pltpu.SemaphoreType.DMA((slots + 1,)),
        ],
        compiler_params=PARAMS,
        cost_estimate=cost(2 * slots * steps * depth * GROUP, 2 * slots * depth * GROUP),
        name="products",
    )(tokens, in_weight, *after)


def encode_kernel(first, mine_ref, theirs_ref, out_ref, sum_ref):
    steps, width = sum_ref.shape
    blocks = width // LANES
    top = jnp.zeros((steps, LANES), F32)
    for block in range(blocks):
        cols = pl.ds(first + block * LANES, LANES)
        both = mine_ref[:, cols] + theirs_ref[:, cols]
        sum_ref[:, pl.ds(block * LANES, LANES)] = both
        top = jnp.maximum(top, jnp.abs(both))
    top = jnp.max(top, axis=0, keepdims=True)
    top = jnp.maximum(top, 1e-30) * 1.0078125
    scale = top.astype(BF16).astype(F32)
    out_ref[pl.ds(blocks * steps, SUB), :] = jnp.broadcast_to(scale, (SUB, LANES)).astype(BF16)
    inverse = 1.0 / scale
    for block in range(blocks):
        value = sum_ref[:, pl.ds(block * LANES, LANES)]
        level = jnp.sqrt(jnp.abs(value) * inverse) * BINADES - LOWEST
        code = jnp.exp2(level)
        out_ref[pl.ds(block * steps, steps), :] = jnp.where(value < 0.0, -code, code).astype(BF16)


def encoded(mine, theirs, first, width):
    steps = mine.shape[0]
    rows = steps * (width // LANES) + SUB
    return pl.pallas_call(
        functools.partial(encode_kernel, first),
        out_shape=pltpu.VMEM((rows, LANES), BF16),
        in_specs=vmem(2),
        out_specs=pl.BlockSpec(memory_space=pltpu.VMEM),
        scratch_shapes=[pltpu.VMEM((steps, width), F32)],
        compiler_params=PARAMS,
        cost_estimate=cost(20 * steps * width, 10 * steps * width),
        name="encode",
    )(mine, theirs)


def decoded(code, scale):
    level = (jnp.log2(jnp.abs(code)) + LOWEST) * (1.0 / BINADES)
    size = level * level * scale
    return jnp.where(code < 0.0, -size, size)


def compose(early, later):
    e1, e2, e3, e4, e5, e6 = early
    l1, l2, l3, l4, l5, l6 = later
    return (
        l1 * e1 + l2 * e3,
        l1 * e2 + l2 * e4,
        l3 * e1 + l4 * e3,
        l3 * e2 + l4 * e4,
        l1 * e5 + l2 * e6 + l5,
        l3 * e5 + l4 * e6 + l6,
    )


def compose_lower(early, later):
    e1, e3, e4, e5, e6 = early
    l1, l3, l4, l5, l6 = later
    return (
        l1 * e1,
        l3 * e1 + l4 * e3,
        l4 * e4,
        l1 * e5 + l5,
        l3 * e5 + l4 * e6 + l6,
    )


def sub_blocks(terms, join, identity):
    row = lax.broadcasted_iota(jnp.int32, (SUB, LANES), 0)
    reach = 1
    while reach < SUB:
        moved = tuple(
            jnp.where(row >= reach, pltpu.roll(term, reach, 0), unit)
            for term, unit in zip(terms, identity)
        )
        terms = join(moved, terms)
        reach *= 2
    before = tuple(
        jnp.where(row >= 1, pltpu.roll(term, 1, 0), unit) for term, unit in zip(terms, identity)
    )
    return before, terms


LOWER_UNIT = (1.0, 0.0, 1.0, 0.0, 0.0)
UNIT = (1.0, 0.0, 0.0, 1.0, 0.0, 0.0)


def sigmoid(x):
    return 1.0 / (1.0 + jnp.exp(-x))


def first_kernel(start, places, earlier, *refs):
    groups, remotes = 1, len(places)
    refs = list(refs)
    mine_ref, theirs_ref = refs[:2]
    codes = refs[2 : 2 + remotes]
    bias_ref, weight_ref, offset_ref = refs[2 + remotes : 5 + remotes]
    totals_before = refs[5 + remotes : 5 + remotes + earlier]
    kept_ref, prefix_ref, totals_ref, sum_ref, late_ref = refs[5 + remotes + earlier :]
    steps = mine_ref.shape[0]
    runs = steps // SUB
    done = 0
    for ref in totals_before:
        totals_ref[pl.ds(done, ref.shape[0]), :] = ref[...]
        done += ref.shape[0]
    scales = [
        ref[pl.ds(ref.shape[0] - SUB, SUB), :][0:1, :].astype(F32) for ref in codes
    ]
    late_ref[...] = jnp.broadcast_to(offset_ref[...], (LANES, steps)).T
    lane = lax.broadcasted_iota(jnp.int32, (SUB, LANES), 1)
    quarter = lane // (LANES // GATES)
    inner = lane % (LANES // GATES)
    picks = [inner * GATES + (quarter - q + GATES) % GATES for q in range(GATES)]
    for group in range(groups):
        for q in range(GATES):
            block = group * GATES + q
            cols = pl.ds(start * GROUP + block * LANES, LANES)
            value = mine_ref[:, cols] + theirs_ref[:, cols]
            for ref, scale, place in zip(codes, scales, places):
                rows = pl.ds((place * GATES + block) * steps, steps)
                value = value + decoded(ref[rows, :].astype(F32), scale)
            sum_ref[q] = value
        channels = pl.ds((start + group) * LANES, LANES)
        biases = [
            jnp.broadcast_to(bias_ref[k : k + 1, channels], (SUB, LANES)) for k in range(GATES)
        ]
        out_weight = jnp.broadcast_to(weight_ref[1:2, channels], (SUB, LANES))
        run = None
        for i in range(runs):
            loaded = [
                jnp.take_along_axis(sum_ref[q, pl.ds(i, SUB, stride=runs), :], picks[q], axis=1)
                for q in range(GATES)
            ]
            pre = []
            for k in range(GATES):
                part = loaded[(0 - k) % GATES]
                for p in range(1, GATES):
                    part = jnp.where(quarter == p, loaded[(p - k) % GATES], part)
                if k:
                    part = pltpu.roll(part, LANES - k * (LANES // GATES), 1)
                pre.append(part + biases[k])
            pre_forget = pre[1] - late_ref[pl.ds(i, SUB, stride=runs), :]
            forget = sigmoid(pre_forget)
            output = sigmoid(pre[3])
            cell = sigmoid(pre[0]) * jnp.tanh(pre[2])
            squashed = jnp.tanh(cell)
            hidden_cell = output * (1.0 - squashed * squashed) * forget
            hidden_hidden = output * (1.0 - output) * out_weight * squashed
            term = (forget, hidden_cell, hidden_hidden, cell, output * squashed)
            run = term if run is None else compose_lower(run, term)
            rows = pl.ds(i * SUB, SUB)
            kept_ref[group, 0, rows, :] = pre_forget
            kept_ref[group, 1, rows, :] = pre[3]
            kept_ref[group, 2, rows, :] = cell
        before, total = sub_blocks(run, compose_lower, LOWER_UNIT)
        for index, term in enumerate(before):
            prefix_ref[group, index] = term
        for index, term in enumerate(total):
            totals_ref[pl.ds(done + group * SUB + index, 1), :] = term[SUB - 1 : SUB, :]
        for index in range(len(total), SUB):
            totals_ref[pl.ds(done + group * SUB + index, 1), :] = jnp.zeros((1, LANES), F32)


def first(start, places, mine, theirs, codes, bias, weight, offset, earlier):
    steps = mine.shape[0]
    groups = 1
    rows = sum(e.shape[0] for e in earlier) + groups * SUB
    count = 5 + len(codes) + len(earlier)
    return pl.pallas_call(
        functools.partial(first_kernel, start, places, len(earlier)),
        out_shape=(
            pltpu.VMEM((groups, 3, steps, LANES), F32),
            pltpu.VMEM((groups, 5, SUB, LANES), F32),
            pltpu.VMEM((rows, LANES), F32),
        ),
        in_specs=vmem(count),
        out_specs=vmem(3),
        scratch_shapes=[
            pltpu.VMEM((GATES, steps, LANES), F32),
            pltpu.VMEM((steps, LANES), F32),
        ],
        compiler_params=PARAMS,
        cost_estimate=cost(60 * steps * groups * GROUP, 20 * steps * groups * GROUP),
        name="first",
    )(mine, theirs, *codes, bias, weight, offset, *earlier)


def in_turn(me, count, own_xor, received):
    for position in range(count - 1):
        picked = received[0]
        for k in range(2, count):
            picked = jnp.where(position == (me ^ k if own_xor else me - k), received[k - 1], picked)
        yield picked, position < me


def arriving(count, own_xor, received, group, lower):
    me = lax.axis_index("tm")
    rows = [ref[pl.ds(group * SUB, SUB), :] for ref in received]
    cell = jnp.zeros((1, LANES), F32)
    hidden = jnp.zeros((1, LANES), F32)
    for maps, counts in in_turn(me, count, own_xor, rows):
        if lower:
            a, c, d, u, v = (maps[j : j + 1, :] for j in range(5))
            new_cell = a * cell + u
        else:
            a, b, c, d, u, v = (maps[j : j + 1, :] for j in range(6))
            new_cell = a * cell + b * hidden + u
        new_hidden = c * cell + d * hidden + v
        cell = jnp.where(counts, new_cell, cell)
        hidden = jnp.where(counts, new_hidden, hidden)
    return cell, hidden


def second_kernel(count, own_xor, chunks, *refs):
    refs = list(refs)
    received = refs[: count - 1]
    kept = refs[count - 1 : count - 1 + chunks]
    prefixes = refs[count - 1 + chunks : count - 1 + 2 * chunks]
    weight_ref = refs[count - 1 + 2 * chunks]
    hidden_ref, prefix_ref, totals_ref = refs[count + 2 * chunks :]
    group = 0
    for kept_ref, before_ref in zip(kept, prefixes):
        groups, _, steps, _ = kept_ref.shape
        for local in range(groups):
            cell, hidden = arriving(count, own_xor, received, group, True)
            a, c, d, u, v = (before_ref[local, j] for j in range(5))
            cell, hidden = a * cell + u, c * cell + d * hidden + v
            channels = pl.ds(group * LANES, LANES)
            forget_weight = jnp.broadcast_to(weight_ref[0:1, channels], (SUB, LANES))
            out_weight = jnp.broadcast_to(weight_ref[1:2, channels], (SUB, LANES))
            run = None
            for i in range(steps // SUB):
                rows = pl.ds(i * SUB, SUB)
                pre_forget = kept_ref[local, 0, rows, :]
                pre_output = kept_ref[local, 1, rows, :]
                fresh = kept_ref[local, 2, rows, :]
                forget = sigmoid(pre_forget + forget_weight * hidden)
                output = sigmoid(pre_output + out_weight * hidden)
                kept_cell = forget * cell
                new_cell = kept_cell + fresh
                squashed = jnp.tanh(new_cell)
                slope = output * (1.0 - squashed * squashed)
                cell_hidden = kept_cell * (1.0 - forget) * forget_weight
                hidden_cell = slope * forget
                hidden_hidden = (
                    output * (1.0 - output) * out_weight * squashed + slope * cell_hidden
                )
                offset_cell = new_cell - kept_cell - cell_hidden * hidden
                offset_hidden = output * squashed - hidden_cell * cell - hidden_hidden * hidden
                term = (
                    forget,
                    cell_hidden,
                    hidden_cell,
                    hidden_hidden,
                    offset_cell,
                    offset_hidden,
                )
                run = term if run is None else compose(run, term)
                hidden_ref[group, 0, rows, :] = run[2]
                hidden_ref[group, 1, rows, :] = run[3]
                hidden_ref[group, 2, rows, :] = run[5]
                forget = sigmoid(pre_forget)
                output = sigmoid(pre_output)
                squashed = jnp.tanh(fresh)
                hidden_cell = output * (1.0 - squashed * squashed) * forget
                hidden_hidden = output * (1.0 - output) * out_weight * squashed
                cell, hidden = (
                    forget * cell + fresh,
                    hidden_cell * cell + hidden_hidden * hidden + output * squashed,
                )
            before, total = sub_blocks(run, compose, UNIT)
            for index, term in enumerate(before):
                prefix_ref[group, index] = term
            for index, term in enumerate(total):
                totals_ref[pl.ds(group * SUB + index, 1), :] = term[SUB - 1 : SUB, :]
            for index in range(len(total), SUB):
                totals_ref[pl.ds(group * SUB + index, 1), :] = jnp.zeros((1, LANES), F32)
            group += 1


def second(own_xor, received, kept, prefixes, weight):
    count = len(received) + 1
    steps = kept[0].shape[2]
    groups = sum(k.shape[0] for k in kept)
    return pl.pallas_call(
        functools.partial(second_kernel, count, own_xor, len(kept)),
        out_shape=(
            pltpu.VMEM((groups, 3, steps, LANES), F32),
            pltpu.VMEM((groups, 6, SUB, LANES), F32),
            pltpu.VMEM((groups * SUB, LANES), F32),
        ),
        in_specs=vmem(count - 1 + 2 * len(kept) + 1),
        out_specs=vmem(3),
        compiler_params=PARAMS,
        cost_estimate=cost(100 * groups * steps * LANES, 24 * groups * steps * LANES),
        name="second",
    )(*received, *kept, *prefixes, weight)


def last_kernel(count, own_xor, *refs):
    received = refs[: count - 1]
    hidden_ref, prefix_ref, out_ref, turn_ref, made_ref, sems = refs[count - 1 :]
    groups, _, steps, _ = hidden_ref.shape
    runs = steps // SUB
    copies = []
    for group in range(groups):
        cell, hidden = arriving(count, own_xor, received, group, False)
        a, b, c, d, u, v = (prefix_ref[group, j] for j in range(6))
        cell, hidden = a * cell + b * hidden + u, c * cell + d * hidden + v
        for i in range(runs):
            rows = pl.ds(i * SUB, SUB)
            turn_ref[pl.ds(i, SUB, stride=runs), :] = (
                hidden_ref[group, 0, rows, :] * cell
                + hidden_ref[group, 1, rows, :] * hidden
                + hidden_ref[group, 2, rows, :]
            )
        rows = pl.ds(group * LANES, LANES)
        made_ref[rows, :] = turn_ref[...].T
        copies.append(pltpu.make_async_copy(made_ref.at[rows], out_ref.at[rows], sems.at[group]))
        copies[-1].start()
    for copy in copies:
        copy.wait()


def last(own_xor, received, hiddens, prefix):
    count = len(received) + 1
    groups, _, steps, _ = hiddens.shape
    return pl.pallas_call(
        functools.partial(last_kernel, count, own_xor),
        out_shape=jax.ShapeDtypeStruct((groups * LANES, steps), F32),
        in_specs=vmem(count + 1),
        compiler_params=PARAMS,
        out_specs=pl.BlockSpec(memory_space=pltpu.HBM),
        scratch_shapes=[
            pltpu.VMEM((steps, LANES), F32),
            pltpu.VMEM((groups * LANES, steps), F32),
            pltpu.SemaphoreType.DMA((groups,)),
        ],
        cost_estimate=cost(10 * groups * steps * LANES, 16 * groups * steps * LANES),
        name="last",
    )(*received, hiddens, prefix)


def pieces_of(groups, chips):
    half = max(1, groups // 2)
    pieces = [(1, 0, half), (1, half, groups - half)]
    pieces += [(away, 0, groups) for away in range(2, chips)]
    return [piece for piece in pieces if piece[2]]


def shards(tokens, in_weight, recur_weight, gate_bias, forget_offset):
    steps = tokens.shape[0]
    channels = recur_weight.shape[0]
    groups = channels // LANES
    per_owner = channels * GATES
    owners = lax.axis_size("chan")
    chips = owners // 2
    blocks = lax.axis_size("tm")
    own_xor = blocks & (blocks - 1) == 0

    bias = on_chip(gate_bias.T)
    weight = on_chip(recur_weight.T)
    offset = on_chip(forget_offset.reshape(1, steps))

    def to_core(value):
        return on_chip(lax.ppermute(value, "chan", [(i, i ^ 1) for i in range(owners)]))

    def to_chip(value, away):
        pairs = [(i, (i + 2 * away) % owners) for i in range(owners)]
        return on_chip(lax.ppermute(value, "chan", pairs))

    def to_blocks(value):
        arriving = []
        for k in range(1, blocks):
            pairs = [(i, i ^ k if own_xor else i + k) for i in range(blocks)]
            sent = lax.ppermute(value, "tm", [pair for pair in pairs if pair[1] < blocks])
            arriving.append(on_chip(sent))
        return arriving

    tokens, in_weight = off_chip(tokens), off_chip(in_weight)

    def product(parts, after):
        return products(tokens, in_weight, chips, per_owner, parts, after)

    coded = [[] for _ in range(groups)]

    def send(away, start, count, mine, theirs, inside):
        code = encoded(mine, theirs, inside, count * GROUP)
        arrived = to_chip(code, away)
        for place in range(count):
            coded[start + place].append((arrived, place))
        return code

    local_give, local_keep = ((0, which, 0, per_owner) for which in (GIVE, KEEP))
    given = None
    codes = []
    for index, (away, start, count) in enumerate(pieces_of(groups, chips)):
        last_piece = index == len(pieces_of(groups, chips)) - 1
        parts = tuple((away, which, start * GROUP, count * GROUP) for which in (GIVE, KEEP))
        if index == 0:
            (give,) = product(parts[:1], [])
            theirs = to_core(give)
            keep, *more = product(parts[1:] + (local_give,) * last_piece, [])
        else:
            give, keep, *more = product(parts + (local_give,) * last_piece, codes[-1:])
            theirs = to_core(give)
        if last_piece:
            given = to_core(more[0])
        if index == 0:
            codes.append(send(away, start, count, keep, theirs, 0))
        else:
            for group in range(start, start + count):
                codes.append(send(away, group, 1, keep, theirs, (group - start) * GROUP))
    (keep,) = product((local_keep,), codes[-1:])
    kept, prefixes, totals = [], [], []
    for group in range(groups):
        arrived, places = zip(*coded[group]) if coded[group] else ((), ())
        k, p, total = first(
            group, places, keep, given, list(arrived), bias, weight, offset, totals
        )
        totals = [total]
        kept.append(k)
        prefixes.append(p)
    hiddens, prefix, total = second(own_xor, to_blocks(totals[0]), kept, prefixes, weight)
    return last(own_xor, to_blocks(total), hiddens, prefix)


def solution(mesh):
    placed = (
        P(("groups", "tm"), "chan"),
        P("chan", None),
        P("chan", None),
        P("chan", None),
        P(("groups", "tm")),
    )

    return jax.shard_map(
        shards, mesh=mesh, in_specs=placed, out_specs=P("chan", ("groups", "tm")), check_vma=False
    )
```

```python
import functools

import jax
import jax.numpy as jnp
from jax import lax
from jax.experimental import pallas as pl
from jax.experimental.pallas import tpu as pltpu
from jax.sharding import PartitionSpec as P


LANES = 128
SUB = 8
GATES = 4
GROUP = LANES * GATES
BINADES = 251.0
LOWEST = 125.0
GIVE, KEEP = 0, 1
F32 = jnp.float32
BF16 = jnp.bfloat16


def cost(flops, moved):
    return pl.CostEstimate(flops=int(flops), bytes_accessed=int(moved), transcendentals=0)


def vmem(count):
    return [pl.BlockSpec(memory_space=pltpu.VMEM)] * count


def in_hbm(count):
    return [pl.BlockSpec(memory_space=pltpu.HBM)] * count


def off_chip(value):
    return pltpu.with_memory_space_constraint(value, pltpu.HBM)


def on_chip(value):
    return pltpu.with_memory_space_constraint(value, pltpu.VMEM)


PARAMS = pltpu.CompilerParams(vmem_limit_bytes=16 << 20)


def product_kernel(chips, parts, per_owner, tokens_ref, weight_ref, *refs):
    outs, (x_ref, w_ref, sems) = refs[-3 - len(parts) : -3], refs[-3:]
    me = lax.axis_index("chan")
    chip, core = me // 2, me % 2
    tokens_copy = pltpu.make_async_copy(tokens_ref, x_ref, sems.at[w_ref.shape[0]])
    tokens_copy.start()
    copies = []
    for (away, which, first, width), out_ref in zip(parts, outs):
        owner = 2 * lax.rem(chip + away, chips) + (core if which == KEEP else 1 - core)
        for start in range(0, width, GROUP):
            slot = len(copies)
            column = pl.multiple_of(owner * per_owner + first + start, GROUP)
            copy = pltpu.make_async_copy(
                weight_ref.at[:, pl.ds(column, GROUP)], w_ref.at[slot], sems.at[slot]
            )
            copy.start()
            copies.append((copy, out_ref, start))
    tokens_copy.wait()
    for slot, (copy, out_ref, start) in enumerate(copies):
        copy.wait()
        out_ref[:, pl.ds(start, GROUP)] = jnp.dot(
            x_ref[...], w_ref[slot], preferred_element_type=F32
        )


def products(tokens, in_weight, chips, per_owner, parts, after):
    steps, depth = tokens.shape
    slots = sum(width for _, _, _, width in parts) // GROUP
    return pl.pallas_call(
        functools.partial(product_kernel, chips, parts, per_owner),
        out_shape=[pltpu.VMEM((steps, width), F32) for _, _, _, width in parts],
        in_specs=in_hbm(2) + vmem(len(after)),
        out_specs=vmem(len(parts)),
        scratch_shapes=[
            pltpu.VMEM((steps, depth), BF16),
            pltpu.VMEM((slots, depth, GROUP), BF16),
            pltpu.SemaphoreType.DMA((slots + 1,)),
        ],
        compiler_params=PARAMS,
        cost_estimate=cost(2 * slots * steps * depth * GROUP, 2 * slots * depth * GROUP),
        name="products",
    )(tokens, in_weight, *after)


def encode_kernel(first, mine_ref, theirs_ref, out_ref, sum_ref):
    steps, width = sum_ref.shape
    blocks = width // LANES
    top = jnp.zeros((steps, LANES), F32)
    for block in range(blocks):
        cols = pl.ds(first + block * LANES, LANES)
        both = mine_ref[:, cols] + theirs_ref[:, cols]
        sum_ref[:, pl.ds(block * LANES, LANES)] = both
        top = jnp.maximum(top, jnp.abs(both))
    top = jnp.max(top, axis=0, keepdims=True)
    top = jnp.maximum(top, 1e-30) * 1.0078125
    scale = top.astype(BF16).astype(F32)
    out_ref[pl.ds(blocks * steps, SUB), :] = jnp.broadcast_to(scale, (SUB, LANES)).astype(BF16)
    inverse = 1.0 / scale
    for block in range(blocks):
        value = sum_ref[:, pl.ds(block * LANES, LANES)]
        level = jnp.sqrt(jnp.abs(value) * inverse) * BINADES - LOWEST
        code = jnp.exp2(level)
        out_ref[pl.ds(block * steps, steps), :] = jnp.where(value < 0.0, -code, code).astype(BF16)


def encoded(mine, theirs, first, width):
    steps = mine.shape[0]
    rows = steps * (width // LANES) + SUB
    return pl.pallas_call(
        functools.partial(encode_kernel, first),
        out_shape=pltpu.VMEM((rows, LANES), BF16),
        in_specs=vmem(2),
        out_specs=pl.BlockSpec(memory_space=pltpu.VMEM),
        scratch_shapes=[pltpu.VMEM((steps, width), F32)],
        compiler_params=PARAMS,
        cost_estimate=cost(20 * steps * width, 10 * steps * width),
        name="encode",
    )(mine, theirs)


def decoded(code, scale):
    level = (jnp.log2(jnp.abs(code)) + LOWEST) * (1.0 / BINADES)
    size = level * level * scale
    return jnp.where(code < 0.0, -size, size)


def compose(early, later):
    e1, e2, e3, e4, e5, e6 = early
    l1, l2, l3, l4, l5, l6 = later
    return (
        l1 * e1 + l2 * e3,
        l1 * e2 + l2 * e4,
        l3 * e1 + l4 * e3,
        l3 * e2 + l4 * e4,
        l1 * e5 + l2 * e6 + l5,
        l3 * e5 + l4 * e6 + l6,
    )


def compose_lower(early, later):
    e1, e3, e4, e5, e6 = early
    l1, l3, l4, l5, l6 = later
    return (
        l1 * e1,
        l3 * e1 + l4 * e3,
        l4 * e4,
        l1 * e5 + l5,
        l3 * e5 + l4 * e6 + l6,
    )


def sub_blocks(terms, join, identity):
    row = lax.broadcasted_iota(jnp.int32, (SUB, LANES), 0)
    reach = 1
    while reach < SUB:
        moved = tuple(
            jnp.where(row >= reach, pltpu.roll(term, reach, 0), unit)
            for term, unit in zip(terms, identity)
        )
        terms = join(moved, terms)
        reach *= 2
    before = tuple(
        jnp.where(row >= 1, pltpu.roll(term, 1, 0), unit) for term, unit in zip(terms, identity)
    )
    return before, terms


LOWER_UNIT = (1.0, 0.0, 1.0, 0.0, 0.0)
UNIT = (1.0, 0.0, 0.0, 1.0, 0.0, 0.0)


def sigmoid(x):
    return 1.0 / (1.0 + jnp.exp(-x))


def first_kernel(start, places, earlier, *refs):
    groups, remotes = 1, len(places)
    refs = list(refs)
    mine_ref, theirs_ref = refs[:2]
    codes = refs[2 : 2 + remotes]
    bias_ref, weight_ref, offset_ref = refs[2 + remotes : 5 + remotes]
    totals_before = refs[5 + remotes : 5 + remotes + earlier]
    kept_ref, prefix_ref, totals_ref, sum_ref, late_ref = refs[5 + remotes + earlier :]
    steps = mine_ref.shape[0]
    runs = steps // SUB
    done = 0
    for ref in totals_before:
        totals_ref[pl.ds(done, ref.shape[0]), :] = ref[...]
        done += ref.shape[0]
    scales = [
        ref[pl.ds(ref.shape[0] - SUB, SUB), :][0:1, :].astype(F32) for ref in codes
    ]
    late_ref[...] = jnp.broadcast_to(offset_ref[...], (LANES, steps)).T
    lane = lax.broadcasted_iota(jnp.int32, (SUB, LANES), 1)
    quarter = lane // (LANES // GATES)
    inner = lane % (LANES // GATES)
    picks = [inner * GATES + (quarter - q + GATES) % GATES for q in range(GATES)]
    for group in range(groups):
        for q in range(GATES):
            block = group * GATES + q
            cols = pl.ds(start * GROUP + block * LANES, LANES)
            value = mine_ref[:, cols] + theirs_ref[:, cols]
            for ref, scale, place in zip(codes, scales, places):
                rows = pl.ds((place * GATES + block) * steps, steps)
                value = value + decoded(ref[rows, :].astype(F32), scale)
            sum_ref[q] = value
        channels = pl.ds((start + group) * LANES, LANES)
        biases = [
            jnp.broadcast_to(bias_ref[k : k + 1, channels], (SUB, LANES)) for k in range(GATES)
        ]
        out_weight = jnp.broadcast_to(weight_ref[1:2, channels], (SUB, LANES))
        run = None
        for i in range(runs):
            loaded = [
                jnp.take_along_axis(sum_ref[q, pl.ds(i, SUB, stride=runs), :], picks[q], axis=1)
                for q in range(GATES)
            ]
            pre = []
            for k in range(GATES):
                part = loaded[(0 - k) % GATES]
                for p in range(1, GATES):
                    part = jnp.where(quarter == p, loaded[(p - k) % GATES], part)
                if k:
                    part = pltpu.roll(part, LANES - k * (LANES // GATES), 1)
                pre.append(part + biases[k])
            pre_forget = pre[1] - late_ref[pl.ds(i, SUB, stride=runs), :]
            forget = sigmoid(pre_forget)
            output = sigmoid(pre[3])
            cell = sigmoid(pre[0]) * jnp.tanh(pre[2])
            squashed = jnp.tanh(cell)
            hidden_cell = output * (1.0 - squashed * squashed) * forget
            hidden_hidden = output * (1.0 - output) * out_weight * squashed
            term = (forget, hidden_cell, hidden_hidden, cell, output * squashed)
            run = term if run is None else compose_lower(run, term)
            rows = pl.ds(i * SUB, SUB)
            kept_ref[group, 0, rows, :] = pre_forget
            kept_ref[group, 1, rows, :] = pre[3]
            kept_ref[group, 2, rows, :] = cell
        before, total = sub_blocks(run, compose_lower, LOWER_UNIT)
        for index, term in enumerate(before):
            prefix_ref[group, index] = term
        for index, term in enumerate(total):
            totals_ref[pl.ds(done + group * SUB + index, 1), :] = term[SUB - 1 : SUB, :]
        for index in range(len(total), SUB):
            totals_ref[pl.ds(done + group * SUB + index, 1), :] = jnp.zeros((1, LANES), F32)


def first(start, places, mine, theirs, codes, bias, weight, offset, earlier):
    steps = mine.shape[0]
    groups = 1
    rows = sum(e.shape[0] for e in earlier) + groups * SUB
    count = 5 + len(codes) + len(earlier)
    return pl.pallas_call(
        functools.partial(first_kernel, start, places, len(earlier)),
        out_shape=(
            pltpu.VMEM((groups, 3, steps, LANES), F32),
            pltpu.VMEM((groups, 5, SUB, LANES), F32),
            pltpu.VMEM((rows, LANES), F32),
        ),
        in_specs=vmem(count),
        out_specs=vmem(3),
        scratch_shapes=[
            pltpu.VMEM((GATES, steps, LANES), F32),
            pltpu.VMEM((steps, LANES), F32),
        ],
        compiler_params=PARAMS,
        cost_estimate=cost(60 * steps * groups * GROUP, 20 * steps * groups * GROUP),
        name="first",
    )(mine, theirs, *codes, bias, weight, offset, *earlier)


def in_turn(me, count, own_xor, received):
    for position in range(count - 1):
        picked = received[0]
        for k in range(2, count):
            picked = jnp.where(position == (me ^ k if own_xor else me - k), received[k - 1], picked)
        yield picked, position < me


def arriving(count, own_xor, received, group, lower):
    me = lax.axis_index("tm")
    rows = [ref[pl.ds(group * SUB, SUB), :] for ref in received]
    cell = jnp.zeros((1, LANES), F32)
    hidden = jnp.zeros((1, LANES), F32)
    for maps, counts in in_turn(me, count, own_xor, rows):
        if lower:
            a, c, d, u, v = (maps[j : j + 1, :] for j in range(5))
            new_cell = a * cell + u
        else:
            a, b, c, d, u, v = (maps[j : j + 1, :] for j in range(6))
            new_cell = a * cell + b * hidden + u
        new_hidden = c * cell + d * hidden + v
        cell = jnp.where(counts, new_cell, cell)
        hidden = jnp.where(counts, new_hidden, hidden)
    return cell, hidden


def second_kernel(count, own_xor, chunks, *refs):
    refs = list(refs)
    received = refs[: count - 1]
    kept = refs[count - 1 : count - 1 + chunks]
    prefixes = refs[count - 1 + chunks : count - 1 + 2 * chunks]
    weight_ref = refs[count - 1 + 2 * chunks]
    hidden_ref, prefix_ref, totals_ref = refs[count + 2 * chunks :]
    group = 0
    for kept_ref, before_ref in zip(kept, prefixes):
        groups, _, steps, _ = kept_ref.shape
        for local in range(groups):
            cell, hidden = arriving(count, own_xor, received, group, True)
            a, c, d, u, v = (before_ref[local, j] for j in range(5))
            cell, hidden = a * cell + u, c * cell + d * hidden + v
            channels = pl.ds(group * LANES, LANES)
            forget_weight = jnp.broadcast_to(weight_ref[0:1, channels], (SUB, LANES))
            out_weight = jnp.broadcast_to(weight_ref[1:2, channels], (SUB, LANES))
            run = None
            for i in range(steps // SUB):
                rows = pl.ds(i * SUB, SUB)
                pre_forget = kept_ref[local, 0, rows, :]
                pre_output = kept_ref[local, 1, rows, :]
                fresh = kept_ref[local, 2, rows, :]
                forget = sigmoid(pre_forget + forget_weight * hidden)
                output = sigmoid(pre_output + out_weight * hidden)
                kept_cell = forget * cell
                new_cell = kept_cell + fresh
                squashed = jnp.tanh(new_cell)
                slope = output * (1.0 - squashed * squashed)
                cell_hidden = kept_cell * (1.0 - forget) * forget_weight
                hidden_cell = slope * forget
                hidden_hidden = (
                    output * (1.0 - output) * out_weight * squashed + slope * cell_hidden
                )
                offset_cell = new_cell - kept_cell - cell_hidden * hidden
                offset_hidden = output * squashed - hidden_cell * cell - hidden_hidden * hidden
                term = (
                    forget,
                    cell_hidden,
                    hidden_cell,
                    hidden_hidden,
                    offset_cell,
                    offset_hidden,
                )
                run = term if run is None else compose(run, term)
                hidden_ref[group, 0, rows, :] = run[2]
                hidden_ref[group, 1, rows, :] = run[3]
                hidden_ref[group, 2, rows, :] = run[5]
                forget = sigmoid(pre_forget)
                output = sigmoid(pre_output)
                squashed = jnp.tanh(fresh)
                hidden_cell = output * (1.0 - squashed * squashed) * forget
                hidden_hidden = output * (1.0 - output) * out_weight * squashed
                cell, hidden = (
                    forget * cell + fresh,
                    hidden_cell * cell + hidden_hidden * hidden + output * squashed,
                )
            before, total = sub_blocks(run, compose, UNIT)
            for index, term in enumerate(before):
                prefix_ref[group, index] = term
            for index, term in enumerate(total):
                totals_ref[pl.ds(group * SUB + index, 1), :] = term[SUB - 1 : SUB, :]
            for index in range(len(total), SUB):
                totals_ref[pl.ds(group * SUB + index, 1), :] = jnp.zeros((1, LANES), F32)
            group += 1


def second(own_xor, received, kept, prefixes, weight):
    count = len(received) + 1
    steps = kept[0].shape[2]
    groups = sum(k.shape[0] for k in kept)
    return pl.pallas_call(
        functools.partial(second_kernel, count, own_xor, len(kept)),
        out_shape=(
            pltpu.VMEM((groups, 3, steps, LANES), F32),
            pltpu.VMEM((groups, 6, SUB, LANES), F32),
            pltpu.VMEM((groups * SUB, LANES), F32),
        ),
        in_specs=vmem(count - 1 + 2 * len(kept) + 1),
        out_specs=vmem(3),
        compiler_params=PARAMS,
        cost_estimate=cost(100 * groups * steps * LANES, 24 * groups * steps * LANES),
        name="second",
    )(*received, *kept, *prefixes, weight)


def last_kernel(count, own_xor, *refs):
    received = refs[: count - 1]
    hidden_ref, prefix_ref, out_ref, turn_ref, made_ref, sems = refs[count - 1 :]
    groups, _, steps, _ = hidden_ref.shape
    runs = steps // SUB
    copies = []
    for group in range(groups):
        cell, hidden = arriving(count, own_xor, received, group, False)
        a, b, c, d, u, v = (prefix_ref[group, j] for j in range(6))
        cell, hidden = a * cell + b * hidden + u, c * cell + d * hidden + v
        for i in range(runs):
            rows = pl.ds(i * SUB, SUB)
            turn_ref[pl.ds(i, SUB, stride=runs), :] = (
                hidden_ref[group, 0, rows, :] * cell
                + hidden_ref[group, 1, rows, :] * hidden
                + hidden_ref[group, 2, rows, :]
            )
        rows = pl.ds(group * LANES, LANES)
        made_ref[rows, :] = turn_ref[...].T
        copies.append(pltpu.make_async_copy(made_ref.at[rows], out_ref.at[rows], sems.at[group]))
        copies[-1].start()
    for copy in copies:
        copy.wait()


def last(own_xor, received, hiddens, prefix):
    count = len(received) + 1
    groups, _, steps, _ = hiddens.shape
    return pl.pallas_call(
        functools.partial(last_kernel, count, own_xor),
        out_shape=jax.ShapeDtypeStruct((groups * LANES, steps), F32),
        in_specs=vmem(count + 1),
        compiler_params=PARAMS,
        out_specs=pl.BlockSpec(memory_space=pltpu.HBM),
        scratch_shapes=[
            pltpu.VMEM((steps, LANES), F32),
            pltpu.VMEM((groups * LANES, steps), F32),
            pltpu.SemaphoreType.DMA((groups,)),
        ],
        cost_estimate=cost(10 * groups * steps * LANES, 16 * groups * steps * LANES),
        name="last",
    )(*received, hiddens, prefix)


def pieces_of(groups, chips):
    half = max(1, groups // 2)
    pieces = [(1, 0, half)] + [(1, group, 1) for group in range(half, groups)]
    return pieces + [(away, 0, groups) for away in range(2, chips)]


def shards(tokens, in_weight, recur_weight, gate_bias, forget_offset):
    steps = tokens.shape[0]
    channels = recur_weight.shape[0]
    groups = channels // LANES
    per_owner = channels * GATES
    owners = lax.axis_size("chan")
    chips = owners // 2
    blocks = lax.axis_size("tm")
    own_xor = blocks & (blocks - 1) == 0

    bias = on_chip(gate_bias.T)
    weight = on_chip(recur_weight.T)
    offset = on_chip(forget_offset.reshape(1, steps))

    def to_core(value):
        return on_chip(lax.ppermute(value, "chan", [(i, i ^ 1) for i in range(owners)]))

    def to_chip(value, away):
        pairs = [(i, (i + 2 * away) % owners) for i in range(owners)]
        return on_chip(lax.ppermute(value, "chan", pairs))

    def to_blocks(value):
        arriving = []
        for k in range(1, blocks):
            pairs = [(i, i ^ k if own_xor else i + k) for i in range(blocks)]
            sent = lax.ppermute(value, "tm", [pair for pair in pairs if pair[1] < blocks])
            arriving.append(on_chip(sent))
        return arriving

    tokens, in_weight = off_chip(tokens), off_chip(in_weight)

    def product(parts, after):
        return products(tokens, in_weight, chips, per_owner, parts, after)

    coded = [[] for _ in range(groups)]

    def send(away, start, count, mine, theirs, inside):
        code = encoded(mine, theirs, inside, count * GROUP)
        arrived = to_chip(code, away)
        for place in range(count):
            coded[start + place].append((arrived, place))
        return code

    local_give, local_keep = ((0, which, 0, per_owner) for which in (GIVE, KEEP))
    given = None
    codes = []
    for index, (away, start, count) in enumerate(pieces_of(groups, chips)):
        last_piece = index == len(pieces_of(groups, chips)) - 1
        parts = tuple((away, which, start * GROUP, count * GROUP) for which in (GIVE, KEEP))
        if index == 0:
            (give,) = product(parts[:1], [])
            theirs = to_core(give)
            keep, *more = product(parts[1:] + (local_give,) * last_piece, [])
        else:
            give, keep, *more = product(parts + (local_give,) * last_piece, codes[-2:][:1])
            theirs = to_core(give)
        if last_piece:
            given = to_core(more[0])
        if index == 0:
            codes.append(send(away, start, count, keep, theirs, 0))
        else:
            for group in range(start, start + count):
                codes.append(send(away, group, 1, keep, theirs, (group - start) * GROUP))
    (keep,) = product((local_keep,), codes[-1:])
    kept, prefixes, totals = [], [], []
    for group in range(groups):
        arrived, places = zip(*coded[group]) if coded[group] else ((), ())
        k, p, total = first(
            group, places, keep, given, list(arrived), bias, weight, offset, totals
        )
        totals = [total]
        kept.append(k)
        prefixes.append(p)
    hiddens, prefix, total = second(own_xor, to_blocks(totals[0]), kept, prefixes, weight)
    return last(own_xor, to_blocks(total), hiddens, prefix)


def solution(mesh):
    placed = (
        P(("groups", "tm"), "chan"),
        P("chan", None),
        P("chan", None),
        P("chan", None),
        P(("groups", "tm")),
    )

    return jax.shard_map(
        shards, mesh=mesh, in_specs=placed, out_specs=P("chan", ("groups", "tm")), check_vma=False
    )
```

```python
import functools

import jax
import jax.numpy as jnp
from jax import lax
from jax.experimental import pallas as pl
from jax.experimental.pallas import tpu as pltpu
from jax.sharding import PartitionSpec as P


LANES = 128
SUB = 8
GATES = 4
GROUP = LANES * GATES
BINADES = 251.0
LOWEST = 125.0
GIVE, KEEP = 0, 1
F32 = jnp.float32
BF16 = jnp.bfloat16


def cost(flops, moved):
    return pl.CostEstimate(flops=int(flops), bytes_accessed=int(moved), transcendentals=0)


def vmem(count):
    return [pl.BlockSpec(memory_space=pltpu.VMEM)] * count


def in_hbm(count):
    return [pl.BlockSpec(memory_space=pltpu.HBM)] * count


def off_chip(value):
    return pltpu.with_memory_space_constraint(value, pltpu.HBM)


def on_chip(value):
    return pltpu.with_memory_space_constraint(value, pltpu.VMEM)


PARAMS = pltpu.CompilerParams(vmem_limit_bytes=16 << 20)


def product_kernel(chips, parts, per_owner, tokens_ref, weight_ref, *refs):
    outs, (x_ref, w_ref, sems) = refs[-3 - len(parts) : -3], refs[-3:]
    me = lax.axis_index("chan")
    chip, core = me // 2, me % 2
    tokens_copy = pltpu.make_async_copy(tokens_ref, x_ref, sems.at[w_ref.shape[0]])
    tokens_copy.start()
    copies = []
    for (away, which, first, width), out_ref in zip(parts, outs):
        owner = 2 * lax.rem(chip + away, chips) + (core if which == KEEP else 1 - core)
        for start in range(0, width, GROUP):
            slot = len(copies)
            column = pl.multiple_of(owner * per_owner + first + start, GROUP)
            copy = pltpu.make_async_copy(
                weight_ref.at[:, pl.ds(column, GROUP)], w_ref.at[slot], sems.at[slot]
            )
            copy.start()
            copies.append((copy, out_ref, start))
    tokens_copy.wait()
    for slot, (copy, out_ref, start) in enumerate(copies):
        copy.wait()
        out_ref[:, pl.ds(start, GROUP)] = jnp.dot(
            x_ref[...], w_ref[slot], preferred_element_type=F32
        )


def products(tokens, in_weight, chips, per_owner, parts, after):
    steps, depth = tokens.shape
    slots = sum(width for _, _, _, width in parts) // GROUP
    return pl.pallas_call(
        functools.partial(product_kernel, chips, parts, per_owner),
        out_shape=[pltpu.VMEM((steps, width), F32) for _, _, _, width in parts],
        in_specs=in_hbm(2) + vmem(len(after)),
        out_specs=vmem(len(parts)),
        scratch_shapes=[
            pltpu.VMEM((steps, depth), BF16),
            pltpu.VMEM((slots, depth, GROUP), BF16),
            pltpu.SemaphoreType.DMA((slots + 1,)),
        ],
        compiler_params=PARAMS,
        cost_estimate=cost(2 * slots * steps * depth * GROUP, 2 * slots * depth * GROUP),
        name="products",
    )(tokens, in_weight, *after)


def encode_kernel(first, mine_ref, theirs_ref, out_ref, sum_ref):
    steps, width = sum_ref.shape
    blocks = width // LANES
    top = jnp.zeros((steps, LANES), F32)
    for block in range(blocks):
        cols = pl.ds(first + block * LANES, LANES)
        both = mine_ref[:, cols] + theirs_ref[:, cols]
        sum_ref[:, pl.ds(block * LANES, LANES)] = both
        top = jnp.maximum(top, jnp.abs(both))
    top = jnp.max(top, axis=0, keepdims=True)
    top = jnp.maximum(top, 1e-30) * 1.0078125
    scale = top.astype(BF16).astype(F32)
    out_ref[pl.ds(blocks * steps, SUB), :] = jnp.broadcast_to(scale, (SUB, LANES)).astype(BF16)
    inverse = 1.0 / scale
    for block in range(blocks):
        value = sum_ref[:, pl.ds(block * LANES, LANES)]
        level = jnp.sqrt(jnp.abs(value) * inverse) * BINADES - LOWEST
        code = jnp.exp2(level)
        out_ref[pl.ds(block * steps, steps), :] = jnp.where(value < 0.0, -code, code).astype(BF16)


def encoded(mine, theirs, first, width):
    steps = mine.shape[0]
    rows = steps * (width // LANES) + SUB
    return pl.pallas_call(
        functools.partial(encode_kernel, first),
        out_shape=pltpu.VMEM((rows, LANES), BF16),
        in_specs=vmem(2),
        out_specs=pl.BlockSpec(memory_space=pltpu.VMEM),
        scratch_shapes=[pltpu.VMEM((steps, width), F32)],
        compiler_params=PARAMS,
        cost_estimate=cost(20 * steps * width, 10 * steps * width),
        name="encode",
    )(mine, theirs)


def decoded(code, scale):
    level = (jnp.log2(jnp.abs(code)) + LOWEST) * (1.0 / BINADES)
    size = level * level * scale
    return jnp.where(code < 0.0, -size, size)


def compose(early, later):
    e1, e2, e3, e4, e5, e6 = early
    l1, l2, l3, l4, l5, l6 = later
    return (
        l1 * e1 + l2 * e3,
        l1 * e2 + l2 * e4,
        l3 * e1 + l4 * e3,
        l3 * e2 + l4 * e4,
        l1 * e5 + l2 * e6 + l5,
        l3 * e5 + l4 * e6 + l6,
    )


def compose_lower(early, later):
    e1, e3, e4, e5, e6 = early
    l1, l3, l4, l5, l6 = later
    return (
        l1 * e1,
        l3 * e1 + l4 * e3,
        l4 * e4,
        l1 * e5 + l5,
        l3 * e5 + l4 * e6 + l6,
    )


def sub_blocks(terms, join, identity):
    row = lax.broadcasted_iota(jnp.int32, (SUB, LANES), 0)
    reach = 1
    while reach < SUB:
        moved = tuple(
            jnp.where(row >= reach, pltpu.roll(term, reach, 0), unit)
            for term, unit in zip(terms, identity)
        )
        terms = join(moved, terms)
        reach *= 2
    before = tuple(
        jnp.where(row >= 1, pltpu.roll(term, 1, 0), unit) for term, unit in zip(terms, identity)
    )
    return before, terms


LOWER_UNIT = (1.0, 0.0, 1.0, 0.0, 0.0)
UNIT = (1.0, 0.0, 0.0, 1.0, 0.0, 0.0)


def sigmoid(x):
    return 1.0 / (1.0 + jnp.exp(-x))


def first_kernel(start, places, earlier, *refs):
    groups, remotes = 1, len(places)
    refs = list(refs)
    mine_ref, theirs_ref = refs[:2]
    codes = refs[2 : 2 + remotes]
    bias_ref, weight_ref, offset_ref = refs[2 + remotes : 5 + remotes]
    totals_before = refs[5 + remotes : 5 + remotes + earlier]
    kept_ref, prefix_ref, totals_ref, sum_ref, late_ref = refs[5 + remotes + earlier :]
    steps = mine_ref.shape[0]
    runs = steps // SUB
    done = 0
    for ref in totals_before:
        totals_ref[pl.ds(done, ref.shape[0]), :] = ref[...]
        done += ref.shape[0]
    scales = [
        ref[pl.ds(ref.shape[0] - SUB, SUB), :][0:1, :].astype(F32) for ref in codes
    ]
    late_ref[...] = jnp.broadcast_to(offset_ref[...], (LANES, steps)).T
    lane = lax.broadcasted_iota(jnp.int32, (SUB, LANES), 1)
    quarter = lane // (LANES // GATES)
    inner = lane % (LANES // GATES)
    picks = [inner * GATES + (quarter - q + GATES) % GATES for q in range(GATES)]
    for group in range(groups):
        for q in range(GATES):
            block = group * GATES + q
            cols = pl.ds(start * GROUP + block * LANES, LANES)
            value = mine_ref[:, cols] + theirs_ref[:, cols]
            for ref, scale, place in zip(codes, scales, places):
                rows = pl.ds((place * GATES + block) * steps, steps)
                value = value + decoded(ref[rows, :].astype(F32), scale)
            sum_ref[q] = value
        channels = pl.ds((start + group) * LANES, LANES)
        biases = [
            jnp.broadcast_to(bias_ref[k : k + 1, channels], (SUB, LANES)) for k in range(GATES)
        ]
        out_weight = jnp.broadcast_to(weight_ref[1:2, channels], (SUB, LANES))
        run = None
        for i in range(runs):
            loaded = [
                jnp.take_along_axis(sum_ref[q, pl.ds(i, SUB, stride=runs), :], picks[q], axis=1)
                for q in range(GATES)
            ]
            pre = []
            for k in range(GATES):
                part = loaded[(0 - k) % GATES]
                for p in range(1, GATES):
                    part = jnp.where(quarter == p, loaded[(p - k) % GATES], part)
                if k:
                    part = pltpu.roll(part, LANES - k * (LANES // GATES), 1)
                pre.append(part + biases[k])
            pre_forget = pre[1] - late_ref[pl.ds(i, SUB, stride=runs), :]
            forget = sigmoid(pre_forget)
            output = sigmoid(pre[3])
            cell = sigmoid(pre[0]) * jnp.tanh(pre[2])
            squashed = jnp.tanh(cell)
            hidden_cell = output * (1.0 - squashed * squashed) * forget
            hidden_hidden = output * (1.0 - output) * out_weight * squashed
            term = (forget, hidden_cell, hidden_hidden, cell, output * squashed)
            run = term if run is None else compose_lower(run, term)
            rows = pl.ds(i * SUB, SUB)
            kept_ref[group, 0, rows, :] = pre_forget
            kept_ref[group, 1, rows, :] = pre[3]
            kept_ref[group, 2, rows, :] = cell
        before, total = sub_blocks(run, compose_lower, LOWER_UNIT)
        for index, term in enumerate(before):
            prefix_ref[group, index] = term
        for index, term in enumerate(total):
            totals_ref[pl.ds(done + group * SUB + index, 1), :] = term[SUB - 1 : SUB, :]
        for index in range(len(total), SUB):
            totals_ref[pl.ds(done + group * SUB + index, 1), :] = jnp.zeros((1, LANES), F32)


def first(start, places, mine, theirs, codes, bias, weight, offset, earlier):
    steps = mine.shape[0]
    groups = 1
    rows = sum(e.shape[0] for e in earlier) + groups * SUB
    count = 5 + len(codes) + len(earlier)
    return pl.pallas_call(
        functools.partial(first_kernel, start, places, len(earlier)),
        out_shape=(
            pltpu.VMEM((groups, 3, steps, LANES), F32),
            pltpu.VMEM((groups, 5, SUB, LANES), F32),
            pltpu.VMEM((rows, LANES), F32),
        ),
        in_specs=vmem(count),
        out_specs=vmem(3),
        scratch_shapes=[
            pltpu.VMEM((GATES, steps, LANES), F32),
            pltpu.VMEM((steps, LANES), F32),
        ],
        compiler_params=PARAMS,
        cost_estimate=cost(60 * steps * groups * GROUP, 20 * steps * groups * GROUP),
        name="first",
    )(mine, theirs, *codes, bias, weight, offset, *earlier)


def in_turn(me, count, own_xor, received):
    for position in range(count - 1):
        picked = received[0]
        for k in range(2, count):
            picked = jnp.where(position == (me ^ k if own_xor else me - k), received[k - 1], picked)
        yield picked, position < me


def arriving(count, own_xor, received, group, lower):
    me = lax.axis_index("tm")
    rows = [ref[pl.ds(group * SUB, SUB), :] for ref in received]
    cell = jnp.zeros((1, LANES), F32)
    hidden = jnp.zeros((1, LANES), F32)
    for maps, counts in in_turn(me, count, own_xor, rows):
        if lower:
            a, c, d, u, v = (maps[j : j + 1, :] for j in range(5))
            new_cell = a * cell + u
        else:
            a, b, c, d, u, v = (maps[j : j + 1, :] for j in range(6))
            new_cell = a * cell + b * hidden + u
        new_hidden = c * cell + d * hidden + v
        cell = jnp.where(counts, new_cell, cell)
        hidden = jnp.where(counts, new_hidden, hidden)
    return cell, hidden


def second_kernel(count, own_xor, chunks, *refs):
    refs = list(refs)
    received = refs[: count - 1]
    kept = refs[count - 1 : count - 1 + chunks]
    prefixes = refs[count - 1 + chunks : count - 1 + 2 * chunks]
    weight_ref = refs[count - 1 + 2 * chunks]
    hidden_ref, prefix_ref, totals_ref = refs[count + 2 * chunks :]
    group = 0
    for kept_ref, before_ref in zip(kept, prefixes):
        groups, _, steps, _ = kept_ref.shape
        for local in range(groups):
            cell, hidden = arriving(count, own_xor, received, group, True)
            a, c, d, u, v = (before_ref[local, j] for j in range(5))
            cell, hidden = a * cell + u, c * cell + d * hidden + v
            channels = pl.ds(group * LANES, LANES)
            forget_weight = jnp.broadcast_to(weight_ref[0:1, channels], (SUB, LANES))
            out_weight = jnp.broadcast_to(weight_ref[1:2, channels], (SUB, LANES))
            run = None
            for i in range(steps // SUB):
                rows = pl.ds(i * SUB, SUB)
                pre_forget = kept_ref[local, 0, rows, :]
                pre_output = kept_ref[local, 1, rows, :]
                fresh = kept_ref[local, 2, rows, :]
                forget = sigmoid(pre_forget + forget_weight * hidden)
                output = sigmoid(pre_output + out_weight * hidden)
                kept_cell = forget * cell
                new_cell = kept_cell + fresh
                squashed = jnp.tanh(new_cell)
                slope = output * (1.0 - squashed * squashed)
                cell_hidden = kept_cell * (1.0 - forget) * forget_weight
                hidden_cell = slope * forget
                hidden_hidden = (
                    output * (1.0 - output) * out_weight * squashed + slope * cell_hidden
                )
                offset_cell = new_cell - kept_cell - cell_hidden * hidden
                offset_hidden = output * squashed - hidden_cell * cell - hidden_hidden * hidden
                term = (
                    forget,
                    cell_hidden,
                    hidden_cell,
                    hidden_hidden,
                    offset_cell,
                    offset_hidden,
                )
                run = term if run is None else compose(run, term)
                hidden_ref[group, 0, rows, :] = run[2]
                hidden_ref[group, 1, rows, :] = run[3]
                hidden_ref[group, 2, rows, :] = run[5]
                forget = sigmoid(pre_forget)
                output = sigmoid(pre_output)
                squashed = jnp.tanh(fresh)
                hidden_cell = output * (1.0 - squashed * squashed) * forget
                hidden_hidden = output * (1.0 - output) * out_weight * squashed
                cell, hidden = (
                    forget * cell + fresh,
                    hidden_cell * cell + hidden_hidden * hidden + output * squashed,
                )
            before, total = sub_blocks(run, compose, UNIT)
            for index, term in enumerate(before):
                prefix_ref[group, index] = term
            for index, term in enumerate(total):
                totals_ref[pl.ds(group * SUB + index, 1), :] = term[SUB - 1 : SUB, :]
            for index in range(len(total), SUB):
                totals_ref[pl.ds(group * SUB + index, 1), :] = jnp.zeros((1, LANES), F32)
            group += 1


def second(own_xor, received, kept, prefixes, weight):
    count = len(received) + 1
    steps = kept[0].shape[2]
    groups = sum(k.shape[0] for k in kept)
    return pl.pallas_call(
        functools.partial(second_kernel, count, own_xor, len(kept)),
        out_shape=(
            pltpu.VMEM((groups, 3, steps, LANES), F32),
            pltpu.VMEM((groups, 6, SUB, LANES), F32),
            pltpu.VMEM((groups * SUB, LANES), F32),
        ),
        in_specs=vmem(count - 1 + 2 * len(kept) + 1),
        out_specs=vmem(3),
        compiler_params=PARAMS,
        cost_estimate=cost(100 * groups * steps * LANES, 24 * groups * steps * LANES),
        name="second",
    )(*received, *kept, *prefixes, weight)


def last_kernel(count, own_xor, *refs):
    received = refs[: count - 1]
    hidden_ref, prefix_ref, out_ref, turn_ref, made_ref, sems = refs[count - 1 :]
    groups, _, steps, _ = hidden_ref.shape
    runs = steps // SUB
    copies = []
    for group in range(groups):
        cell, hidden = arriving(count, own_xor, received, group, False)
        a, b, c, d, u, v = (prefix_ref[group, j] for j in range(6))
        cell, hidden = a * cell + b * hidden + u, c * cell + d * hidden + v
        for i in range(runs):
            rows = pl.ds(i * SUB, SUB)
            turn_ref[pl.ds(i, SUB, stride=runs), :] = (
                hidden_ref[group, 0, rows, :] * cell
                + hidden_ref[group, 1, rows, :] * hidden
                + hidden_ref[group, 2, rows, :]
            )
        rows = pl.ds(group * LANES, LANES)
        made_ref[rows, :] = turn_ref[...].T
        copies.append(pltpu.make_async_copy(made_ref.at[rows], out_ref.at[rows], sems.at[group]))
        copies[-1].start()
    for copy in copies:
        copy.wait()


def last(own_xor, received, hiddens, prefix):
    count = len(received) + 1
    groups, _, steps, _ = hiddens.shape
    return pl.pallas_call(
        functools.partial(last_kernel, count, own_xor),
        out_shape=jax.ShapeDtypeStruct((groups * LANES, steps), F32),
        in_specs=vmem(count + 1),
        compiler_params=PARAMS,
        out_specs=pl.BlockSpec(memory_space=pltpu.HBM),
        scratch_shapes=[
            pltpu.VMEM((steps, LANES), F32),
            pltpu.VMEM((groups * LANES, steps), F32),
            pltpu.SemaphoreType.DMA((groups,)),
        ],
        cost_estimate=cost(10 * groups * steps * LANES, 16 * groups * steps * LANES),
        name="last",
    )(*received, hiddens, prefix)


def pieces_of(groups, chips):
    half = max(1, groups // 2)
    pieces = [(1, 0, half), (1, half, groups - half)]
    pieces += [(away, 0, groups) for away in range(2, chips)]
    return [piece for piece in pieces if piece[2]]


def shards(tokens, in_weight, recur_weight, gate_bias, forget_offset):
    steps = tokens.shape[0]
    channels = recur_weight.shape[0]
    groups = channels // LANES
    per_owner = channels * GATES
    owners = lax.axis_size("chan")
    chips = owners // 2
    blocks = lax.axis_size("tm")
    own_xor = blocks & (blocks - 1) == 0

    bias = on_chip(gate_bias.T)
    weight = on_chip(recur_weight.T)
    offset = on_chip(forget_offset.reshape(1, steps))

    def to_core(value):
        return on_chip(lax.ppermute(value, "chan", [(i, i ^ 1) for i in range(owners)]))

    def to_chip(value, away):
        pairs = [(i, (i + 2 * away) % owners) for i in range(owners)]
        return on_chip(lax.ppermute(value, "chan", pairs))

    def to_blocks(value):
        arriving = []
        for k in range(1, blocks):
            pairs = [(i, i ^ k if own_xor else i + k) for i in range(blocks)]
            sent = lax.ppermute(value, "tm", [pair for pair in pairs if pair[1] < blocks])
            arriving.append(on_chip(sent))
        return arriving

    tokens, in_weight = off_chip(tokens), off_chip(in_weight)

    def product(parts, after):
        return products(tokens, in_weight, chips, per_owner, parts, after)

    coded = [[] for _ in range(groups)]

    def send(away, start, count, mine, theirs, inside):
        code = encoded(mine, theirs, inside, count * GROUP)
        arrived = to_chip(code, away)
        for place in range(count):
            coded[start + place].append((arrived, place))
        return code

    local_give, local_keep = ((0, which, 0, per_owner) for which in (GIVE, KEEP))
    codes = []
    for index, (away, start, count) in enumerate(pieces_of(groups, chips)):
        parts = tuple((away, which, start * GROUP, count * GROUP) for which in (GIVE, KEEP))
        if index == 0:
            (give,) = product(parts[:1], [])
            theirs = to_core(give)
            (keep,) = product(parts[1:], [])
            codes.append(send(away, start, count, keep, theirs, 0))
        else:
            give, keep = product(parts, codes[-1:])
            theirs = to_core(give)
            for group in range(start, start + count):
                codes.append(send(away, group, 1, keep, theirs, (group - start) * GROUP))
    (give,) = product((local_give,), codes[-1:])
    given = to_core(give)
    (keep,) = product((local_keep,), codes[-1:])
    kept, prefixes, totals = [], [], []
    for group in range(groups):
        arrived, places = zip(*coded[group]) if coded[group] else ((), ())
        k, p, total = first(
            group, places, keep, given, list(arrived), bias, weight, offset, totals
        )
        totals = [total]
        kept.append(k)
        prefixes.append(p)
    hiddens, prefix, total = second(own_xor, to_blocks(totals[0]), kept, prefixes, weight)
    return last(own_xor, to_blocks(total), hiddens, prefix)


def solution(mesh):
    placed = (
        P(("groups", "tm"), "chan"),
        P("chan", None),
        P("chan", None),
        P("chan", None),
        P(("groups", "tm")),
    )

    return jax.shard_map(
        shards, mesh=mesh, in_specs=placed, out_specs=P("chan", ("groups", "tm")), check_vma=False
    )
```

```python
import functools

import jax
import jax.numpy as jnp
from jax import lax
from jax.experimental import pallas as pl
from jax.experimental.pallas import tpu as pltpu
from jax.sharding import PartitionSpec as P


LANES = 128
SUB = 8
GATES = 4
GROUP = LANES * GATES
BINADES = 251.0
LOWEST = 125.0
GIVE, KEEP = 0, 1
F32 = jnp.float32
BF16 = jnp.bfloat16


def cost(flops, moved):
    return pl.CostEstimate(flops=int(flops), bytes_accessed=int(moved), transcendentals=0)


def vmem(count):
    return [pl.BlockSpec(memory_space=pltpu.VMEM)] * count


def in_hbm(count):
    return [pl.BlockSpec(memory_space=pltpu.HBM)] * count


def off_chip(value):
    return pltpu.with_memory_space_constraint(value, pltpu.HBM)


def on_chip(value):
    return pltpu.with_memory_space_constraint(value, pltpu.VMEM)


PARAMS = pltpu.CompilerParams(vmem_limit_bytes=16 << 20)


def product_kernel(chips, parts, per_owner, tokens_ref, weight_ref, *refs):
    outs, (x_ref, w_ref, sems) = refs[-3 - len(parts) : -3], refs[-3:]
    me = lax.axis_index("chan")
    chip, core = me // 2, me % 2
    tokens_copy = pltpu.make_async_copy(tokens_ref, x_ref, sems.at[w_ref.shape[0]])
    tokens_copy.start()
    copies = []
    for (away, which, first, width), out_ref in zip(parts, outs):
        owner = 2 * lax.rem(chip + away, chips) + (core if which == KEEP else 1 - core)
        for start in range(0, width, GROUP):
            slot = len(copies)
            column = pl.multiple_of(owner * per_owner + first + start, GROUP)
            copy = pltpu.make_async_copy(
                weight_ref.at[:, pl.ds(column, GROUP)], w_ref.at[slot], sems.at[slot]
            )
            copy.start()
            copies.append((copy, out_ref, start))
    tokens_copy.wait()
    for slot, (copy, out_ref, start) in enumerate(copies):
        copy.wait()
        out_ref[:, pl.ds(start, GROUP)] = jnp.dot(
            x_ref[...], w_ref[slot], preferred_element_type=F32
        )


def products(tokens, in_weight, chips, per_owner, parts, after):
    steps, depth = tokens.shape
    slots = sum(width for _, _, _, width in parts) // GROUP
    return pl.pallas_call(
        functools.partial(product_kernel, chips, parts, per_owner),
        out_shape=[pltpu.VMEM((steps, width), F32) for _, _, _, width in parts],
        in_specs=in_hbm(2) + vmem(len(after)),
        out_specs=vmem(len(parts)),
        scratch_shapes=[
            pltpu.VMEM((steps, depth), BF16),
            pltpu.VMEM((slots, depth, GROUP), BF16),
            pltpu.SemaphoreType.DMA((slots + 1,)),
        ],
        compiler_params=PARAMS,
        cost_estimate=cost(2 * slots * steps * depth * GROUP, 2 * slots * depth * GROUP),
        name="products",
    )(tokens, in_weight, *after)


def encode_kernel(first, mine_ref, theirs_ref, out_ref, sum_ref):
    steps, width = sum_ref.shape
    blocks = width // LANES
    top = jnp.zeros((steps, LANES), F32)
    for block in range(blocks):
        cols = pl.ds(first + block * LANES, LANES)
        both = mine_ref[:, cols] + theirs_ref[:, cols]
        sum_ref[:, pl.ds(block * LANES, LANES)] = both
        top = jnp.maximum(top, jnp.abs(both))
    top = jnp.max(top, axis=0, keepdims=True)
    top = jnp.maximum(top, 1e-30) * 1.0078125
    scale = top.astype(BF16).astype(F32)
    out_ref[pl.ds(blocks * steps, SUB), :] = jnp.broadcast_to(scale, (SUB, LANES)).astype(BF16)
    inverse = 1.0 / scale
    for block in range(blocks):
        value = sum_ref[:, pl.ds(block * LANES, LANES)]
        level = jnp.sqrt(jnp.abs(value) * inverse) * BINADES - LOWEST
        code = jnp.exp2(level)
        out_ref[pl.ds(block * steps, steps), :] = jnp.where(value < 0.0, -code, code).astype(BF16)


def encoded(mine, theirs, first, width):
    steps = mine.shape[0]
    rows = steps * (width // LANES) + SUB
    return pl.pallas_call(
        functools.partial(encode_kernel, first),
        out_shape=pltpu.VMEM((rows, LANES), BF16),
        in_specs=vmem(2),
        out_specs=pl.BlockSpec(memory_space=pltpu.VMEM),
        scratch_shapes=[pltpu.VMEM((steps, width), F32)],
        compiler_params=PARAMS,
        cost_estimate=cost(20 * steps * width, 10 * steps * width),
        name="encode",
    )(mine, theirs)


def decoded(code, scale):
    level = (jnp.log2(jnp.abs(code)) + LOWEST) * (1.0 / BINADES)
    size = level * level * scale
    return jnp.where(code < 0.0, -size, size)


def compose(early, later):
    e1, e2, e3, e4, e5, e6 = early
    l1, l2, l3, l4, l5, l6 = later
    return (
        l1 * e1 + l2 * e3,
        l1 * e2 + l2 * e4,
        l3 * e1 + l4 * e3,
        l3 * e2 + l4 * e4,
        l1 * e5 + l2 * e6 + l5,
        l3 * e5 + l4 * e6 + l6,
    )


def compose_lower(early, later):
    e1, e3, e4, e5, e6 = early
    l1, l3, l4, l5, l6 = later
    return (
        l1 * e1,
        l3 * e1 + l4 * e3,
        l4 * e4,
        l1 * e5 + l5,
        l3 * e5 + l4 * e6 + l6,
    )


def sub_blocks(terms, join, identity):
    row = lax.broadcasted_iota(jnp.int32, (SUB, LANES), 0)
    reach = 1
    while reach < SUB:
        moved = tuple(
            jnp.where(row >= reach, pltpu.roll(term, reach, 0), unit)
            for term, unit in zip(terms, identity)
        )
        terms = join(moved, terms)
        reach *= 2
    before = tuple(
        jnp.where(row >= 1, pltpu.roll(term, 1, 0), unit) for term, unit in zip(terms, identity)
    )
    return before, terms


LOWER_UNIT = (1.0, 0.0, 1.0, 0.0, 0.0)
UNIT = (1.0, 0.0, 0.0, 1.0, 0.0, 0.0)


def sigmoid(x):
    return 1.0 / (1.0 + jnp.exp(-x))


def first_kernel(start, places, earlier, *refs):
    groups, remotes = 1, len(places)
    refs = list(refs)
    mine_ref, theirs_ref = refs[:2]
    codes = refs[2 : 2 + remotes]
    bias_ref, weight_ref, offset_ref = refs[2 + remotes : 5 + remotes]
    totals_before = refs[5 + remotes : 5 + remotes + earlier]
    kept_ref, run_ref, prefix_ref, totals_ref, sum_ref, late_ref = refs[5 + remotes + earlier :]
    steps = mine_ref.shape[0]
    runs = steps // SUB
    done = 0
    for ref in totals_before:
        totals_ref[pl.ds(done, ref.shape[0]), :] = ref[...]
        done += ref.shape[0]
    scales = [
        ref[pl.ds(ref.shape[0] - SUB, SUB), :][0:1, :].astype(F32) for ref in codes
    ]
    late_ref[...] = jnp.broadcast_to(offset_ref[...], (LANES, steps)).T
    lane = lax.broadcasted_iota(jnp.int32, (SUB, LANES), 1)
    quarter = lane // (LANES // GATES)
    inner = lane % (LANES // GATES)
    picks = [inner * GATES + (quarter - q + GATES) % GATES for q in range(GATES)]
    for group in range(groups):
        for q in range(GATES):
            block = group * GATES + q
            cols = pl.ds(start * GROUP + block * LANES, LANES)
            value = mine_ref[:, cols] + theirs_ref[:, cols]
            for ref, scale, place in zip(codes, scales, places):
                rows = pl.ds((place * GATES + block) * steps, steps)
                value = value + decoded(ref[rows, :].astype(F32), scale)
            sum_ref[q] = value
        channels = pl.ds((start + group) * LANES, LANES)
        biases = [
            jnp.broadcast_to(bias_ref[k : k + 1, channels], (SUB, LANES)) for k in range(GATES)
        ]
        out_weight = jnp.broadcast_to(weight_ref[1:2, channels], (SUB, LANES))
        run = None
        for i in range(runs):
            loaded = [
                jnp.take_along_axis(sum_ref[q, pl.ds(i, SUB, stride=runs), :], picks[q], axis=1)
                for q in range(GATES)
            ]
            pre = []
            for k in range(GATES):
                part = loaded[(0 - k) % GATES]
                for p in range(1, GATES):
                    part = jnp.where(quarter == p, loaded[(p - k) % GATES], part)
                if k:
                    part = pltpu.roll(part, LANES - k * (LANES // GATES), 1)
                pre.append(part + biases[k])
            pre_forget = pre[1] - late_ref[pl.ds(i, SUB, stride=runs), :]
            forget = sigmoid(pre_forget)
            output = sigmoid(pre[3])
            cell = sigmoid(pre[0]) * jnp.tanh(pre[2])
            squashed = jnp.tanh(cell)
            hidden_cell = output * (1.0 - squashed * squashed) * forget
            hidden_hidden = output * (1.0 - output) * out_weight * squashed
            term = (forget, hidden_cell, hidden_hidden, cell, output * squashed)
            run = term if run is None else compose_lower(run, term)
            rows = pl.ds(i * SUB, SUB)
            kept_ref[group, 0, rows, :] = pre_forget
            kept_ref[group, 1, rows, :] = pre[3]
            kept_ref[group, 2, rows, :] = cell
            for index, part in enumerate(run):
                run_ref[group, index, rows, :] = part
        before, total = sub_blocks(run, compose_lower, LOWER_UNIT)
        for index, term in enumerate(before):
            prefix_ref[group, index] = term
        for index, term in enumerate(total):
            totals_ref[pl.ds(done + group * SUB + index, 1), :] = term[SUB - 1 : SUB, :]
        for index in range(len(total), SUB):
            totals_ref[pl.ds(done + group * SUB + index, 1), :] = jnp.zeros((1, LANES), F32)


def first(start, places, mine, theirs, codes, bias, weight, offset, earlier):
    steps = mine.shape[0]
    groups = 1
    rows = sum(e.shape[0] for e in earlier) + groups * SUB
    count = 5 + len(codes) + len(earlier)
    return pl.pallas_call(
        functools.partial(first_kernel, start, places, len(earlier)),
        out_shape=(
            pltpu.VMEM((groups, 3, steps, LANES), F32),
            pltpu.VMEM((groups, 5, steps, LANES), F32),
            pltpu.VMEM((groups, 5, SUB, LANES), F32),
            pltpu.VMEM((rows, LANES), F32),
        ),
        in_specs=vmem(count),
        out_specs=vmem(4),
        scratch_shapes=[
            pltpu.VMEM((GATES, steps, LANES), F32),
            pltpu.VMEM((steps, LANES), F32),
        ],
        compiler_params=PARAMS,
        cost_estimate=cost(60 * steps * groups * GROUP, 20 * steps * groups * GROUP),
        name="first",
    )(mine, theirs, *codes, bias, weight, offset, *earlier)


def in_turn(me, count, own_xor, received):
    for position in range(count - 1):
        picked = received[0]
        for k in range(2, count):
            picked = jnp.where(position == (me ^ k if own_xor else me - k), received[k - 1], picked)
        yield picked, position < me


def arriving(count, own_xor, received, group, lower):
    me = lax.axis_index("tm")
    rows = [ref[pl.ds(group * SUB, SUB), :] for ref in received]
    cell = jnp.zeros((1, LANES), F32)
    hidden = jnp.zeros((1, LANES), F32)
    for maps, counts in in_turn(me, count, own_xor, rows):
        if lower:
            a, c, d, u, v = (maps[j : j + 1, :] for j in range(5))
            new_cell = a * cell + u
        else:
            a, b, c, d, u, v = (maps[j : j + 1, :] for j in range(6))
            new_cell = a * cell + b * hidden + u
        new_hidden = c * cell + d * hidden + v
        cell = jnp.where(counts, new_cell, cell)
        hidden = jnp.where(counts, new_hidden, hidden)
    return cell, hidden


def lead_kernel(groups, *refs):
    runs, befores, lead_ref = refs[:groups], refs[groups : 2 * groups], refs[-1]
    steps = lead_ref.shape[2]
    for group in range(groups):
        before = tuple(befores[group][0, j] for j in range(5))
        for i in range(steps // SUB):
            terms = before
            if i:
                rows = pl.ds((i - 1) * SUB, SUB)
                terms = compose_lower(before, tuple(runs[group][0, j, rows, :] for j in range(5)))
            for index, term in enumerate(terms):
                lead_ref[group, index, pl.ds(i * SUB, SUB), :] = term


def leads(runs, befores):
    groups, steps = len(runs), runs[0].shape[2]
    return pl.pallas_call(
        functools.partial(lead_kernel, groups),
        out_shape=pltpu.VMEM((groups, 5, steps, LANES), F32),
        in_specs=vmem(2 * groups),
        out_specs=pl.BlockSpec(memory_space=pltpu.VMEM),
        compiler_params=PARAMS,
        cost_estimate=cost(12 * groups * steps * LANES, 40 * groups * steps * LANES),
        name="leads",
    )(*runs, *befores)


def second_kernel(count, own_xor, groups, *refs):
    received, kept = refs[: count - 1], refs[count - 1 : count - 1 + groups]
    lead_ref, weight_ref, hidden_ref, prefix_ref, totals_ref = refs[count - 1 + groups :]
    steps = lead_ref.shape[2]
    for group, kept_ref in enumerate(kept):
        first_cell, first_hidden = arriving(count, own_xor, received, group, True)
        first_cell = jnp.broadcast_to(first_cell, (SUB, LANES))
        first_hidden = jnp.broadcast_to(first_hidden, (SUB, LANES))
        channels = pl.ds(group * LANES, LANES)
        forget_weight = jnp.broadcast_to(weight_ref[0:1, channels], (SUB, LANES))
        out_weight = jnp.broadcast_to(weight_ref[1:2, channels], (SUB, LANES))
        run = None
        for i in range(steps // SUB):
            rows = pl.ds(i * SUB, SUB)
            a, c, d, u, v = (lead_ref[group, j, rows, :] for j in range(5))
            cell = a * first_cell + u
            hidden = c * first_cell + d * first_hidden + v
            forget = sigmoid(kept_ref[0, 0, rows, :] + forget_weight * hidden)
            output = sigmoid(kept_ref[0, 1, rows, :] + out_weight * hidden)
            kept_cell = forget * cell
            new_cell = kept_cell + kept_ref[0, 2, rows, :]
            squashed = jnp.tanh(new_cell)
            slope = output * (1.0 - squashed * squashed)
            cell_hidden = kept_cell * (1.0 - forget) * forget_weight
            hidden_cell = slope * forget
            hidden_hidden = output * (1.0 - output) * out_weight * squashed + slope * cell_hidden
            offset_cell = new_cell - kept_cell - cell_hidden * hidden
            offset_hidden = output * squashed - hidden_cell * cell - hidden_hidden * hidden
            term = (forget, cell_hidden, hidden_cell, hidden_hidden, offset_cell, offset_hidden)
            run = term if run is None else compose(run, term)
            hidden_ref[group, 0, rows, :] = run[2]
            hidden_ref[group, 1, rows, :] = run[3]
            hidden_ref[group, 2, rows, :] = run[5]
        before, total = sub_blocks(run, compose, UNIT)
        for index, term in enumerate(before):
            prefix_ref[group, index] = term
        for index, term in enumerate(total):
            totals_ref[pl.ds(group * SUB + index, 1), :] = term[SUB - 1 : SUB, :]
        for index in range(len(total), SUB):
            totals_ref[pl.ds(group * SUB + index, 1), :] = jnp.zeros((1, LANES), F32)


def second(own_xor, received, kept, lead, weight):
    count = len(received) + 1
    groups, steps = len(kept), lead.shape[2]
    return pl.pallas_call(
        functools.partial(second_kernel, count, own_xor, groups),
        out_shape=(
            pltpu.VMEM((groups, 3, steps, LANES), F32),
            pltpu.VMEM((groups, 6, SUB, LANES), F32),
            pltpu.VMEM((groups * SUB, LANES), F32),
        ),
        in_specs=vmem(count - 1 + groups + 2),
        out_specs=vmem(3),
        compiler_params=PARAMS,
        cost_estimate=cost(80 * groups * steps * LANES, 24 * groups * steps * LANES),
        name="second",
    )(*received, *kept, lead, weight)


def ordered_kernel(hidden_ref, prefix_ref, out_ref):
    groups, _, steps, _ = hidden_ref.shape
    runs = steps // SUB
    for group in range(groups):
        a, b, c, d, u, v = (prefix_ref[group, j] for j in range(6))
        for i in range(runs):
            rows, times = pl.ds(i * SUB, SUB), pl.ds(i, SUB, stride=runs)
            by_cell, by_hidden, offset = (hidden_ref[group, j, rows, :] for j in range(3))
            out_ref[3 * group, times, :] = by_cell * a + by_hidden * c
            out_ref[3 * group + 1, times, :] = by_cell * b + by_hidden * d
            out_ref[3 * group + 2, times, :] = by_cell * u + by_hidden * v + offset


def ordered(hiddens, prefix):
    groups, _, steps, _ = hiddens.shape
    return pl.pallas_call(
        ordered_kernel,
        out_shape=pltpu.VMEM((3 * groups, steps, LANES), F32),
        in_specs=vmem(2),
        out_specs=pl.BlockSpec(memory_space=pltpu.VMEM),
        compiler_params=PARAMS,
        cost_estimate=cost(10 * groups * steps * LANES, 24 * groups * steps * LANES),
        name="ordered",
    )(hiddens, prefix)


def last_kernel(count, own_xor, *refs):
    received = refs[: count - 1]
    maps_ref, out_ref, made_ref, sems = refs[count - 1 :]
    groups = maps_ref.shape[0] // 3
    copies = []
    for group in range(groups):
        cell, hidden = arriving(count, own_xor, received, group, False)
        made = maps_ref[3 * group] * cell + maps_ref[3 * group + 1] * hidden
        rows = pl.ds(group * LANES, LANES)
        made_ref[rows, :] = (made + maps_ref[3 * group + 2]).T
        copies.append(pltpu.make_async_copy(made_ref.at[rows], out_ref.at[rows], sems.at[group]))
        copies[-1].start()
    for copy in copies:
        copy.wait()


def last(own_xor, received, maps):
    count = len(received) + 1
    groups, steps = maps.shape[0] // 3, maps.shape[1]
    return pl.pallas_call(
        functools.partial(last_kernel, count, own_xor),
        out_shape=jax.ShapeDtypeStruct((groups * LANES, steps), F32),
        in_specs=vmem(count),
        out_specs=pl.BlockSpec(memory_space=pltpu.HBM),
        scratch_shapes=[
            pltpu.VMEM((groups * LANES, steps), F32),
            pltpu.SemaphoreType.DMA((groups,)),
        ],
        compiler_params=PARAMS,
        cost_estimate=cost(10 * groups * steps * LANES, 16 * groups * steps * LANES),
        name="last",
    )(*received, maps)


def pieces_of(groups, chips):
    half = max(1, groups - 1)
    pieces = [(1, 0, half), (1, half, groups - half)]
    pieces += [(away, 0, groups) for away in range(2, chips)]
    return [piece for piece in pieces if piece[2]]


def shards(tokens, in_weight, recur_weight, gate_bias, forget_offset):
    steps = tokens.shape[0]
    channels = recur_weight.shape[0]
    groups = channels // LANES
    per_owner = channels * GATES
    owners = lax.axis_size("chan")
    chips = owners // 2
    blocks = lax.axis_size("tm")
    own_xor = blocks & (blocks - 1) == 0

    bias = on_chip(gate_bias.T)
    weight = on_chip(recur_weight.T)
    offset = on_chip(forget_offset.reshape(1, steps))

    def to_core(value):
        return on_chip(lax.ppermute(value, "chan", [(i, i ^ 1) for i in range(owners)]))

    def to_chip(value, away):
        pairs = [(i, (i + 2 * away) % owners) for i in range(owners)]
        return on_chip(lax.ppermute(value, "chan", pairs))

    def to_blocks(value):
        arriving = []
        for k in range(1, blocks):
            pairs = [(i, i ^ k if own_xor else i + k) for i in range(blocks)]
            sent = lax.ppermute(value, "tm", [pair for pair in pairs if pair[1] < blocks])
            arriving.append(on_chip(sent))
        return arriving

    tokens, in_weight = off_chip(tokens), off_chip(in_weight)

    def product(parts, after):
        return products(tokens, in_weight, chips, per_owner, parts, after)

    coded = [[] for _ in range(groups)]

    def send(away, start, count, mine, theirs, inside):
        code = encoded(mine, theirs, inside, count * GROUP)
        arrived = to_chip(code, away)
        for place in range(count):
            coded[start + place].append((arrived, place))
        return code

    local_give, local_keep = ((0, which, 0, per_owner) for which in (GIVE, KEEP))
    codes = []
    for index, (away, start, count) in enumerate(pieces_of(groups, chips)):
        parts = tuple((away, which, start * GROUP, count * GROUP) for which in (GIVE, KEEP))
        if index == 0:
            (give,) = product(parts[:1], [])
            theirs = to_core(give)
            (keep,) = product(parts[1:], [])
            codes.append(send(away, start, count, keep, theirs, 0))
        else:
            give, keep = product(parts, codes[-1:])
            theirs = to_core(give)
            codes.append(send(away, start, count, keep, theirs, 0))
    (give,) = product((local_give,), codes[-1:])
    given = to_core(give)
    (keep,) = product((local_keep,), codes[-1:])
    kept, runs, prefixes, totals = [], [], [], []
    for group in range(groups):
        arrived, places = zip(*coded[group]) if coded[group] else ((), ())
        k, r, p, total = first(
            group, places, keep, given, list(arrived), bias, weight, offset, totals
        )
        totals = [total]
        kept.append(k)
        runs.append(r)
        prefixes.append(p)
    received = to_blocks(totals[0])
    lead = leads(runs, prefixes)
    hiddens, prefix, total = second(own_xor, received, kept, lead, weight)
    received = to_blocks(total)
    maps = ordered(hiddens, prefix)
    return last(own_xor, received, maps)


def solution(mesh):
    placed = (
        P(("groups", "tm"), "chan"),
        P("chan", None),
        P("chan", None),
        P("chan", None),
        P(("groups", "tm")),
    )

    return jax.shard_map(
        shards, mesh=mesh, in_specs=placed, out_specs=P("chan", ("groups", "tm")), check_vma=False
    )
```

```python
import functools

import jax
import jax.numpy as jnp
from jax import lax
from jax.experimental import pallas as pl
from jax.experimental.pallas import tpu as pltpu
from jax.sharding import PartitionSpec as P


LANES = 128
SUB = 8
GATES = 4
GROUP = LANES * GATES
BINADES = 251.0
LOWEST = 125.0
GIVE, KEEP = 0, 1
F32 = jnp.float32
BF16 = jnp.bfloat16


def cost(flops, moved):
    return pl.CostEstimate(flops=int(flops), bytes_accessed=int(moved), transcendentals=0)


def vmem(count):
    return [pl.BlockSpec(memory_space=pltpu.VMEM)] * count


def in_hbm(count):
    return [pl.BlockSpec(memory_space=pltpu.HBM)] * count


def off_chip(value):
    return pltpu.with_memory_space_constraint(value, pltpu.HBM)


def on_chip(value):
    return pltpu.with_memory_space_constraint(value, pltpu.VMEM)


PARAMS = pltpu.CompilerParams(vmem_limit_bytes=16 << 20)


def product_kernel(chips, parts, per_owner, tokens_ref, weight_ref, *refs):
    outs, (x_ref, w_ref, sems) = refs[-3 - len(parts) : -3], refs[-3:]
    me = lax.axis_index("chan")
    chip, core = me // 2, me % 2
    tokens_copy = pltpu.make_async_copy(tokens_ref, x_ref, sems.at[w_ref.shape[0]])
    tokens_copy.start()
    copies = []
    for (away, which, first, width), out_ref in zip(parts, outs):
        owner = 2 * lax.rem(chip + away, chips) + (core if which == KEEP else 1 - core)
        for start in range(0, width, GROUP):
            slot = len(copies)
            column = pl.multiple_of(owner * per_owner + first + start, GROUP)
            copy = pltpu.make_async_copy(
                weight_ref.at[:, pl.ds(column, GROUP)], w_ref.at[slot], sems.at[slot]
            )
            copy.start()
            copies.append((copy, out_ref, start))
    tokens_copy.wait()
    for slot, (copy, out_ref, start) in enumerate(copies):
        copy.wait()
        out_ref[:, pl.ds(start, GROUP)] = jnp.dot(
            x_ref[...], w_ref[slot], preferred_element_type=F32
        )


def products(tokens, in_weight, chips, per_owner, parts, after):
    steps, depth = tokens.shape
    slots = sum(width for _, _, _, width in parts) // GROUP
    return pl.pallas_call(
        functools.partial(product_kernel, chips, parts, per_owner),
        out_shape=[pltpu.VMEM((steps, width), F32) for _, _, _, width in parts],
        in_specs=in_hbm(2) + vmem(len(after)),
        out_specs=vmem(len(parts)),
        scratch_shapes=[
            pltpu.VMEM((steps, depth), BF16),
            pltpu.VMEM((slots, depth, GROUP), BF16),
            pltpu.SemaphoreType.DMA((slots + 1,)),
        ],
        compiler_params=PARAMS,
        cost_estimate=cost(2 * slots * steps * depth * GROUP, 2 * slots * depth * GROUP),
        name="products",
    )(tokens, in_weight, *after)


def encode_kernel(first, mine_ref, theirs_ref, out_ref, sum_ref):
    steps, width = sum_ref.shape
    blocks = width // LANES
    top = jnp.zeros((steps, LANES), F32)
    for block in range(blocks):
        cols = pl.ds(first + block * LANES, LANES)
        both = mine_ref[:, cols] + theirs_ref[:, cols]
        sum_ref[:, pl.ds(block * LANES, LANES)] = both
        top = jnp.maximum(top, jnp.abs(both))
    top = jnp.max(top, axis=0, keepdims=True)
    top = jnp.maximum(top, 1e-30) * 1.0078125
    scale = top.astype(BF16).astype(F32)
    out_ref[pl.ds(blocks * steps, SUB), :] = jnp.broadcast_to(scale, (SUB, LANES)).astype(BF16)
    inverse = 1.0 / scale
    for block in range(blocks):
        value = sum_ref[:, pl.ds(block * LANES, LANES)]
        level = jnp.sqrt(jnp.abs(value) * inverse) * BINADES - LOWEST
        code = jnp.exp2(level)
        out_ref[pl.ds(block * steps, steps), :] = jnp.where(value < 0.0, -code, code).astype(BF16)


def encoded(mine, theirs, first, width):
    steps = mine.shape[0]
    rows = steps * (width // LANES) + SUB
    return pl.pallas_call(
        functools.partial(encode_kernel, first),
        out_shape=pltpu.VMEM((rows, LANES), BF16),
        in_specs=vmem(2),
        out_specs=pl.BlockSpec(memory_space=pltpu.VMEM),
        scratch_shapes=[pltpu.VMEM((steps, width), F32)],
        compiler_params=PARAMS,
        cost_estimate=cost(20 * steps * width, 10 * steps * width),
        name="encode",
    )(mine, theirs)


def decoded(code, scale):
    level = (jnp.log2(jnp.abs(code)) + LOWEST) * (1.0 / BINADES)
    size = level * level * scale
    return jnp.where(code < 0.0, -size, size)


def compose(early, later):
    e1, e2, e3, e4, e5, e6 = early
    l1, l2, l3, l4, l5, l6 = later
    return (
        l1 * e1 + l2 * e3,
        l1 * e2 + l2 * e4,
        l3 * e1 + l4 * e3,
        l3 * e2 + l4 * e4,
        l1 * e5 + l2 * e6 + l5,
        l3 * e5 + l4 * e6 + l6,
    )


def compose_lower(early, later):
    e1, e3, e4, e5, e6 = early
    l1, l3, l4, l5, l6 = later
    return (
        l1 * e1,
        l3 * e1 + l4 * e3,
        l4 * e4,
        l1 * e5 + l5,
        l3 * e5 + l4 * e6 + l6,
    )


def sub_blocks(terms, join, identity):
    row = lax.broadcasted_iota(jnp.int32, (SUB, LANES), 0)
    reach = 1
    while reach < SUB:
        moved = tuple(
            jnp.where(row >= reach, pltpu.roll(term, reach, 0), unit)
            for term, unit in zip(terms, identity)
        )
        terms = join(moved, terms)
        reach *= 2
    before = tuple(
        jnp.where(row >= 1, pltpu.roll(term, 1, 0), unit) for term, unit in zip(terms, identity)
    )
    return before, terms


LOWER_UNIT = (1.0, 0.0, 1.0, 0.0, 0.0)
UNIT = (1.0, 0.0, 0.0, 1.0, 0.0, 0.0)


def sigmoid(x):
    return 1.0 / (1.0 + jnp.exp(-x))


def first_kernel(start, places, earlier, *refs):
    groups, remotes = 1, len(places)
    refs = list(refs)
    mine_ref, theirs_ref = refs[:2]
    codes = refs[2 : 2 + remotes]
    bias_ref, weight_ref, offset_ref = refs[2 + remotes : 5 + remotes]
    totals_before = refs[5 + remotes : 5 + remotes + earlier]
    kept_ref, run_ref, prefix_ref, totals_ref, sum_ref, late_ref = refs[5 + remotes + earlier :]
    steps = mine_ref.shape[0]
    runs = steps // SUB
    done = 0
    for ref in totals_before:
        totals_ref[pl.ds(done, ref.shape[0]), :] = ref[...]
        done += ref.shape[0]
    scales = [
        ref[pl.ds(ref.shape[0] - SUB, SUB), :][0:1, :].astype(F32) for ref in codes
    ]
    late_ref[...] = jnp.broadcast_to(offset_ref[...], (LANES, steps)).T
    lane = lax.broadcasted_iota(jnp.int32, (SUB, LANES), 1)
    quarter = lane // (LANES // GATES)
    inner = lane % (LANES // GATES)
    picks = [inner * GATES + (quarter - q + GATES) % GATES for q in range(GATES)]
    for group in range(groups):
        for q in range(GATES):
            block = group * GATES + q
            cols = pl.ds(start * GROUP + block * LANES, LANES)
            value = mine_ref[:, cols] + theirs_ref[:, cols]
            for ref, scale, place in zip(codes, scales, places):
                rows = pl.ds((place * GATES + block) * steps, steps)
                value = value + decoded(ref[rows, :].astype(F32), scale)
            sum_ref[q] = value
        channels = pl.ds((start + group) * LANES, LANES)
        biases = [
            jnp.broadcast_to(bias_ref[k : k + 1, channels], (SUB, LANES)) for k in range(GATES)
        ]
        out_weight = jnp.broadcast_to(weight_ref[1:2, channels], (SUB, LANES))
        run = None
        for i in range(runs):
            loaded = [
                jnp.take_along_axis(sum_ref[q, pl.ds(i, SUB, stride=runs), :], picks[q], axis=1)
                for q in range(GATES)
            ]
            pre = []
            for k in range(GATES):
                part = loaded[(0 - k) % GATES]
                for p in range(1, GATES):
                    part = jnp.where(quarter == p, loaded[(p - k) % GATES], part)
                if k:
                    part = pltpu.roll(part, LANES - k * (LANES // GATES), 1)
                pre.append(part + biases[k])
            pre_forget = pre[1] - late_ref[pl.ds(i, SUB, stride=runs), :]
            forget = sigmoid(pre_forget)
            output = sigmoid(pre[3])
            cell = sigmoid(pre[0]) * jnp.tanh(pre[2])
            squashed = jnp.tanh(cell)
            hidden_cell = output * (1.0 - squashed * squashed) * forget
            hidden_hidden = output * (1.0 - output) * out_weight * squashed
            term = (forget, hidden_cell, hidden_hidden, cell, output * squashed)
            run = term if run is None else compose_lower(run, term)
            rows = pl.ds(i * SUB, SUB)
            kept_ref[group, 0, rows, :] = pre_forget
            kept_ref[group, 1, rows, :] = pre[3]
            kept_ref[group, 2, rows, :] = cell
            for index, part in enumerate(run):
                run_ref[group, index, rows, :] = part
        before, total = sub_blocks(run, compose_lower, LOWER_UNIT)
        for index, term in enumerate(before):
            prefix_ref[group, index] = term
        for index, term in enumerate(total):
            totals_ref[pl.ds(done + group * SUB + index, 1), :] = term[SUB - 1 : SUB, :]
        for index in range(len(total), SUB):
            totals_ref[pl.ds(done + group * SUB + index, 1), :] = jnp.zeros((1, LANES), F32)


def first(start, places, mine, theirs, codes, bias, weight, offset, earlier):
    steps = mine.shape[0]
    groups = 1
    rows = sum(e.shape[0] for e in earlier) + groups * SUB
    count = 5 + len(codes) + len(earlier)
    return pl.pallas_call(
        functools.partial(first_kernel, start, places, len(earlier)),
        out_shape=(
            pltpu.VMEM((groups, 3, steps, LANES), F32),
            pltpu.VMEM((groups, 5, steps, LANES), F32),
            pltpu.VMEM((groups, 5, SUB, LANES), F32),
            pltpu.VMEM((rows, LANES), F32),
        ),
        in_specs=vmem(count),
        out_specs=vmem(4),
        scratch_shapes=[
            pltpu.VMEM((GATES, steps, LANES), F32),
            pltpu.VMEM((steps, LANES), F32),
        ],
        compiler_params=PARAMS,
        cost_estimate=cost(60 * steps * groups * GROUP, 20 * steps * groups * GROUP),
        name="first",
    )(mine, theirs, *codes, bias, weight, offset, *earlier)


def in_turn(me, count, own_xor, received):
    for position in range(count - 1):
        picked = received[0]
        for k in range(2, count):
            picked = jnp.where(position == (me ^ k if own_xor else me - k), received[k - 1], picked)
        yield picked, position < me


def arriving(count, own_xor, received, group, lower):
    me = lax.axis_index("tm")
    rows = [ref[pl.ds(group * SUB, SUB), :] for ref in received]
    cell = jnp.zeros((1, LANES), F32)
    hidden = jnp.zeros((1, LANES), F32)
    for maps, counts in in_turn(me, count, own_xor, rows):
        if lower:
            a, c, d, u, v = (maps[j : j + 1, :] for j in range(5))
            new_cell = a * cell + u
        else:
            a, b, c, d, u, v = (maps[j : j + 1, :] for j in range(6))
            new_cell = a * cell + b * hidden + u
        new_hidden = c * cell + d * hidden + v
        cell = jnp.where(counts, new_cell, cell)
        hidden = jnp.where(counts, new_hidden, hidden)
    return cell, hidden


def lead_kernel(groups, *refs):
    runs, befores, lead_ref = refs[:groups], refs[groups : 2 * groups], refs[-1]
    steps = lead_ref.shape[2]
    for group in range(groups):
        before = tuple(befores[group][0, j] for j in range(5))
        for i in range(steps // SUB):
            terms = before
            if i:
                rows = pl.ds((i - 1) * SUB, SUB)
                terms = compose_lower(before, tuple(runs[group][0, j, rows, :] for j in range(5)))
            for index, term in enumerate(terms):
                lead_ref[group, index, pl.ds(i * SUB, SUB), :] = term


def leads(runs, befores):
    groups, steps = len(runs), runs[0].shape[2]
    return pl.pallas_call(
        functools.partial(lead_kernel, groups),
        out_shape=pltpu.VMEM((groups, 5, steps, LANES), F32),
        in_specs=vmem(2 * groups),
        out_specs=pl.BlockSpec(memory_space=pltpu.VMEM),
        compiler_params=PARAMS,
        cost_estimate=cost(12 * groups * steps * LANES, 40 * groups * steps * LANES),
        name="leads",
    )(*runs, *befores)


def second_kernel(count, own_xor, groups, *refs):
    received, kept = refs[: count - 1], refs[count - 1 : count - 1 + groups]
    lead_ref, weight_ref, hidden_ref, prefix_ref, totals_ref = refs[count - 1 + groups :]
    steps = lead_ref.shape[2]
    for group, kept_ref in enumerate(kept):
        first_cell, first_hidden = arriving(count, own_xor, received, group, True)
        first_cell = jnp.broadcast_to(first_cell, (SUB, LANES))
        first_hidden = jnp.broadcast_to(first_hidden, (SUB, LANES))
        channels = pl.ds(group * LANES, LANES)
        forget_weight = jnp.broadcast_to(weight_ref[0:1, channels], (SUB, LANES))
        out_weight = jnp.broadcast_to(weight_ref[1:2, channels], (SUB, LANES))
        run = None
        for i in range(steps // SUB):
            rows = pl.ds(i * SUB, SUB)
            a, c, d, u, v = (lead_ref[group, j, rows, :] for j in range(5))
            cell = a * first_cell + u
            hidden = c * first_cell + d * first_hidden + v
            forget = sigmoid(kept_ref[0, 0, rows, :] + forget_weight * hidden)
            output = sigmoid(kept_ref[0, 1, rows, :] + out_weight * hidden)
            kept_cell = forget * cell
            new_cell = kept_cell + kept_ref[0, 2, rows, :]
            squashed = jnp.tanh(new_cell)
            slope = output * (1.0 - squashed * squashed)
            cell_hidden = kept_cell * (1.0 - forget) * forget_weight
            hidden_cell = slope * forget
            hidden_hidden = output * (1.0 - output) * out_weight * squashed + slope * cell_hidden
            offset_cell = new_cell - kept_cell - cell_hidden * hidden
            offset_hidden = output * squashed - hidden_cell * cell - hidden_hidden * hidden
            term = (forget, cell_hidden, hidden_cell, hidden_hidden, offset_cell, offset_hidden)
            run = term if run is None else compose(run, term)
            hidden_ref[group, 0, rows, :] = run[2]
            hidden_ref[group, 1, rows, :] = run[3]
            hidden_ref[group, 2, rows, :] = run[5]
        before, total = sub_blocks(run, compose, UNIT)
        for index, term in enumerate(before):
            prefix_ref[group, index] = term
        for index, term in enumerate(total):
            totals_ref[pl.ds(group * SUB + index, 1), :] = term[SUB - 1 : SUB, :]
        for index in range(len(total), SUB):
            totals_ref[pl.ds(group * SUB + index, 1), :] = jnp.zeros((1, LANES), F32)


def second(own_xor, received, kept, lead, weight):
    count = len(received) + 1
    groups, steps = len(kept), lead.shape[2]
    return pl.pallas_call(
        functools.partial(second_kernel, count, own_xor, groups),
        out_shape=(
            pltpu.VMEM((groups, 3, steps, LANES), F32),
            pltpu.VMEM((groups, 6, SUB, LANES), F32),
            pltpu.VMEM((groups * SUB, LANES), F32),
        ),
        in_specs=vmem(count - 1 + groups + 2),
        out_specs=vmem(3),
        compiler_params=PARAMS,
        cost_estimate=cost(80 * groups * steps * LANES, 24 * groups * steps * LANES),
        name="second",
    )(*received, *kept, lead, weight)


def ordered_kernel(hidden_ref, prefix_ref, out_ref):
    groups, _, steps, _ = hidden_ref.shape
    runs = steps // SUB
    for group in range(groups):
        a, b, c, d, u, v = (prefix_ref[group, j] for j in range(6))
        for i in range(runs):
            rows, times = pl.ds(i * SUB, SUB), pl.ds(i, SUB, stride=runs)
            by_cell, by_hidden, offset = (hidden_ref[group, j, rows, :] for j in range(3))
            out_ref[3 * group, times, :] = by_cell * a + by_hidden * c
            out_ref[3 * group + 1, times, :] = by_cell * b + by_hidden * d
            out_ref[3 * group + 2, times, :] = by_cell * u + by_hidden * v + offset


def ordered(hiddens, prefix):
    groups, _, steps, _ = hiddens.shape
    return pl.pallas_call(
        ordered_kernel,
        out_shape=pltpu.VMEM((3 * groups, steps, LANES), F32),
        in_specs=vmem(2),
        out_specs=pl.BlockSpec(memory_space=pltpu.VMEM),
        compiler_params=PARAMS,
        cost_estimate=cost(10 * groups * steps * LANES, 24 * groups * steps * LANES),
        name="ordered",
    )(hiddens, prefix)


def last_kernel(count, own_xor, *refs):
    received = refs[: count - 1]
    maps_ref, out_ref, made_ref, sems = refs[count - 1 :]
    groups = maps_ref.shape[0] // 3
    copies = []
    for group in range(groups):
        cell, hidden = arriving(count, own_xor, received, group, False)
        made = maps_ref[3 * group] * cell + maps_ref[3 * group + 1] * hidden
        rows = pl.ds(group * LANES, LANES)
        made_ref[rows, :] = (made + maps_ref[3 * group + 2]).T
        copies.append(pltpu.make_async_copy(made_ref.at[rows], out_ref.at[rows], sems.at[group]))
        copies[-1].start()
    for copy in copies:
        copy.wait()


def last(own_xor, received, maps):
    count = len(received) + 1
    groups, steps = maps.shape[0] // 3, maps.shape[1]
    return pl.pallas_call(
        functools.partial(last_kernel, count, own_xor),
        out_shape=jax.ShapeDtypeStruct((groups * LANES, steps), F32),
        in_specs=vmem(count),
        out_specs=pl.BlockSpec(memory_space=pltpu.HBM),
        scratch_shapes=[
            pltpu.VMEM((groups * LANES, steps), F32),
            pltpu.SemaphoreType.DMA((groups,)),
        ],
        compiler_params=PARAMS,
        cost_estimate=cost(10 * groups * steps * LANES, 16 * groups * steps * LANES),
        name="last",
    )(*received, maps)


def pieces_of(groups, chips):
    half = max(1, groups // 2)
    pieces = [(1, 0, half)] + [(1, group, 1) for group in range(half, groups)]
    return pieces + [(away, 0, groups) for away in range(2, chips)]


def shards(tokens, in_weight, recur_weight, gate_bias, forget_offset):
    steps = tokens.shape[0]
    channels = recur_weight.shape[0]
    groups = channels // LANES
    per_owner = channels * GATES
    owners = lax.axis_size("chan")
    chips = owners // 2
    blocks = lax.axis_size("tm")
    own_xor = blocks & (blocks - 1) == 0

    bias = on_chip(gate_bias.T)
    weight = on_chip(recur_weight.T)
    offset = on_chip(forget_offset.reshape(1, steps))

    def to_core(value):
        return on_chip(lax.ppermute(value, "chan", [(i, i ^ 1) for i in range(owners)]))

    def to_chip(value, away):
        pairs = [(i, (i + 2 * away) % owners) for i in range(owners)]
        return on_chip(lax.ppermute(value, "chan", pairs))

    def to_blocks(value):
        arriving = []
        for k in range(1, blocks):
            pairs = [(i, i ^ k if own_xor else i + k) for i in range(blocks)]
            sent = lax.ppermute(value, "tm", [pair for pair in pairs if pair[1] < blocks])
            arriving.append(on_chip(sent))
        return arriving

    tokens, in_weight = off_chip(tokens), off_chip(in_weight)

    def product(parts, after):
        return products(tokens, in_weight, chips, per_owner, parts, after)

    coded = [[] for _ in range(groups)]

    def send(away, start, count, mine, theirs, inside):
        code = encoded(mine, theirs, inside, count * GROUP)
        arrived = to_chip(code, away)
        for place in range(count):
            coded[start + place].append((arrived, place))
        return code

    local_give, local_keep = ((0, which, 0, per_owner) for which in (GIVE, KEEP))
    codes = []
    for index, (away, start, count) in enumerate(pieces_of(groups, chips)):
        parts = tuple((away, which, start * GROUP, count * GROUP) for which in (GIVE, KEEP))
        if index == 0:
            give, keep = product(parts, [])
            theirs = to_core(give)
            codes.append(send(away, start, count, keep, theirs, 0))
        else:
            give, keep = product(parts, codes[-2:-1])
            theirs = to_core(give)
            codes.append(send(away, start, count, keep, theirs, 0))
    (give,) = product((local_give,), codes[-1:])
    given = to_core(give)
    (keep,) = product((local_keep,), codes[-1:])
    kept, runs, prefixes, totals = [], [], [], []
    for group in range(groups):
        arrived, places = zip(*coded[group]) if coded[group] else ((), ())
        k, r, p, total = first(
            group, places, keep, given, list(arrived), bias, weight, offset, totals
        )
        totals = [total]
        kept.append(k)
        runs.append(r)
        prefixes.append(p)
    received = to_blocks(totals[0])
    lead = leads(runs, prefixes)
    hiddens, prefix, total = second(own_xor, received, kept, lead, weight)
    received = to_blocks(total)
    maps = ordered(hiddens, prefix)
    return last(own_xor, received, maps)


def solution(mesh):
    placed = (
        P(("groups", "tm"), "chan"),
        P("chan", None),
        P("chan", None),
        P("chan", None),
        P(("groups", "tm")),
    )

    return jax.shard_map(
        shards, mesh=mesh, in_specs=placed, out_specs=P("chan", ("groups", "tm")), check_vma=False
    )
```

```python
import functools

import jax
import jax.numpy as jnp
from jax import lax
from jax.experimental import pallas as pl
from jax.experimental.pallas import tpu as pltpu
from jax.sharding import PartitionSpec as P


LANES = 128
SUB = 8
GATES = 4
GROUP = LANES * GATES
BINADES = 251.0
LOWEST = 125.0
GIVE, KEEP = 0, 1
F32 = jnp.float32
BF16 = jnp.bfloat16


def cost(flops, moved):
    return pl.CostEstimate(flops=int(flops), bytes_accessed=int(moved), transcendentals=0)


def vmem(count):
    return [pl.BlockSpec(memory_space=pltpu.VMEM)] * count


def in_hbm(count):
    return [pl.BlockSpec(memory_space=pltpu.HBM)] * count


def off_chip(value):
    return pltpu.with_memory_space_constraint(value, pltpu.HBM)


def on_chip(value):
    return pltpu.with_memory_space_constraint(value, pltpu.VMEM)


PARAMS = pltpu.CompilerParams(vmem_limit_bytes=16 << 20)


def product_kernel(chips, parts, per_owner, tokens_ref, weight_ref, *refs):
    outs, (x_ref, w_ref, sems) = refs[-3 - len(parts) : -3], refs[-3:]
    me = lax.axis_index("chan")
    chip, core = me // 2, me % 2
    tokens_copy = pltpu.make_async_copy(tokens_ref, x_ref, sems.at[w_ref.shape[0]])
    tokens_copy.start()
    copies = []
    for (away, which, first, width), out_ref in zip(parts, outs):
        owner = 2 * lax.rem(chip + away, chips) + (core if which == KEEP else 1 - core)
        for start in range(0, width, GROUP):
            slot = len(copies)
            column = pl.multiple_of(owner * per_owner + first + start, GROUP)
            copy = pltpu.make_async_copy(
                weight_ref.at[:, pl.ds(column, GROUP)], w_ref.at[slot], sems.at[slot]
            )
            copy.start()
            copies.append((copy, out_ref, start))
    tokens_copy.wait()
    for slot, (copy, out_ref, start) in enumerate(copies):
        copy.wait()
        out_ref[:, pl.ds(start, GROUP)] = jnp.dot(
            x_ref[...], w_ref[slot], preferred_element_type=F32
        )


def products(tokens, in_weight, chips, per_owner, parts, after):
    steps, depth = tokens.shape
    slots = sum(width for _, _, _, width in parts) // GROUP
    return pl.pallas_call(
        functools.partial(product_kernel, chips, parts, per_owner),
        out_shape=[pltpu.VMEM((steps, width), F32) for _, _, _, width in parts],
        in_specs=in_hbm(2) + vmem(len(after)),
        out_specs=vmem(len(parts)),
        scratch_shapes=[
            pltpu.VMEM((steps, depth), BF16),
            pltpu.VMEM((slots, depth, GROUP), BF16),
            pltpu.SemaphoreType.DMA((slots + 1,)),
        ],
        compiler_params=PARAMS,
        cost_estimate=cost(2 * slots * steps * depth * GROUP, 2 * slots * depth * GROUP),
        name="products",
    )(tokens, in_weight, *after)


def encode_kernel(first, mine_ref, theirs_ref, out_ref, sum_ref):
    steps, width = sum_ref.shape
    blocks = width // LANES
    top = jnp.zeros((steps, LANES), F32)
    for block in range(blocks):
        cols = pl.ds(first + block * LANES, LANES)
        both = mine_ref[:, cols] + theirs_ref[:, cols]
        sum_ref[:, pl.ds(block * LANES, LANES)] = both
        top = jnp.maximum(top, jnp.abs(both))
    top = jnp.max(top, axis=0, keepdims=True)
    top = jnp.maximum(top, 1e-30) * 1.0078125
    scale = top.astype(BF16).astype(F32)
    out_ref[pl.ds(blocks * steps, SUB), :] = jnp.broadcast_to(scale, (SUB, LANES)).astype(BF16)
    inverse = 1.0 / scale
    for block in range(blocks):
        value = sum_ref[:, pl.ds(block * LANES, LANES)]
        share = jnp.abs(value) * inverse
        level = share * lax.rsqrt(jnp.maximum(share, 1e-30)) * BINADES - LOWEST
        code = jnp.exp2(level)
        out_ref[pl.ds(block * steps, steps), :] = jnp.where(value < 0.0, -code, code).astype(BF16)


def encoded(mine, theirs, first, width):
    steps = mine.shape[0]
    rows = steps * (width // LANES) + SUB
    return pl.pallas_call(
        functools.partial(encode_kernel, first),
        out_shape=pltpu.VMEM((rows, LANES), BF16),
        in_specs=vmem(2),
        out_specs=pl.BlockSpec(memory_space=pltpu.VMEM),
        scratch_shapes=[pltpu.VMEM((steps, width), F32)],
        compiler_params=PARAMS,
        cost_estimate=cost(20 * steps * width, 10 * steps * width),
        name="encode",
    )(mine, theirs)


def decoded(code, scale):
    level = (jnp.log2(jnp.abs(code)) + LOWEST) * (1.0 / BINADES)
    size = level * level * scale
    return jnp.where(code < 0.0, -size, size)


def compose(early, later):
    e1, e2, e3, e4, e5, e6 = early
    l1, l2, l3, l4, l5, l6 = later
    return (
        l1 * e1 + l2 * e3,
        l1 * e2 + l2 * e4,
        l3 * e1 + l4 * e3,
        l3 * e2 + l4 * e4,
        l1 * e5 + l2 * e6 + l5,
        l3 * e5 + l4 * e6 + l6,
    )


def compose_lower(early, later):
    e1, e3, e4, e5, e6 = early
    l1, l3, l4, l5, l6 = later
    return (
        l1 * e1,
        l3 * e1 + l4 * e3,
        l4 * e4,
        l1 * e5 + l5,
        l3 * e5 + l4 * e6 + l6,
    )


def sub_blocks(terms, join, identity):
    row = lax.broadcasted_iota(jnp.int32, (SUB, LANES), 0)
    reach = 1
    while reach < SUB:
        moved = tuple(
            jnp.where(row >= reach, pltpu.roll(term, reach, 0), unit)
            for term, unit in zip(terms, identity)
        )
        terms = join(moved, terms)
        reach *= 2
    before = tuple(
        jnp.where(row >= 1, pltpu.roll(term, 1, 0), unit) for term, unit in zip(terms, identity)
    )
    return before, terms


LOWER_UNIT = (1.0, 0.0, 1.0, 0.0, 0.0)
UNIT = (1.0, 0.0, 0.0, 1.0, 0.0, 0.0)


def sigmoid(x):
    return 1.0 / (1.0 + jnp.exp(-x))


def first_kernel(start, places, earlier, *refs):
    groups, remotes = 1, len(places)
    refs = list(refs)
    mine_ref, theirs_ref = refs[:2]
    codes = refs[2 : 2 + remotes]
    bias_ref, weight_ref, offset_ref = refs[2 + remotes : 5 + remotes]
    totals_before = refs[5 + remotes : 5 + remotes + earlier]
    kept_ref, run_ref, prefix_ref, totals_ref, sum_ref, late_ref = refs[5 + remotes + earlier :]
    steps = mine_ref.shape[0]
    runs = steps // SUB
    done = 0
    for ref in totals_before:
        totals_ref[pl.ds(done, ref.shape[0]), :] = ref[...]
        done += ref.shape[0]
    scales = [
        ref[pl.ds(ref.shape[0] - SUB, SUB), :][0:1, :].astype(F32) for ref in codes
    ]
    late_ref[...] = jnp.broadcast_to(offset_ref[...], (LANES, steps)).T
    lane = lax.broadcasted_iota(jnp.int32, (SUB, LANES), 1)
    quarter = lane // (LANES // GATES)
    inner = lane % (LANES // GATES)
    picks = [inner * GATES + (quarter - q + GATES) % GATES for q in range(GATES)]
    for group in range(groups):
        for q in range(GATES):
            block = group * GATES + q
            cols = pl.ds(start * GROUP + block * LANES, LANES)
            value = mine_ref[:, cols] + theirs_ref[:, cols]
            for ref, scale, place in zip(codes, scales, places):
                rows = pl.ds((place * GATES + block) * steps, steps)
                value = value + decoded(ref[rows, :].astype(F32), scale)
            sum_ref[q] = value
        channels = pl.ds((start + group) * LANES, LANES)
        biases = [
            jnp.broadcast_to(bias_ref[k : k + 1, channels], (SUB, LANES)) for k in range(GATES)
        ]
        out_weight = jnp.broadcast_to(weight_ref[1:2, channels], (SUB, LANES))
        run = None
        for i in range(runs):
            loaded = [
                jnp.take_along_axis(sum_ref[q, pl.ds(i, SUB, stride=runs), :], picks[q], axis=1)
                for q in range(GATES)
            ]
            pre = []
            for k in range(GATES):
                part = loaded[(0 - k) % GATES]
                for p in range(1, GATES):
                    part = jnp.where(quarter == p, loaded[(p - k) % GATES], part)
                if k:
                    part = pltpu.roll(part, LANES - k * (LANES // GATES), 1)
                pre.append(part + biases[k])
            pre_forget = pre[1] - late_ref[pl.ds(i, SUB, stride=runs), :]
            forget = sigmoid(pre_forget)
            output = sigmoid(pre[3])
            cell = sigmoid(pre[0]) * jnp.tanh(pre[2])
            squashed = jnp.tanh(cell)
            hidden_cell = output * (1.0 - squashed * squashed) * forget
            hidden_hidden = output * (1.0 - output) * out_weight * squashed
            term = (forget, hidden_cell, hidden_hidden, cell, output * squashed)
            run = term if run is None else compose_lower(run, term)
            rows = pl.ds(i * SUB, SUB)
            kept_ref[group, 0, rows, :] = pre_forget
            kept_ref[group, 1, rows, :] = pre[3]
            kept_ref[group, 2, rows, :] = cell
            for index, part in enumerate(run):
                run_ref[group, index, rows, :] = part
        before, total = sub_blocks(run, compose_lower, LOWER_UNIT)
        for index, term in enumerate(before):
            prefix_ref[group, index] = term
        for index, term in enumerate(total):
            totals_ref[pl.ds(done + group * SUB + index, 1), :] = term[SUB - 1 : SUB, :]
        for index in range(len(total), SUB):
            totals_ref[pl.ds(done + group * SUB + index, 1), :] = jnp.zeros((1, LANES), F32)


def first(start, places, mine, theirs, codes, bias, weight, offset, earlier):
    steps = mine.shape[0]
    groups = 1
    rows = sum(e.shape[0] for e in earlier) + groups * SUB
    count = 5 + len(codes) + len(earlier)
    return pl.pallas_call(
        functools.partial(first_kernel, start, places, len(earlier)),
        out_shape=(
            pltpu.VMEM((groups, 3, steps, LANES), F32),
            pltpu.VMEM((groups, 5, steps, LANES), F32),
            pltpu.VMEM((groups, 5, SUB, LANES), F32),
            pltpu.VMEM((rows, LANES), F32),
        ),
        in_specs=vmem(count),
        out_specs=vmem(4),
        scratch_shapes=[
            pltpu.VMEM((GATES, steps, LANES), F32),
            pltpu.VMEM((steps, LANES), F32),
        ],
        compiler_params=PARAMS,
        cost_estimate=cost(60 * steps * groups * GROUP, 20 * steps * groups * GROUP),
        name="first",
    )(mine, theirs, *codes, bias, weight, offset, *earlier)


def in_turn(me, count, own_xor, received):
    for position in range(count - 1):
        picked = received[0]
        for k in range(2, count):
            picked = jnp.where(position == (me ^ k if own_xor else me - k), received[k - 1], picked)
        yield picked, position < me


def arriving(count, own_xor, received, group, lower):
    me = lax.axis_index("tm")
    rows = [ref[pl.ds(group * SUB, SUB), :] for ref in received]
    cell = jnp.zeros((1, LANES), F32)
    hidden = jnp.zeros((1, LANES), F32)
    for maps, counts in in_turn(me, count, own_xor, rows):
        if lower:
            a, c, d, u, v = (maps[j : j + 1, :] for j in range(5))
            new_cell = a * cell + u
        else:
            a, b, c, d, u, v = (maps[j : j + 1, :] for j in range(6))
            new_cell = a * cell + b * hidden + u
        new_hidden = c * cell + d * hidden + v
        cell = jnp.where(counts, new_cell, cell)
        hidden = jnp.where(counts, new_hidden, hidden)
    return cell, hidden


def lead_kernel(groups, *refs):
    runs, befores, lead_ref = refs[:groups], refs[groups : 2 * groups], refs[-1]
    steps = lead_ref.shape[2]
    for group in range(groups):
        before = tuple(befores[group][0, j] for j in range(5))
        for i in range(steps // SUB):
            terms = before
            if i:
                rows = pl.ds((i - 1) * SUB, SUB)
                terms = compose_lower(before, tuple(runs[group][0, j, rows, :] for j in range(5)))
            for index, term in enumerate(terms):
                lead_ref[group, index, pl.ds(i * SUB, SUB), :] = term


def leads(runs, befores):
    groups, steps = len(runs), runs[0].shape[2]
    return pl.pallas_call(
        functools.partial(lead_kernel, groups),
        out_shape=pltpu.VMEM((groups, 5, steps, LANES), F32),
        in_specs=vmem(2 * groups),
        out_specs=pl.BlockSpec(memory_space=pltpu.VMEM),
        compiler_params=PARAMS,
        cost_estimate=cost(12 * groups * steps * LANES, 40 * groups * steps * LANES),
        name="leads",
    )(*runs, *befores)


def second_kernel(count, own_xor, groups, *refs):
    received, kept = refs[: count - 1], refs[count - 1 : count - 1 + groups]
    lead_ref, weight_ref, hidden_ref, prefix_ref, totals_ref = refs[count - 1 + groups :]
    steps = lead_ref.shape[2]
    for group, kept_ref in enumerate(kept):
        first_cell, first_hidden = arriving(count, own_xor, received, group, True)
        first_cell = jnp.broadcast_to(first_cell, (SUB, LANES))
        first_hidden = jnp.broadcast_to(first_hidden, (SUB, LANES))
        channels = pl.ds(group * LANES, LANES)
        forget_weight = jnp.broadcast_to(weight_ref[0:1, channels], (SUB, LANES))
        out_weight = jnp.broadcast_to(weight_ref[1:2, channels], (SUB, LANES))
        run = None
        for i in range(steps // SUB):
            rows = pl.ds(i * SUB, SUB)
            a, c, d, u, v = (lead_ref[group, j, rows, :] for j in range(5))
            cell = a * first_cell + u
            hidden = c * first_cell + d * first_hidden + v
            forget = sigmoid(kept_ref[0, 0, rows, :] + forget_weight * hidden)
            output = sigmoid(kept_ref[0, 1, rows, :] + out_weight * hidden)
            kept_cell = forget * cell
            new_cell = kept_cell + kept_ref[0, 2, rows, :]
            squashed = jnp.tanh(new_cell)
            slope = output * (1.0 - squashed * squashed)
            cell_hidden = kept_cell * (1.0 - forget) * forget_weight
            hidden_cell = slope * forget
            hidden_hidden = output * (1.0 - output) * out_weight * squashed + slope * cell_hidden
            offset_cell = new_cell - kept_cell - cell_hidden * hidden
            offset_hidden = output * squashed - hidden_cell * cell - hidden_hidden * hidden
            term = (forget, cell_hidden, hidden_cell, hidden_hidden, offset_cell, offset_hidden)
            run = term if run is None else compose(run, term)
            hidden_ref[group, 0, rows, :] = run[2]
            hidden_ref[group, 1, rows, :] = run[3]
            hidden_ref[group, 2, rows, :] = run[5]
        before, total = sub_blocks(run, compose, UNIT)
        for index, term in enumerate(before):
            prefix_ref[group, index] = term
        for index, term in enumerate(total):
            totals_ref[pl.ds(group * SUB + index, 1), :] = term[SUB - 1 : SUB, :]
        for index in range(len(total), SUB):
            totals_ref[pl.ds(group * SUB + index, 1), :] = jnp.zeros((1, LANES), F32)


def second(own_xor, received, kept, lead, weight):
    count = len(received) + 1
    groups, steps = len(kept), lead.shape[2]
    return pl.pallas_call(
        functools.partial(second_kernel, count, own_xor, groups),
        out_shape=(
            pltpu.VMEM((groups, 3, steps, LANES), F32),
            pltpu.VMEM((groups, 6, SUB, LANES), F32),
            pltpu.VMEM((groups * SUB, LANES), F32),
        ),
        in_specs=vmem(count - 1 + groups + 2),
        out_specs=vmem(3),
        compiler_params=PARAMS,
        cost_estimate=cost(80 * groups * steps * LANES, 24 * groups * steps * LANES),
        name="second",
    )(*received, *kept, lead, weight)


def ordered_kernel(hidden_ref, prefix_ref, out_ref):
    groups, _, steps, _ = hidden_ref.shape
    runs = steps // SUB
    for group in range(groups):
        a, b, c, d, u, v = (prefix_ref[group, j] for j in range(6))
        for i in range(runs):
            rows, times = pl.ds(i * SUB, SUB), pl.ds(i, SUB, stride=runs)
            by_cell, by_hidden, offset = (hidden_ref[group, j, rows, :] for j in range(3))
            out_ref[3 * group, times, :] = by_cell * a + by_hidden * c
            out_ref[3 * group + 1, times, :] = by_cell * b + by_hidden * d
            out_ref[3 * group + 2, times, :] = by_cell * u + by_hidden * v + offset


def ordered(hiddens, prefix):
    groups, _, steps, _ = hiddens.shape
    return pl.pallas_call(
        ordered_kernel,
        out_shape=pltpu.VMEM((3 * groups, steps, LANES), F32),
        in_specs=vmem(2),
        out_specs=pl.BlockSpec(memory_space=pltpu.VMEM),
        compiler_params=PARAMS,
        cost_estimate=cost(10 * groups * steps * LANES, 24 * groups * steps * LANES),
        name="ordered",
    )(hiddens, prefix)


def last_kernel(count, own_xor, *refs):
    received = refs[: count - 1]
    maps_ref, out_ref, made_ref, sems = refs[count - 1 :]
    groups = maps_ref.shape[0] // 3
    copies = []
    for group in range(groups):
        cell, hidden = arriving(count, own_xor, received, group, False)
        made = maps_ref[3 * group] * cell + maps_ref[3 * group + 1] * hidden
        rows = pl.ds(group * LANES, LANES)
        made_ref[rows, :] = (made + maps_ref[3 * group + 2]).T
        copies.append(pltpu.make_async_copy(made_ref.at[rows], out_ref.at[rows], sems.at[group]))
        copies[-1].start()
    for copy in copies:
        copy.wait()


def last(own_xor, received, maps):
    count = len(received) + 1
    groups, steps = maps.shape[0] // 3, maps.shape[1]
    return pl.pallas_call(
        functools.partial(last_kernel, count, own_xor),
        out_shape=jax.ShapeDtypeStruct((groups * LANES, steps), F32),
        in_specs=vmem(count),
        out_specs=pl.BlockSpec(memory_space=pltpu.HBM),
        scratch_shapes=[
            pltpu.VMEM((groups * LANES, steps), F32),
            pltpu.SemaphoreType.DMA((groups,)),
        ],
        compiler_params=PARAMS,
        cost_estimate=cost(10 * groups * steps * LANES, 16 * groups * steps * LANES),
        name="last",
    )(*received, maps)


def pieces_of(groups, chips):
    half = max(1, groups // 2)
    pieces = [(1, 0, half)] + [(1, group, 1) for group in range(half, groups)]
    return pieces + [(away, 0, groups) for away in range(2, chips)]


def shards(tokens, in_weight, recur_weight, gate_bias, forget_offset):
    steps = tokens.shape[0]
    channels = recur_weight.shape[0]
    groups = channels // LANES
    per_owner = channels * GATES
    owners = lax.axis_size("chan")
    chips = owners // 2
    blocks = lax.axis_size("tm")
    own_xor = blocks & (blocks - 1) == 0

    bias = on_chip(gate_bias.T)
    weight = on_chip(recur_weight.T)
    offset = on_chip(forget_offset.reshape(1, steps))

    def to_core(value):
        return on_chip(lax.ppermute(value, "chan", [(i, i ^ 1) for i in range(owners)]))

    def to_chip(value, away):
        pairs = [(i, (i + 2 * away) % owners) for i in range(owners)]
        return on_chip(lax.ppermute(value, "chan", pairs))

    def to_blocks(value):
        arriving = []
        for k in range(1, blocks):
            pairs = [(i, i ^ k if own_xor else i + k) for i in range(blocks)]
            sent = lax.ppermute(value, "tm", [pair for pair in pairs if pair[1] < blocks])
            arriving.append(on_chip(sent))
        return arriving

    tokens, in_weight = off_chip(tokens), off_chip(in_weight)

    def product(parts, after):
        return products(tokens, in_weight, chips, per_owner, parts, after)

    coded = [[] for _ in range(groups)]

    def send(away, start, count, mine, theirs, inside):
        code = encoded(mine, theirs, inside, count * GROUP)
        arrived = to_chip(code, away)
        for place in range(count):
            coded[start + place].append((arrived, place))
        return code

    local_give, local_keep = ((0, which, 0, per_owner) for which in (GIVE, KEEP))
    codes = []
    pieces = pieces_of(groups, chips)
    owed = None
    for index, (away, start, count) in enumerate(pieces):
        parts = tuple((away, which, start * GROUP, count * GROUP) for which in (GIVE, KEEP))
        if index == 0:
            give, keep = product(parts, [])
            codes.append(send(away, start, count, keep, to_core(give), 0))
        elif index == 1 and len(pieces) > 2:
            (give,) = product(parts[:1], [])
            owed = (away, start, count, to_core(give), parts[1:])
        else:
            before = () if owed is None else owed[4]
            *rest, give, keep = product(before + parts, codes[:1])
            theirs = to_core(give)
            ready = [(away, start, count, keep, theirs)]
            if owed is not None:
                ready.insert(0, (*owed[:3], rest[0], owed[3]))
                owed = None
            for away_, start_, count_, keep_, theirs_ in ready:
                for group in range(start_, start_ + count_):
                    inside = (group - start_) * GROUP
                    codes.append(send(away_, group, 1, keep_, theirs_, inside))
    (give,) = product((local_give,), codes[-1:])
    given = to_core(give)
    (keep,) = product((local_keep,), codes[-1:])
    kept, runs, prefixes, totals = [], [], [], []
    for group in range(groups):
        arrived, places = zip(*coded[group]) if coded[group] else ((), ())
        k, r, p, total = first(
            group, places, keep, given, list(arrived), bias, weight, offset, totals
        )
        totals = [total]
        kept.append(k)
        runs.append(r)
        prefixes.append(p)
    received = to_blocks(totals[0])
    lead = leads(runs, prefixes)
    hiddens, prefix, total = second(own_xor, received, kept, lead, weight)
    received = to_blocks(total)
    maps = ordered(hiddens, prefix)
    return last(own_xor, received, maps)


def solution(mesh):
    placed = (
        P(("groups", "tm"), "chan"),
        P("chan", None),
        P("chan", None),
        P("chan", None),
        P(("groups", "tm")),
    )

    return jax.shard_map(
        shards, mesh=mesh, in_specs=placed, out_specs=P("chan", ("groups", "tm")), check_vma=False
    )
```
